128 devices in a mesh: dp: 4 (over y_lo, core), tp: 32 (over y_hi, z, x).
Axes of the slice: x: 4, y: 4 (y_hi: 2, y_lo: 2; y = y_hi * 2 + y_lo), z: 4, core: 2. Of those that a mesh axis runs over, the one named last changes fastest.
Arguments:
- teacher_partial: bfloat16 [32, 512, 4608], P('tp', 'dp'), may hold values from -6 to 6
- teacher_residual: bfloat16 [512, 4608], P(('dp', 'tp')), may hold values from -120 to 120
- post_gain: float32 [4608], replicated, may hold values from 0.5 to 1.5
- final_gain: float32 [4608], replicated, may hold values from 0.5 to 1.5
- teacher_head: bfloat16 [4608, 131072], P(None, ('dp', 'tp')), may hold values from -40 to 40
- student_hidden: bfloat16 [512, 3584], P(('dp', 'tp')), may hold values from -120 to 120
- student_gain: float32 [3584], replicated, may hold values from 0.5 to 1.5
- student_head: bfloat16 [3584, 131072], P(None, ('dp', 'tp')), may hold values from -40 to 40
- labels: int32 [512], P('dp'), may hold values from 0 to 131071
- lengths: int32 [4, 8], P('dp'), may hold values from 1 to 48, 96 in all within a row
Outputs:
- grad_hidden: float32 [512, 3584], P(('dp', 'tp'))
- token_loss: float32 [512], P(('dp', 'tp'))
The draws below stay inside these ranges and needn't reach their ends.
Inputs may be any that keep to these rules, and one draw needn't show every extreme that they name: `lengths`: group g's 8 sequences fill, in order, its first 96 rows; its remaining 128 - 96 rows are padding.
All inputs are finite; a program needn't handle non-finite values.
Results may differ from the reference program's by a relative error of at most 0.03.
Values may be sent and summed in bfloat16 or wider, within the bound.
A program may use at most 128 MiB of HBM per device.

```python
import math
import jax
import jax.numpy as jnp
import numpy as np
from jax import lax

D_T = 4608
D_S = 3584
TOK_G = 128
NSEQ = 8
LIVE = 96
MOST = 48
GROUPS = 4
SPLITS = 32
TOKENS = 512
VOCAB = 131072


def hidden_draw(key, width, salt):
    values = jnp.clip(jax.random.normal(jax.random.fold_in(key, salt + 10), (TOKENS, width)), -6.0, 6.0)
    return values.astype(jnp.bfloat16)


def head_draw(key, width, salt):
    normal_part = jnp.clip(jax.random.normal(jax.random.fold_in(key, salt + 40), (width, VOCAB)), -6.0, 6.0)
    values = normal_part * (3.0 / math.sqrt(width))
    return values.astype(jnp.bfloat16)


def draw_teacher_residual(key, part):
    return hidden_draw(key, D_T, 4)


def draw_student_hidden(key, part):
    return hidden_draw(key, D_S, 5)


def draw_teacher_head(key, part):
    return head_draw(key, D_T, 4)


def draw_student_head(key, part):
    return head_draw(key, D_S, 5)


def plant(entries, own_key, low, largest):
    longest = entries.shape.index(max(entries.shape))
    spots = []
    for shift in (0, 1):
        where = [jax.random.randint(jax.random.fold_in(own_key, axis), (), 0, length) for axis, length in enumerate(entries.shape)]
        where[longest] = (where[longest] + shift) % entries.shape[longest]
        spots.append(tuple(where))
    return entries.at[spots[0]].set(low).at[spots[1]].set(largest)


def with_spikes(values, key, source, target, shards_of, factor):
    owner, partner = [(jnp.arange(values.shape[dim]) // (values.shape[dim] // shards_of)).reshape([-1 if axis == dim else 1 for axis in range(values.ndim)]) for dim in (source, target)]
    chosen = jax.random.permutation(key, shards_of)[partner]
    strong = (owner == chosen) | (owner == (partner + shards_of // 2) % shards_of)
    return jnp.where(strong, factor * values, values)


def block_scale(key, extent, split, low, largest):
    def one(position, shards_of):
        draws = jax.random.uniform(jax.random.fold_in(jax.random.fold_in(key, 6), position), (shards_of,), jnp.float32, low / len(split), largest / len(split))
        return jnp.repeat(jnp.exp(draws), extent[position] // shards_of).reshape((-1,) + (1,) * (len(extent) - position - 1))

    level = one(*split[0])
    for cut in split[1:]:
        level = level * one(*cut)
    return level


def split_up(number_of, total, most, lean):
    portions = [(1 << 20) // math.isqrt(grade ** lean) + 1 for grade in range(2, number_of + 1)]
    rest, holding = total - most - (number_of - 1), [1] * (number_of - 1)
    while rest > 0:
        free = [i for i in range(number_of - 1) if holding[i] < most]
        pool, remaining = sum([portions[i] for i in free]), rest
        for i in free:
            extra = min(most - holding[i], max(1, remaining * portions[i] // pool), rest)
            holding[i] = holding[i] + extra
            rest = rest - extra
    return np.array([most] + holding)


def ragged(rng, count, total, limit, skew):
    if count == 2:
        one = jax.random.randint(rng, (), max(1, total - limit), min(limit, total - 1) + 1)
        return jnp.stack([one, total - one])
    tallies = jnp.asarray(split_up(count, total, limit, skew), jnp.int32)
    twos = (count - 1) // 2
    donor, sink = tallies[1:1 + 2 * twos:2], tallies[2:2 + 2 * twos:2]
    slack = jnp.minimum(donor - 1, limit - sink)
    moved = jax.random.randint(jax.random.fold_in(rng, 1), (twos,), 0, 1 << 20) % (slack + 1)
    tallies = tallies.at[1:1 + 2 * twos:2].set(donor - moved).at[2:2 + 2 * twos:2].set(sink + moved)
    return tallies[jax.random.permutation(jax.random.fold_in(rng, 2), count)]


def bell_draw_with(rng, extent, scale, limit, split, heavy, held_as=jnp.bfloat16):
    values = scale * jax.random.normal(rng, extent, jnp.float32)
    if split:
        values = values * block_scale(rng, extent, split, -0.22, 0.18)
    return jnp.clip(with_spikes(values, jax.random.fold_in(rng, 3), *heavy), -limit, limit).astype(held_as)


def setup_inputs(seed: int = 0) -> dict:
    key_list = jax.random.split(jax.random.key(seed), 11)
    teacher_partial = bell_draw_with(key_list[0], (SPLITS, TOKENS, D_T), 0.25, 6.0, ((0, 32), (1, 4)), (0, 1, 32, 2.75))
    teacher_residual = draw_teacher_residual(jax.random.fold_in(key_list[10], 71), 0)
    post_gain = jnp.clip(1.0 + 0.1 * jax.random.normal(key_list[2], (D_T,), jnp.float32), 0.5, 1.5)
    final_gain = jnp.clip(1.0 + 0.1 * jax.random.normal(key_list[3], (D_T,), jnp.float32), 0.5, 1.5)
    teacher_head = draw_teacher_head(jax.random.fold_in(key_list[10], 71), 0)
    student_hidden = draw_student_hidden(jax.random.fold_in(key_list[10], 71), 0)
    student_gain = jnp.clip(1.0 + 0.1 * jax.random.normal(key_list[6], (D_S,), jnp.float32), 0.5, 1.5)
    student_head = draw_student_head(jax.random.fold_in(key_list[10], 71), 0)
    labels = plant(jax.random.randint(key_list[8], (TOKENS,), 0, VOCAB), jax.random.fold_in(key_list[8], 1), 0, VOCAB - 1).astype(jnp.int32)
    lengths = jax.vmap(lambda own: ragged(own, NSEQ, LIVE, MOST, 2))(jax.random.split(key_list[9], GROUPS)).reshape((GROUPS, NSEQ)).astype(jnp.int32)
    return {"teacher_partial": teacher_partial, "teacher_residual": teacher_residual, "post_gain": post_gain, "final_gain": final_gain, "teacher_head": teacher_head, "student_hidden": student_hidden, "student_gain": student_gain, "student_head": student_head, "labels": labels, "lengths": lengths}


EPS = 1e-06
BETA = 0.5
LOSS_SCALE = 1024.0

def norm_rows(values, gain):
    inverse = lax.rsqrt(lax.optimization_barrier(jnp.mean(values * values, axis=-1, keepdims=True)) + EPS)
    return (values * inverse * gain, inverse)

def token_weights(lengths, tok_rows):
    ends = jnp.cumsum(lengths, axis=1).astype(jnp.int32)
    starts = ends - lengths
    places = jnp.arange(tok_rows, dtype=jnp.int32)
    inside = (places[None, :, None] >= starts[:, None, :]) & (places[None, :, None] < ends[:, None, :])
    spans = lax.optimization_barrier(jnp.sum(jnp.where(inside, lengths[:, None, :], 0), axis=2))
    covered = lax.optimization_barrier(jnp.sum(inside.astype(jnp.int32), axis=2))
    return covered.astype(jnp.float32) / jnp.maximum(spans, 1).astype(jnp.float32)

def reference(teacher_partial, teacher_residual, post_gain, final_gain, teacher_head, student_hidden, student_gain, student_head, labels, lengths):
    mlp_sum = lax.optimization_barrier(jnp.sum(teacher_partial, axis=0, dtype=jnp.float32))
    post, unused = norm_rows(mlp_sum, post_gain)
    final = teacher_residual.astype(jnp.float32) + post
    teacher_norm = norm_rows(final, final_gain)[0].astype(jnp.bfloat16)
    student_f = student_hidden.astype(jnp.float32)
    student_scaled, inverse = norm_rows(student_f, student_gain)
    student_norm = student_scaled.astype(jnp.bfloat16)
    weight = token_weights(lengths, TOK_G).reshape(-1)
    t_logits = jnp.dot(teacher_norm.astype(jnp.float32), teacher_head.astype(jnp.float32), preferred_element_type=jnp.float32)
    s_logits = jnp.dot(student_norm.astype(jnp.float32), student_head.astype(jnp.float32), preferred_element_type=jnp.float32)
    t_max = lax.optimization_barrier(jnp.max(t_logits, axis=1))
    t_log = t_max + jnp.log(lax.optimization_barrier(jnp.sum(jnp.exp(t_logits - t_max[:, None]), axis=1)))
    s_max = lax.optimization_barrier(jnp.max(s_logits, axis=1))
    s_log = s_max + jnp.log(lax.optimization_barrier(jnp.sum(jnp.exp(s_logits - s_max[:, None]), axis=1)))
    t_logp = t_logits - t_log[:, None]
    s_logp = s_logits - s_log[:, None]
    t_prob = jnp.exp(t_logp)
    s_prob = jnp.exp(s_logp)
    divergence = lax.optimization_barrier(jnp.sum(t_prob * (t_logp - s_logp), axis=1))
    columns = jnp.arange(VOCAB, dtype=jnp.int32)
    hit = labels[:, None] == columns[None, :]
    label_value = lax.optimization_barrier(jnp.sum(jnp.where(hit, s_logits, 0.0), axis=1))
    label_term = s_log - label_value
    token_loss = jnp.where(weight > 0, divergence + BETA * label_term, 0.0)
    scale = (LOSS_SCALE * weight)[:, None]
    logit_grad = (scale * ((1.0 + BETA) * s_prob - t_prob - BETA * hit.astype(jnp.float32))).astype(jnp.bfloat16)
    norm_grad = jnp.dot(logit_grad.astype(jnp.float32), student_head.T.astype(jnp.float32), preferred_element_type=jnp.float32)
    scaled = norm_grad * student_gain
    inner = lax.optimization_barrier(jnp.mean(scaled * student_f, axis=1, keepdims=True))
    grad_hidden = inverse * scaled - student_f * (inverse * inverse * inverse) * inner
    return (grad_hidden, token_loss)
```

```python
import functools

import jax
import jax.numpy as jnp
from jax import lax
from jax.experimental import pallas as pl
from jax.experimental.pallas import tpu as pltpu
from jax.sharding import Mesh
from jax.sharding import PartitionSpec as P

TP = ("tp_0", "tp_1", "tp_2")
DP = ("dp_0", "dp_1")
DP_TP = ("dp_0", "dp_1", "tp_0", "tp_1", "tp_2")
MESH = pl.DeviceIdType.MESH

EPS = 1e-06
BETA = 0.5
LOSS_SCALE = 1024.0

F32 = jnp.float32
BF16 = jnp.bfloat16

D_T = 4608
D_S = 3584
QT = D_T // 4
QS = D_S // 4
VOC = 1024
ROWS = 384
NSEQ = 8
LANES = 128

PARTS_T = ((0, 384, "xyz"), (384, 384, "yzx"), (768, 384, "zxy"))
PARTS_S = ((0, 256, "xyz"), (256, 384, "yzx"), (640, 256, "zxy"))
PARTS_G = ((0, 256, "zyx"), (256, 384, "xzy"), (640, 256, "yxz"))


def live_pieces():
    first = [(c, y, z) for c in range(2) for y in range(2) for z in range(4)]
    second = [(c, y, z) for c in range(2) for y in range(2, 4) for z in range(2)]
    return first + second


PIECES = live_pieces()


class Place:
    def __init__(self):
        self.c = lax.axis_index("dp_1")
        self.z = lax.axis_index("tp_1")
        self.x = lax.axis_index("tp_2")
        self.y_lo = lax.axis_index("dp_0")
        self.y_hi = lax.axis_index("tp_0")
        self.y = self.y_hi * 2 + self.y_lo

    def at(self, axis):
        return {"x": self.x, "y": self.y, "z": self.z}[axis]

    def shifted(self, axis, k):
        return lax.rem(self.at(axis) + k, 4)

    def along(self, axis, to):
        y_lo, y_hi, z, x = (self.y_lo, self.y_hi, self.z, self.x)
        if axis == "x":
            x = to
        elif axis == "z":
            z = to
        else:
            y_lo, y_hi = lax.rem(to, 2), lax.div(to, 2)
        return (y_lo, self.c, y_hi, z, x)

    def sibling(self):
        return (self.y_lo, 1 - self.c, self.y_hi, self.z, self.x)


def remote(src, dst, send, recv, to):
    return pltpu.make_async_remote_copy(
        src_ref=src, dst_ref=dst, send_sem=send, recv_sem=recv, device_id=to, device_id_type=MESH
    )


def kernel(
    partial_ref,
    residual_ref,
    post_ref,
    final_ref,
    t_head_ref,
    hidden_ref,
    s_gain_ref,
    s_head_ref,
    labels_ref,
    lengths_ref,
    grad_ref,
    loss_ref,
    w_t,
    w_s,
    rb,
    tb,
    sb,
    res_out,
    res_in,
    stu_out,
    stu_in,
    asm_t,
    asm_s,
    mean_out,
    mean_in,
    tab_own,
    tab,
    lab_col,
    wgt_col,
    t_log,
    s_log,
    lg,
    stat,
    stat_in,
    back,
    loss_blk,
    g,
    core_in,
    rr,
    ng_out,
    ng_in,
    sem_w,
    a_send,
    a_recv,
    a_own,
    x_send,
    x_recv,
    tab_send,
    tab_recv,
    ag_send,
    ag_recv,
    sib_send,
    sib_recv,
    st_send,
    st_recv,
    rs_send,
    rs_recv,
):
    me = Place()
    tp = me.y_hi * 16 + me.z * 4 + me.x
    dp = me.y_lo * 2 + me.c
    position = dp * 32 + tp

    load_s = pltpu.make_async_copy(s_head_ref, w_s, sem_w.at[0])
    load_t = pltpu.make_async_copy(t_head_ref, w_t, sem_w.at[1])
    load_s.start()
    load_t.start()

    barrier = pltpu.get_barrier_semaphore()

    def tp_device(p):
        return (me.y_lo, me.c, lax.div(p, 16), lax.rem(lax.div(p, 4), 4), lax.rem(p, 4))

    @pl.loop(1, 32)
    def _(k):
        pl.semaphore_signal(
            barrier, inc=1, device_id=tp_device(lax.rem(tp + k, 32)), device_id_type=MESH
        )

    other = (1 - me.y_lo, 1 - me.c, me.y_hi, me.z, me.x)
    for to in (
        me.along("y", me.shifted("y", 1)),
        me.along("y", me.shifted("y", 3)),
        me.sibling(),
        other,
    ):
        pl.semaphore_signal(barrier, inc=1, device_id=to, device_id_type=MESH)
    pl.semaphore_wait(barrier, 35)

    def a_copy(k, peer):
        rows = pl.ds(pl.multiple_of(lax.div(peer, 4) * 16, 16), 16)
        cols = pl.ds(pl.multiple_of(lax.rem(peer, 4) * QT, 128), QT)
        return remote(
            partial_ref.at[0, rows, cols], rb.at[k], a_send.at[k], a_recv.at[k], tp_device(peer)
        )

    own_rows = pl.ds(pl.multiple_of(lax.div(tp, 4) * 16, 16), 16)
    own_cols = pl.ds(pl.multiple_of(me.x * QT, 128), QT)
    own_copy = pltpu.make_async_copy(partial_ref.at[0, own_rows, own_cols], rb.at[0], a_own)
    own_copy.start()

    @pl.loop(1, 32)
    def _(k):
        a_copy(k, lax.rem(tp + k, 32)).start()

    hidden = hidden_ref[...].astype(F32)
    inverse = lax.rsqrt(jnp.mean(hidden * hidden, axis=-1, keepdims=True) + EPS)
    student = (hidden * inverse * s_gain_ref[...]).astype(BF16)
    residual = residual_ref[...]
    for q in range(4):
        stu_out[q] = student[:, q * QS : (q + 1) * QS]
        res_out[q] = residual[:, q * QT : (q + 1) * QT]
    stu_in[me.x] = stu_out[me.x]
    res_in[me.x] = res_out[me.x]

    def x_copy(kind, src, dst, k):
        to = me.shifted("x", k)
        return remote(
            src.at[to],
            dst.at[me.x],
            x_send.at[kind, k - 1],
            x_recv.at[kind, k - 1],
            me.along("x", to),
        )

    def x_arrival(kind, src, dst, k):
        frm = me.shifted("x", 4 - k)
        return remote(
            src.at[frm],
            dst.at[frm],
            x_send.at[kind, k - 1],
            x_recv.at[kind, k - 1],
            me.along("x", frm),
        )

    for k in (1, 2, 3):
        x_copy(0, stu_out, stu_in, k).start()
        x_copy(1, res_out, res_in, k).start()

    lane = lax.broadcasted_iota(jnp.int32, (1, LANES), 1)
    start = jnp.int32(0)
    weight = jnp.zeros((1, LANES), F32)
    for i in range(NSEQ):
        length = lengths_ref[0, i]
        end = start + length
        inside = (lane >= start) & (lane < end)
        share = 1.0 / jnp.full((1, LANES), length, jnp.int32).astype(F32)
        weight = jnp.where(inside, share, weight)
        start = end
    sub = lax.broadcasted_iota(jnp.int32, (8, LANES), 0)
    label_row = labels_ref[...].astype(F32)
    tab_own[...] = jnp.where(
        sub == 0,
        jnp.broadcast_to(label_row, (8, LANES)),
        jnp.where(sub == 1, jnp.broadcast_to(weight, (8, LANES)), 0.0),
    )
    tab[dp] = tab_own[...]
    dp_peers = ((0, 1), (1, 0), (1, 1))

    def tab_copy(n):
        dy, dc = dp_peers[n]
        y_lo = 1 - me.y_lo if dy else me.y_lo
        c = 1 - me.c if dc else me.c
        to = (y_lo, c, me.y_hi, me.z, me.x)
        return (
            remote(tab_own, tab.at[dp], tab_send.at[n], tab_recv.at[n], to),
            remote(tab_own, tab.at[y_lo * 2 + c], tab_send.at[n], tab_recv.at[n], to),
        )

    for n in range(3):
        tab_copy(n)[0].start()

    def box(buf, axis, to, done, lo, width):
        where = []
        for a in "yzx":
            if a == axis:
                where.append(pl.ds(to, 1))
            elif a in done:
                where.append(pl.ds(0, 4))
            else:
                where.append(pl.ds(me.at(a), 1))
        return buf.at[me.c, where[0], where[1], where[2], :, pl.ds(lo, width)]

    def gather(which, buf, parts, stage):
        out = []
        for p, (lo, width, order) in enumerate(parts):
            axis, done = order[stage], order[:stage]
            own = box(buf, axis, me.at(axis), done, lo, width)
            for k in (1, 2, 3):
                sems = (ag_send.at[which, stage, p, k - 1], ag_recv.at[which, stage, p, k - 1])
                frm = me.shifted(axis, 4 - k)
                theirs = box(buf, axis, frm, done, lo, width)
                out.append(
                    (
                        remote(own, own, *sems, me.along(axis, me.shifted(axis, k))),
                        remote(theirs, theirs, *sems, me.along(axis, frm)),
                    )
                )
        return out

    def start_all(copies):
        for sent, unused in copies:
            sent.start()

    def arrive_all(copies):
        for unused, arrived in copies:
            arrived.wait_recv()

    def sent_all(copies):
        for sent, unused in copies:
            sent.wait_send()

    def swap(which, buf):
        out = []
        for n, (y, z) in enumerate(((pl.ds(0, 2), pl.ds(0, 4)), (pl.ds(2, 2), pl.ds(0, 2)))):
            sems = (sib_send.at[which, n], sib_recv.at[which, n])
            own, theirs = buf.at[me.c, y, z], buf.at[1 - me.c, y, z]
            out.append(
                (remote(own, own, *sems, me.sibling()), remote(theirs, theirs, *sems, me.sibling()))
            )
        return out

    student_stages = [gather(1, sb, PARTS_S, s) for s in range(3)]
    teacher_stages = [gather(0, tb, PARTS_T, s) for s in range(3)]
    student_swap, teacher_swap = swap(1, sb), swap(0, tb)

    for k in (1, 2, 3):
        x_arrival(0, stu_out, stu_in, k).wait_recv()
    for i in range(4):
        asm_s[4 * i : 4 * i + 4, :] = stu_in[i].astype(F32)
    sb[me.c, me.y, me.z, me.x] = asm_s[...].astype(BF16)
    start_all(student_stages[0])

    own_copy.wait()
    total = rb[0].astype(F32)

    def add_one(k, acc):
        frm = lax.rem(tp + 32 - k, 32)
        a_copy(k, frm).wait_recv()
        return acc + rb[k].astype(F32)

    total = lax.fori_loop(1, 32, add_one, total)

    def row_total(n, part):
        mean_out[n] = jnp.broadcast_to(part, (16, LANES))
        mean_in[n, me.x] = mean_out[n]
        copies = []
        for k in (1, 2, 3):
            to, frm = me.shifted("x", k), me.shifted("x", 4 - k)
            sems = (x_send.at[2 + n, k - 1], x_recv.at[2 + n, k - 1])
            copies.append(
                (
                    remote(mean_out.at[n], mean_in.at[n, me.x], *sems, me.along("x", to)),
                    remote(mean_out.at[n], mean_in.at[n, frm], *sems, me.along("x", frm)),
                )
            )
        start_all(copies)
        return copies

    def row_mean(n, copies):
        arrive_all(copies)
        whole = mean_in[n, 0] + mean_in[n, 1] + mean_in[n, 2] + mean_in[n, 3]
        return whole[:, 0:1] / D_T

    first_mean = row_total(0, jnp.sum(total * total, axis=1, keepdims=True))
    arrive_all(student_stages[0])
    start_all(student_stages[1])
    for k in (1, 2, 3):
        x_arrival(1, res_out, res_in, k).wait_recv()
    for i in range(4):
        asm_t[4 * i : 4 * i + 4, :] = res_in[i].astype(F32)
    post = total * lax.rsqrt(row_mean(0, first_mean) + EPS) * post_ref[:, own_cols]
    final = asm_t[...] + post
    second_mean = row_total(1, jnp.sum(final * final, axis=1, keepdims=True))
    arrive_all(student_stages[1])
    start_all(student_stages[2])
    normed = final * lax.rsqrt(row_mean(1, second_mean) + EPS) * final_ref[:, own_cols]
    tb[me.c, me.y, me.z, me.x] = normed.astype(BF16)
    start_all(teacher_stages[0])

    for n in range(3):
        tab_copy(n)[1].wait_recv()
    for group in range(4):
        table = tab[group]
        for row, col in ((0, lab_col), (1, wgt_col)):
            turned = jnp.broadcast_to(table[row : row + 1, :], (LANES, LANES)).T
            for m, (c, y, z) in enumerate(PIECES):
                if (y % 2) * 2 + c == group:
                    j = (y // 2) * 4 + z
                    col[m * 16 : (m + 1) * 16, :] = turned[j * 16 : (j + 1) * 16, :]
    g[:, 2:4, 2:4] = jnp.zeros((2, 2, 2, 4, 16, QS), BF16)
    loss_blk[:, 2:4, 2:4] = jnp.zeros((2, 2, 2, 16, LANES), F32)

    arrive_all(teacher_stages[0])
    start_all(teacher_stages[1])
    arrive_all(student_stages[2])
    start_all(student_swap)
    arrive_all(teacher_stages[1])
    start_all(teacher_stages[2])

    def live_rows(buf, q, width):
        return jnp.concatenate(
            [
                buf[:, 0:2, :, q].reshape(256, width),
                buf[:, 2:4, 0:2, q].reshape(128, width),
            ],
            axis=0,
        )

    def logits(buf, head, out, width):
        @pl.loop(0, VOC // 256)
        def _(n):
            cols = pl.ds(pl.multiple_of(n * 256, 256), 256)
            acc = None
            for q in range(4):
                term = jnp.dot(
                    live_rows(buf, q, width),
                    head[q * width : (q + 1) * width, cols],
                    preferred_element_type=F32,
                )
                acc = term if acc is None else acc + term
            out[:, cols] = acc

    arrive_all(student_swap)
    load_s.wait()
    logits(sb, w_s, s_log, QS)
    arrive_all(teacher_stages[2])
    start_all(teacher_swap)
    load_t.wait()
    arrive_all(teacher_swap)
    logits(tb, w_t, t_log, QT)

    first_col = (position * VOC).astype(F32)

    def columns():
        return lax.broadcasted_iota(jnp.int32, (32, VOC), 1).astype(F32) + first_col

    lanes = lax.broadcasted_iota(jnp.int32, (32, LANES), 1)

    @pl.loop(0, ROWS // 32)
    def _(r):
        rows = pl.ds(pl.multiple_of(r * 32, 32), 32)
        t, s = t_log[rows, :], s_log[rows, :]
        t_max = jnp.max(t, axis=1, keepdims=True)
        s_max = jnp.max(s, axis=1, keepdims=True)
        t_exp = jnp.exp(t - t_max)
        t_sum = jnp.sum(t_exp, axis=1, keepdims=True)
        cross = jnp.sum(t_exp * (t - s), axis=1, keepdims=True)
        s_sum = jnp.sum(jnp.exp(s - s_max), axis=1, keepdims=True)
        hit = columns() == lab_col[rows, 0:1]
        value = jnp.sum(jnp.where(hit, s, 0.0), axis=1, keepdims=True)
        held = wgt_col[rows, :]
        for n, one in enumerate((t_max, t_sum, cross, s_max, s_sum, value)):
            held = jnp.where(lanes == n, one, held)
        back[rows, :] = held

    for i in range(3):
        turned = back[i * 128 : (i + 1) * 128, :].T
        stat[0, :, i * 128 : (i + 1) * 128] = turned[0:8, :]

    def merged(values):
        t_max = functools.reduce(jnp.maximum, [v[0:1] for v in values])
        s_max = functools.reduce(jnp.maximum, [v[3:4] for v in values])
        t_sum = cross = s_sum = label = 0.0
        for v in values:
            t_one = jnp.exp(v[0:1] - t_max)
            s_one = jnp.exp(v[3:4] - s_max)
            t_sum += v[1:2] * t_one
            cross += v[2:3] * t_one
            s_sum += v[4:5] * s_one
            label += v[5:6]
        return [t_max, t_sum, cross, s_max, s_sum, label, values[0][6:7]]

    stat_copies = []
    for n, axis in enumerate("cxyz"):
        copies = []
        for k in (1,) if axis == "c" else (1, 2, 3):
            sems = (st_send.at[n, k - 1], st_recv.at[n, k - 1])
            dst = stat_in.at[n, k - 1]
            to = me.sibling() if axis == "c" else me.along(axis, me.shifted(axis, k))
            copy = remote(stat.at[n], dst, *sems, to)
            copies.append((copy, copy))
        start_all(copies)
        stat_copies += copies
        arrive_all(copies)
        values = [stat[n]] + [stat_in[n, k] for k in range(len(copies))]
        for i, line in enumerate(merged(values)):
            stat[n + 1, i : i + 1, :] = line

    end = stat[4]
    t_whole = end[0:1] + jnp.log(end[1:2])
    s_whole = end[3:4] + jnp.log(end[4:5])
    divergence = end[2:3] / end[1:2] - t_whole + s_whole
    row_loss = jnp.where(end[6:7] > 0, divergence + BETA * (s_whole - end[5:6]), 0.0)
    sub = lax.broadcasted_iota(jnp.int32, (8, ROWS), 0)
    lines = jnp.zeros((8, ROWS), F32)
    for n, one in enumerate((t_whole, s_whole, row_loss)):
        lines = jnp.where(sub == n, jnp.broadcast_to(one, (8, ROWS)), lines)
    for i in range(3):
        tall = jnp.concatenate(
            [lines[:, i * 128 : (i + 1) * 128], jnp.zeros((120, LANES), F32)], axis=0
        )
        back[i * 128 : (i + 1) * 128, :] = tall.T
    for m, (c, y, z) in enumerate(PIECES):
        loss_blk[c, y, z] = jnp.broadcast_to(back[m * 16 : (m + 1) * 16, 2:3], (16, LANES))

    @pl.loop(0, ROWS // 32)
    def _(r):
        rows = pl.ds(pl.multiple_of(r * 32, 32), 32)
        t_prob = jnp.exp(t_log[rows, :] - back[rows, 0:1])
        s_prob = jnp.exp(s_log[rows, :] - back[rows, 1:2])
        hit = (columns() == lab_col[rows, 0:1]).astype(F32)
        scale = LOSS_SCALE * wgt_col[rows, 0:1]
        lg[rows, :] = (scale * ((1.0 + BETA) * s_prob - t_prob - BETA * hit)).astype(BF16)

    for q in range(4):
        for lo in range(0, QS, 128 * 7):
            width = min(128 * 7, QS - lo)
            share = lax.dot_general(
                lg[...],
                w_s[q * QS + lo : q * QS + lo + width, :],
                (((1,), (1,)), ((), ())),
                preferred_element_type=F32,
            ).astype(BF16)
            g[:, 0:2, :, q, :, lo : lo + width] = share[0:256].reshape(2, 2, 4, 16, width)
            g[:, 2:4, 0:2, q, :, lo : lo + width] = share[256:384].reshape(2, 2, 2, 16, width)

    core_copies = []
    for n, (y, z) in enumerate(((pl.ds(0, 2), pl.ds(0, 4)), (pl.ds(2, 2), pl.ds(0, 2)))):
        copy = remote(
            g.at[1 - me.c, y, z],
            core_in.at[y, z],
            sib_send.at[2, n],
            sib_recv.at[2, n],
            me.sibling(),
        )
        core_copies.append((copy, copy))
    start_all(core_copies)
    arrive_all(core_copies)
    for ys, zs in (((0, 1), 4), ((2, 3), 2)):
        for y in ys:

            @pl.loop(0, zs * 4)
            def _(i, y=y):
                z, x = lax.div(i, 4), lax.rem(i, 4)
                both = g[me.c, y, z, x].astype(F32) + core_in[y, z, x].astype(F32)
                g[me.c, y, z, x] = both.astype(BF16)

    totals = []
    for stage in range(3):
        made = []
        for p, (lo, width, order) in enumerate(PARTS_G):
            axis, left = order[stage], order[stage + 1 :]
            for k in (1, 2, 3):
                to = me.shifted(axis, k)
                copy = remote(
                    box(g, axis, to, left, lo, width),
                    rr[stage][p].at[k - 1],
                    rs_send.at[stage, p, k - 1],
                    rs_recv.at[stage, p, k - 1],
                    me.along(axis, to),
                )
                made.append((copy, copy))
        start_all(made)
        arrive_all(made)
        core_copies += made
        for p, (lo, width, order) in enumerate(PARTS_G):
            left = order[stage + 1 :]
            came = rr[stage][p]

            def summed(y, z, x, i, j, k):
                whole = g[me.c, y, z, x, :, lo : lo + width].astype(F32)
                for n in range(3):
                    whole = whole + came[n, i, j, k].astype(F32)
                return whole

            if stage == 2:
                whole = summed(me.y, me.z, me.x, 0, 0, 0)
                for i in range(4):
                    ng_out[i, :, lo : lo + width] = whole[4 * i : 4 * i + 4]
            else:

                @pl.loop(0, 4 ** len(left))
                def _(n, left=left, lo=lo, width=width, summed=summed):
                    at = {a: me.at(a) for a in "yzx"}
                    slot = {a: 0 for a in "yzx"}
                    for a in left:
                        at[a] = slot[a] = lax.rem(n, 4)
                        n = lax.div(n, 4)
                    whole = summed(at["y"], at["z"], at["x"], slot["y"], slot["z"], slot["x"])
                    g[me.c, at["y"], at["z"], at["x"], :, lo : lo + width] = whole.astype(BF16)

    ng_in[me.x] = ng_out[me.x]
    for k in (1, 2, 3):
        x_copy(4, ng_out, ng_in, k).start()

    losses = loss_blk[me.c, me.y, me.z]
    mine = jnp.zeros((4, LANES), F32)
    for i in range(4):
        mine = jnp.where(me.x == i, losses[4 * i : 4 * i + 4], mine)
    diagonal = lax.broadcasted_iota(jnp.int32, (4, LANES), 0) == lax.broadcasted_iota(
        jnp.int32, (4, LANES), 1
    )
    loss_ref[...] = jnp.sum(jnp.where(diagonal, mine, 0.0), axis=0, keepdims=True)

    for k in (1, 2, 3):
        x_arrival(4, ng_out, ng_in, k).wait_recv()
    norm_grad = jnp.concatenate([ng_in[q] for q in range(4)], axis=1)
    live = me.y_hi * 4 + me.z < 6
    scaled = norm_grad * s_gain_ref[...]
    inner = jnp.mean(scaled * hidden, axis=1, keepdims=True)
    grad = inverse * scaled - hidden * (inverse * inverse * inverse) * inner
    grad_ref[...] = jnp.where(live, grad, 0.0)

    @pl.loop(1, 32)
    def _(k):
        a_copy(k, lax.rem(tp + k, 32)).wait_send()

    for k in (1, 2, 3):
        x_copy(0, stu_out, stu_in, k).wait_send()
        x_copy(1, res_out, res_in, k).wait_send()
        x_copy(4, ng_out, ng_in, k).wait_send()
    for n in range(3):
        tab_copy(n)[0].wait_send()
    sent_all(first_mean + second_mean)
    for copies in student_stages + teacher_stages + [student_swap, teacher_swap]:
        sent_all(copies)
    sent_all(stat_copies + core_copies)


def scratch():
    dma = pltpu.SemaphoreType.DMA
    vm = pltpu.VMEM
    rr = []
    for stage in range(3):
        row = []
        for lo, width, order in PARTS_G:
            spots = [4 if a in order[stage + 1 :] else 1 for a in "yzx"]
            row.append(vm((3, *spots, 16, width), BF16))
        rr.append(tuple(row))
    return {
        "w_t": vm((D_T, VOC), BF16),
        "w_s": vm((D_S, VOC), BF16),
        "rb": vm((32, 16, QT), BF16),
        "tb": vm((2, 4, 4, 4, 16, QT), BF16),
        "sb": vm((2, 4, 4, 4, 16, QS), BF16),
        "res_out": vm((4, 4, QT), BF16),
        "res_in": vm((4, 4, QT), BF16),
        "stu_out": vm((4, 4, QS), BF16),
        "stu_in": vm((4, 4, QS), BF16),
        "asm_t": vm((16, QT), F32),
        "asm_s": vm((16, QS), F32),
        "mean_out": vm((2, 16, LANES), F32),
        "mean_in": vm((2, 4, 16, LANES), F32),
        "tab_own": vm((8, LANES), F32),
        "tab": vm((4, 8, LANES), F32),
        "lab_col": vm((ROWS, LANES), F32),
        "wgt_col": vm((ROWS, LANES), F32),
        "t_log": vm((ROWS, VOC), F32),
        "s_log": vm((ROWS, VOC), F32),
        "lg": vm((ROWS, VOC), BF16),
        "stat": vm((5, 8, ROWS), F32),
        "stat_in": vm((4, 3, 8, ROWS), F32),
        "back": vm((ROWS, LANES), F32),
        "loss_blk": vm((2, 4, 4, 16, LANES), F32),
        "g": vm((2, 4, 4, 4, 16, QS), BF16),
        "core_in": vm((4, 4, 4, 16, QS), BF16),
        "rr": tuple(rr),
        "ng_out": vm((4, 4, QS), F32),
        "ng_in": vm((4, 4, QS), F32),
        "sem_w": dma((2,)),
        "a_send": dma((32,)),
        "a_recv": dma((32,)),
        "a_own": dma(()),
        "x_send": dma((5, 3)),
        "x_recv": dma((5, 3)),
        "tab_send": dma((3,)),
        "tab_recv": dma((3,)),
        "ag_send": dma((2, 3, 3, 3)),
        "ag_recv": dma((2, 3, 3, 3)),
        "sib_send": dma((3, 2)),
        "sib_recv": dma((3, 2)),
        "st_send": dma((4, 3)),
        "st_recv": dma((4, 3)),
        "rs_send": dma((3, 3, 3)),
        "rs_recv": dma((3, 3, 3)),
    }


def shards(
    teacher_partial,
    teacher_residual,
    post_gain,
    final_gain,
    teacher_head,
    student_hidden,
    student_gain,
    student_head,
    labels,
    lengths,
):
    whole = pl.BlockSpec(memory_space=pltpu.VMEM)
    place = pl.BlockSpec(memory_space=pl.ANY)
    spaces = scratch()
    names = list(spaces)
    leaves, tree = jax.tree.flatten([spaces[n] for n in names])

    def body(*refs):
        held = jax.tree.unflatten(tree, refs[12:])
        kernel(*refs[:12], **dict(zip(names, held)))

    grad, loss = pl.pallas_call(
        body,
        out_shape=(
            jax.ShapeDtypeStruct((4, D_S), F32),
            jax.ShapeDtypeStruct((1, LANES), F32),
        ),
        in_specs=[
            place,
            whole,
            whole,
            whole,
            place,
            whole,
            whole,
            place,
            whole,
            pl.BlockSpec(memory_space=pltpu.SMEM),
        ],
        out_specs=(whole, whole),
        scratch_shapes=leaves,
        compiler_params=pltpu.CompilerParams(
            collective_id=0, has_side_effects=True, vmem_limit_bytes=60 * 2**20
        ),
        name="distill",
    )(
        teacher_partial,
        teacher_residual,
        post_gain.reshape(1, -1),
        final_gain.reshape(1, -1),
        teacher_head,
        student_hidden,
        student_gain.reshape(1, -1),
        student_head,
        labels.reshape(1, -1),
        lengths,
    )
    return grad, loss[0, :4]


def solution(mesh):
    torus = Mesh(mesh.devices.reshape(2, 2, 2, 4, 4), ("dp_0", "dp_1", "tp_0", "tp_1", "tp_2"))
    return jax.shard_map(
        shards,
        mesh=torus,
        in_specs=(
            P(TP, DP, None),
            P(DP_TP, None),
            P(),
            P(),
            P(None, DP_TP),
            P(DP_TP, None),
            P(),
            P(None, DP_TP),
            P(DP),
            P(DP, None),
        ),
        out_specs=(P(DP_TP, None), P(DP_TP)),
        check_vma=False,
    )
```

```python
import functools
import itertools

import jax
import jax.numpy as jnp
from jax import lax
from jax.experimental import pallas as pl
from jax.experimental.pallas import tpu as pltpu
from jax.sharding import Mesh
from jax.sharding import PartitionSpec as P

TP = ("tp_0", "tp_1", "tp_2")
DP = ("dp_0", "dp_1")
DP_TP = ("dp_0", "dp_1", "tp_0", "tp_1", "tp_2")
MESH = pl.DeviceIdType.MESH

EPS = 1e-06
BETA = 0.5
LOSS_SCALE = 1024.0

F32 = jnp.float32
BF16 = jnp.bfloat16

D_T = 4608
D_S = 3584
QT = D_T // 4
QS = D_S // 4
VOC = 1024
ROWS = 384
HALF = 192
NSEQ = 8
LANES = 128

PARTS_A = ((0, 384, "x", "hz"), (384, 384, "z", "hx"), (768, 384, "h", "zx"))
PARTS_T = ((0, 384, "x", "y", "z"), (384, 384, "x", "z", "y"), (768, 384, "", "yz", "x"))
PARTS_S = ((0, 256, "xyz"), (256, 384, "yzx"), (640, 256, "zxy"))
PARTS_G = ((0, 256, "zyx"), (256, 384, "xzy"), (640, 256, "yxz"))


def live_pieces():
    held = []
    for c in range(2):
        held += [(c, y, z) for y in range(2) for z in range(4)]
        held += [(c, y, z) for y in range(2, 4) for z in range(2)]
    return held


PIECES = live_pieces()


class Place:
    def __init__(self):
        self.c = lax.axis_index("dp_1")
        self.z = lax.axis_index("tp_1")
        self.x = lax.axis_index("tp_2")
        self.y_lo = lax.axis_index("dp_0")
        self.y_hi = lax.axis_index("tp_0")
        self.y = self.y_hi * 2 + self.y_lo

    def at(self, axis):
        return {"x": self.x, "y": self.y, "z": self.z, "h": self.y_hi}[axis]

    def shifted(self, axis, k):
        return lax.rem(self.at(axis) + k, 2 if axis == "h" else 4)

    def to(self, **spots):
        y_lo, y_hi = self.y_lo, self.y_hi
        if "y" in spots:
            y_lo, y_hi = lax.rem(spots["y"], 2), lax.div(spots["y"], 2)
        y_hi = spots.get("h", y_hi)
        return (y_lo, self.c, y_hi, spots.get("z", self.z), spots.get("x", self.x))

    def along(self, axis, to):
        return self.to(**{axis: to})

    def offsets(self, axes):
        sizes = [2 if a == "h" else 4 for a in axes]
        for ks in itertools.product(*[range(n) for n in sizes]):
            if any(ks):
                sent = {a: self.shifted(a, k) for a, k in zip(axes, ks)}
                heard = {a: self.shifted(a, n - k) for a, k, n in zip(axes, ks, sizes)}
                yield (sent, heard)

    def sibling(self):
        return (self.y_lo, 1 - self.c, self.y_hi, self.z, self.x)


def remote(src, dst, send, recv, to):
    return pltpu.make_async_remote_copy(
        src_ref=src, dst_ref=dst, send_sem=send, recv_sem=recv, device_id=to, device_id_type=MESH
    )


def kernel(
    partial_ref,
    residual_ref,
    post_ref,
    final_ref,
    t_head_ref,
    hidden_ref,
    s_gain_ref,
    s_head_ref,
    labels_ref,
    lengths_ref,
    grad_ref,
    loss_ref,
    w_t,
    w_s,
    pb,
    first_in,
    second_in,
    rows_in,
    tb,
    sb,
    res_in,
    stu_out,
    stu_in,
    asm_t,
    asm_s,
    normed,
    tab_own,
    tab,
    lab_col,
    wgt_col,
    t_log,
    s_log,
    lg,
    stat,
    stat_in,
    back,
    loss_blk,
    g,
    core_in,
    rr,
    ng_out,
    ng_in,
    sem_w,
    a_own,
    f_send,
    f_recv,
    h_send,
    h_recv,
    x_send,
    x_recv,
    tab_send,
    tab_recv,
    ag_send,
    ag_recv,
    sib_send,
    sib_recv,
    st_send,
    st_recv,
    rs_send,
    rs_recv,
):
    me = Place()
    tp = me.y_hi * 16 + me.z * 4 + me.x
    dp = me.y_lo * 2 + me.c
    position = dp * 32 + tp

    load_s = pltpu.make_async_copy(s_head_ref, w_s, sem_w.at[0])
    load_t = pltpu.make_async_copy(t_head_ref, w_t, sem_w.at[1])
    load_s.start()
    load_t.start()

    own_copies = []
    for q in range(4):
        copy = pltpu.make_async_copy(
            partial_ref.at[:, :, :, pl.ds(q * QT, QT)], pb.at[:, :, q], a_own.at[q]
        )
        copy.start()
        own_copies.append(copy)

    barrier = pltpu.get_barrier_semaphore()
    near = [me.to(**sent) for sent, heard in me.offsets("yz")]
    near += [me.along("x", me.shifted("x", k)) for k in (1, 2, 3)]
    for k in (1, 2, 3):
        near += [me.to(x=me.shifted("x", k), z=me.shifted("z", n)) for n in (1, 2, 3)]
        near += [me.to(x=me.shifted("x", k), h=1 - me.y_hi)]
    near += [me.sibling(), (1 - me.y_lo, 1 - me.c, me.y_hi, me.z, me.x)]
    for to in near:
        pl.semaphore_signal(barrier, inc=1, device_id=to, device_id_type=MESH)
    pl.semaphore_wait(barrier, len(near))

    opened = []

    def start_all(copies):
        for sent, unused in copies:
            sent.start()
        opened.extend(copies)

    def arrive_all(copies):
        for unused, arrived in copies:
            arrived.wait_recv()

    for copy in own_copies:
        copy.wait()

    def pb_box(spots, lo, width):
        where = [pl.ds(spots[a], 1) if a in spots else slice(None) for a in "hzx"]
        return pb.at[where[0], where[1], where[2], :, pl.ds(lo, width)]

    first_stage, second_stage = [], []
    for p, (lo, width, axis, plane) in enumerate(PARTS_A):
        for n, (sent, heard) in enumerate(me.offsets(axis)):
            copy = remote(
                pb_box(sent, lo, width),
                first_in[p].at[n],
                f_send.at[p, n],
                f_recv.at[p, n],
                me.to(**sent),
            )
            first_stage.append((copy, copy))
        for n, (sent, heard) in enumerate(me.offsets(plane)):
            spots = {axis: me.at(axis), **sent}
            src = pb.at[spots["h"], spots["z"], spots["x"], :, pl.ds(lo, width)]
            copy = remote(
                src, second_in[p].at[n], h_send.at[p, n], h_recv.at[p, n], me.to(**sent)
            )
            second_stage.append((copy, copy))

    hidden = hidden_ref[...].astype(F32)
    s_gain = s_gain_ref[...].reshape(1, D_S)
    inverse = lax.rsqrt(jnp.mean(hidden * hidden, axis=-1, keepdims=True) + EPS)
    student = (hidden * inverse * s_gain).astype(BF16)
    for q in range(4):
        stu_out[q] = student[:, q * QS : (q + 1) * QS]
    stu_in[me.x] = stu_out[me.x]
    res_in[me.x] = residual_ref[...]

    def x_copy(kind, src, dst, k):
        to = me.shifted("x", k)
        return remote(
            src.at[to],
            dst.at[me.x],
            x_send.at[kind, k - 1],
            x_recv.at[kind, k - 1],
            me.along("x", to),
        )

    def x_arrival(kind, src, dst, k):
        frm = me.shifted("x", 4 - k)
        return remote(
            src.at[frm],
            dst.at[frm],
            x_send.at[kind, k - 1],
            x_recv.at[kind, k - 1],
            me.along("x", frm),
        )

    for k in (1, 2, 3):
        x_copy(0, stu_out, stu_in, k).start()
    start_all(first_stage)

    def spread(kind, own, where):
        copies = []
        for k in (1, 2, 3):
            frm = me.shifted("x", 4 - k)
            sems = (x_send.at[kind, k - 1], x_recv.at[kind, k - 1])
            copies.append(
                (
                    remote(own, where(me.x), *sems, me.along("x", me.shifted("x", k))),
                    remote(own, where(frm), *sems, me.along("x", frm)),
                )
            )
        return copies

    residual_copies = spread(1, residual_ref, lambda i: res_in.at[i])
    start_all(residual_copies)

    lane = lax.broadcasted_iota(jnp.int32, (1, LANES), 1)
    start = jnp.int32(0)
    weight = jnp.zeros((1, LANES), F32)
    for i in range(NSEQ):
        length = lengths_ref[0, i]
        end = start + length
        inside = (lane >= start) & (lane < end)
        share = 1.0 / jnp.full((1, LANES), length, jnp.int32).astype(F32)
        weight = jnp.where(inside, share, weight)
        start = end
    sub = lax.broadcasted_iota(jnp.int32, (8, LANES), 0)
    label_row = labels_ref[...].astype(F32)
    tab_own[...] = jnp.where(
        sub == 0,
        jnp.broadcast_to(label_row, (8, LANES)),
        jnp.where(sub == 1, jnp.broadcast_to(weight, (8, LANES)), 0.0),
    )
    tab[dp] = tab_own[...]
    dp_peers = ((0, 1), (1, 0), (1, 1))

    def tab_copy(n):
        dy, dc = dp_peers[n]
        y_lo = 1 - me.y_lo if dy else me.y_lo
        c = 1 - me.c if dc else me.c
        to = (y_lo, c, me.y_hi, me.z, me.x)
        return (
            remote(tab_own, tab.at[dp], tab_send.at[n], tab_recv.at[n], to),
            remote(tab_own, tab.at[y_lo * 2 + c], tab_send.at[n], tab_recv.at[n], to),
        )

    for n in range(3):
        tab_copy(n)[0].start()

    def box(buf, spots, done, lo, width):
        where = []
        for a in "yzx":
            where.append(pl.ds(0, 4) if a in done else pl.ds(spots.get(a, me.at(a)), 1))
        return buf.at[me.c, where[0], where[1], where[2], :, pl.ds(lo, width)]

    def gather(which, buf, parts, stage):
        out = []
        for p, (lo, width, order) in enumerate(parts):
            axis, done = order[stage], order[:stage]
            out += one_part(which, buf, stage, p, lo, width, axis, done)
        return out

    def one_part(which, buf, stage, p, lo, width, axes, done):
        out = []
        own = box(buf, {}, done, lo, width)
        for n, (sent, heard) in enumerate(me.offsets(axes)):
            sems = (ag_send.at[which, stage, p, n], ag_recv.at[which, stage, p, n])
            theirs = box(buf, heard, done, lo, width)
            out.append(
                (remote(own, own, *sems, me.to(**sent)), remote(theirs, theirs, *sems, me.to(**heard)))
            )
        return out

    def swap(which, buf):
        out = []
        for n, (y, z) in enumerate(((pl.ds(0, 2), pl.ds(0, 4)), (pl.ds(2, 2), pl.ds(0, 2)))):
            sems = (sib_send.at[which, n], sib_recv.at[which, n])
            own, theirs = buf.at[me.c, y, z], buf.at[1 - me.c, y, z]
            out.append(
                (remote(own, own, *sems, me.sibling()), remote(theirs, theirs, *sems, me.sibling()))
            )
        return out

    student_stages = [gather(1, sb, PARTS_S, s) for s in range(3)]
    teacher_stages = [[], []]
    for p, (lo, width, done, first, second) in enumerate(PARTS_T):
        teacher_stages[0] += one_part(0, tb, 0, p, lo, width, first, done)
        teacher_stages[1] += one_part(0, tb, 1, p, lo, width, second, done + first)
    student_swap, teacher_swap = swap(1, sb), swap(0, tb)

    for k in (1, 2, 3):
        x_arrival(0, stu_out, stu_in, k).wait_recv()
    for i in range(4):
        asm_s[4 * i : 4 * i + 4, :] = stu_in[i].astype(F32)
    sb[me.c, me.y, me.z, me.x] = asm_s[...].astype(BF16)
    start_all(student_stages[0])

    arrive_all(first_stage)
    for p, (lo, width, axis, plane) in enumerate(PARTS_A):
        came = first_in[p]
        count = came.shape[0]

        @pl.loop(0, came.shape[1] * came.shape[2] * came.shape[3])
        def _(n, lo=lo, width=width, axis=axis, plane=plane, came=came, count=count):
            at, slot = {axis: me.at(axis)}, {axis: 0}
            for a in reversed(plane):
                size = 2 if a == "h" else 4
                at[a] = slot[a] = lax.rem(n, size)
                n = lax.div(n, size)
            cols = slice(lo, lo + width)
            whole = pb[at["h"], at["z"], at["x"], :, cols].astype(F32)
            for i in range(count):
                whole = whole + came[i, slot["h"], slot["z"], slot["x"]].astype(F32)
            pb[at["h"], at["z"], at["x"], :, cols] = whole.astype(BF16)

    start_all(second_stage)
    arrive_all(student_stages[0])
    start_all(student_stages[1])
    arrive_all(residual_copies)
    for q in range(4):
        for i in range(4):
            asm_t[q, 4 * i : 4 * i + 4, :] = res_in[i, :, q * QT : (q + 1) * QT].astype(F32)
    arrive_all(second_stage)
    for p, (lo, width, axis, plane) in enumerate(PARTS_A):
        whole = pb[me.y_hi, me.z, me.x, :, lo : lo + width].astype(F32)
        for n in range(second_in[p].shape[0]):
            whole = whole + second_in[p][n].astype(F32)
        rows_in[me.x, :, lo : lo + width] = whole.astype(BF16)

    row_copies = spread(2, rows_in.at[me.x], lambda i: rows_in.at[i])
    start_all(row_copies)
    arrive_all(student_stages[1])
    start_all(student_stages[2])
    arrive_all(row_copies)

    def row_inverse(quarters):
        total = sum(jnp.sum(v * v, axis=1, keepdims=True) for v in quarters)
        return lax.rsqrt(total / D_T + EPS)

    sums = [rows_in[q].astype(F32) for q in range(4)]
    scale = row_inverse(sums)
    for q in range(4):
        cols = slice(q * QT, (q + 1) * QT)
        asm_t[q] = asm_t[q] + sums[q] * scale * post_ref[cols].reshape(1, QT)
    scale = row_inverse([asm_t[q] for q in range(4)])
    for q in range(4):
        cols = slice(q * QT, (q + 1) * QT)
        normed[q] = (asm_t[q] * scale * final_ref[cols].reshape(1, QT)).astype(BF16)
    for lo, width, done, first, second in PARTS_T:
        cols = slice(lo, lo + width)
        if done:
            for q in range(4):
                tb[me.c, me.y, me.z, q, :, cols] = normed[q, :, cols]
        else:
            tb[me.c, me.y, me.z, me.x, :, cols] = normed[me.x, :, cols]
    start_all(teacher_stages[0])

    for n in range(3):
        tab_copy(n)[1].wait_recv()
    for group in range(4):
        table = tab[group]
        for row, col in ((0, lab_col), (1, wgt_col)):
            turned = jnp.broadcast_to(table[row : row + 1, :], (LANES, LANES)).T
            for m, (c, y, z) in enumerate(PIECES):
                if (y % 2) * 2 + c == group:
                    j = (y // 2) * 4 + z
                    col[m * 16 : (m + 1) * 16, :] = turned[j * 16 : (j + 1) * 16, :]
    g[:, 2:4, 2:4] = jnp.zeros((2, 2, 2, 4, 16, QS), BF16)
    loss_blk[:, 2:4, 2:4] = jnp.zeros((2, 2, 2, 16, LANES), F32)

    arrive_all(teacher_stages[0])
    start_all(teacher_stages[1])
    arrive_all(student_stages[2])
    start_all(student_swap)

    def logits(buf, head, out, width, core):
        rows = pl.ds(pl.multiple_of(core * HALF, HALF), HALF)

        @pl.loop(0, VOC // 256)
        def _(n):
            cols = pl.ds(pl.multiple_of(n * 256, 256), 256)
            acc = None
            for q in range(4):
                live = jnp.concatenate(
                    [
                        buf[core, 0:2, :, q].reshape(128, width),
                        buf[core, 2:4, 0:2, q].reshape(64, width),
                    ],
                    axis=0,
                )
                head_rows = head[q * width : (q + 1) * width, cols]
                term = jnp.dot(live, head_rows, preferred_element_type=F32)
                acc = term if acc is None else acc + term
            out[rows, cols] = acc

    load_s.wait()
    logits(sb, w_s, s_log, QS, me.c)
    arrive_all(student_swap)
    logits(sb, w_s, s_log, QS, 1 - me.c)
    load_t.wait()
    arrive_all(teacher_stages[1])
    start_all(teacher_swap)
    logits(tb, w_t, t_log, QT, me.c)
    arrive_all(teacher_swap)
    logits(tb, w_t, t_log, QT, 1 - me.c)

    first_col = (position * VOC).astype(F32)

    def columns():
        return lax.broadcasted_iota(jnp.int32, (32, VOC), 1).astype(F32) + first_col

    lanes = lax.broadcasted_iota(jnp.int32, (32, LANES), 1)

    @pl.loop(0, ROWS // 32)
    def _(r):
        rows = pl.ds(pl.multiple_of(r * 32, 32), 32)
        t, s = t_log[rows, :], s_log[rows, :]
        t_max = jnp.max(t, axis=1, keepdims=True)
        s_max = jnp.max(s, axis=1, keepdims=True)
        t_exp = jnp.exp(t - t_max)
        t_sum = jnp.sum(t_exp, axis=1, keepdims=True)
        cross = jnp.sum(t_exp * (t - s), axis=1, keepdims=True)
        s_sum = jnp.sum(jnp.exp(s - s_max), axis=1, keepdims=True)
        hit = columns() == lab_col[rows, 0:1]
        value = jnp.sum(jnp.where(hit, s, 0.0), axis=1, keepdims=True)
        held = wgt_col[rows, :]
        for n, one in enumerate((t_max, t_sum, cross, s_max, s_sum, value)):
            held = jnp.where(lanes == n, one, held)
        back[rows, :] = held

    for i in range(3):
        turned = back[i * 128 : (i + 1) * 128, :].T
        stat[0, :, i * 128 : (i + 1) * 128] = turned[0:8, :]

    def merged(values):
        t_max = functools.reduce(jnp.maximum, [v[0:1] for v in values])
        s_max = functools.reduce(jnp.maximum, [v[3:4] for v in values])
        t_sum = cross = s_sum = label = 0.0
        for v in values:
            t_one = jnp.exp(v[0:1] - t_max)
            s_one = jnp.exp(v[3:4] - s_max)
            t_sum += v[1:2] * t_one
            cross += v[2:3] * t_one
            s_sum += v[4:5] * s_one
            label += v[5:6]
        return [t_max, t_sum, cross, s_max, s_sum, label, values[0][6:7]]

    for n, axis in enumerate("cxyz"):
        copies = []
        for k in (1,) if axis == "c" else (1, 2, 3):
            sems = (st_send.at[n, k - 1], st_recv.at[n, k - 1])
            dst = stat_in.at[n, k - 1]
            to = me.sibling() if axis == "c" else me.along(axis, me.shifted(axis, k))
            copy = remote(stat.at[n], dst, *sems, to)
            copies.append((copy, copy))
        start_all(copies)
        arrive_all(copies)
        values = [stat[n]] + [stat_in[n, k] for k in range(len(copies))]
        for i, line in enumerate(merged(values)):
            stat[n + 1, i : i + 1, :] = line

    end = stat[4]
    t_whole = end[0:1] + jnp.log(end[1:2])
    s_whole = end[3:4] + jnp.log(end[4:5])
    divergence = end[2:3] / end[1:2] - t_whole + s_whole
    row_loss = jnp.where(end[6:7] > 0, divergence + BETA * (s_whole - end[5:6]), 0.0)
    sub = lax.broadcasted_iota(jnp.int32, (8, ROWS), 0)
    lines = jnp.zeros((8, ROWS), F32)
    for n, one in enumerate((t_whole, s_whole, row_loss)):
        lines = jnp.where(sub == n, jnp.broadcast_to(one, (8, ROWS)), lines)
    for i in range(3):
        tall = jnp.concatenate(
            [lines[:, i * 128 : (i + 1) * 128], jnp.zeros((120, LANES), F32)], axis=0
        )
        back[i * 128 : (i + 1) * 128, :] = tall.T
    for m, (c, y, z) in enumerate(PIECES):
        loss_blk[c, y, z] = jnp.broadcast_to(back[m * 16 : (m + 1) * 16, 2:3], (16, LANES))

    @pl.loop(0, ROWS // 32)
    def _(r):
        rows = pl.ds(pl.multiple_of(r * 32, 32), 32)
        t_prob = jnp.exp(t_log[rows, :] - back[rows, 0:1])
        s_prob = jnp.exp(s_log[rows, :] - back[rows, 1:2])
        hit = (columns() == lab_col[rows, 0:1]).astype(F32)
        scale = LOSS_SCALE * wgt_col[rows, 0:1]
        lg[rows, :] = (scale * ((1.0 + BETA) * s_prob - t_prob - BETA * hit)).astype(BF16)

    for q in range(4):
        for lo in range(0, QS, 128 * 7):
            width = min(128 * 7, QS - lo)
            share = lax.dot_general(
                lg[...],
                w_s[q * QS + lo : q * QS + lo + width, :],
                (((1,), (1,)), ((), ())),
                preferred_element_type=F32,
            ).astype(BF16)
            cols = slice(lo, lo + width)
            for c in range(2):
                own = share[c * HALF : (c + 1) * HALF]
                g[c, 0:2, :, q, :, cols] = own[0:128].reshape(2, 4, 16, width)
                g[c, 2:4, 0:2, q, :, cols] = own[128:192].reshape(2, 2, 16, width)

    core_copies = []
    for n, (y, z) in enumerate(((pl.ds(0, 2), pl.ds(0, 4)), (pl.ds(2, 2), pl.ds(0, 2)))):
        copy = remote(
            g.at[1 - me.c, y, z],
            core_in.at[y, z],
            sib_send.at[2, n],
            sib_recv.at[2, n],
            me.sibling(),
        )
        core_copies.append((copy, copy))
    start_all(core_copies)
    arrive_all(core_copies)
    for ys, zs in (((0, 1), 4), ((2, 3), 2)):
        for y in ys:

            @pl.loop(0, zs * 4)
            def _(i, y=y):
                z, x = lax.div(i, 4), lax.rem(i, 4)
                both = g[me.c, y, z, x].astype(F32) + core_in[y, z, x].astype(F32)
                g[me.c, y, z, x] = both.astype(BF16)

    totals = []
    for stage in range(3):
        made = []
        for p, (lo, width, order) in enumerate(PARTS_G):
            axis, left = order[stage], order[stage + 1 :]
            for k in (1, 2, 3):
                to = me.shifted(axis, k)
                copy = remote(
                    box(g, {axis: to}, left, lo, width),
                    rr[stage][p].at[k - 1],
                    rs_send.at[stage, p, k - 1],
                    rs_recv.at[stage, p, k - 1],
                    me.along(axis, to),
                )
                made.append((copy, copy))
        start_all(made)
        arrive_all(made)
        for p, (lo, width, order) in enumerate(PARTS_G):
            left = order[stage + 1 :]
            came = rr[stage][p]

            def summed(y, z, x, i, j, k):
                whole = g[me.c, y, z, x, :, lo : lo + width].astype(F32)
                for n in range(3):
                    whole = whole + came[n, i, j, k].astype(F32)
                return whole

            if stage == 2:
                whole = summed(me.y, me.z, me.x, 0, 0, 0)
                for i in range(4):
                    ng_out[i, :, lo : lo + width] = whole[4 * i : 4 * i + 4]
            else:

                @pl.loop(0, 4 ** len(left))
                def _(n, left=left, lo=lo, width=width, summed=summed):
                    at = {a: me.at(a) for a in "yzx"}
                    slot = {a: 0 for a in "yzx"}
                    for a in left:
                        at[a] = slot[a] = lax.rem(n, 4)
                        n = lax.div(n, 4)
                    whole = summed(at["y"], at["z"], at["x"], slot["y"], slot["z"], slot["x"])
                    g[me.c, at["y"], at["z"], at["x"], :, lo : lo + width] = whole.astype(BF16)

    ng_in[me.x] = ng_out[me.x]
    for k in (1, 2, 3):
        x_copy(4, ng_out, ng_in, k).start()

    losses = loss_blk[me.c, me.y, me.z]
    mine = jnp.zeros((4, LANES), F32)
    for i in range(4):
        mine = jnp.where(me.x == i, losses[4 * i : 4 * i + 4], mine)
    diagonal = lax.broadcasted_iota(jnp.int32, (4, LANES), 0) == lax.broadcasted_iota(
        jnp.int32, (4, LANES), 1
    )
    loss_ref[...] = jnp.sum(jnp.where(diagonal, mine, 0.0), axis=0, keepdims=True)

    for k in (1, 2, 3):
        x_arrival(4, ng_out, ng_in, k).wait_recv()
    norm_grad = jnp.concatenate([ng_in[q] for q in range(4)], axis=1)
    live = me.y_hi * 4 + me.z < 6
    scaled = norm_grad * s_gain
    inner = jnp.mean(scaled * hidden, axis=1, keepdims=True)
    grad = inverse * scaled - hidden * (inverse * inverse * inverse) * inner
    grad_ref[...] = jnp.where(live, grad, 0.0)

    for k in (1, 2, 3):
        x_copy(0, stu_out, stu_in, k).wait_send()
        x_copy(4, ng_out, ng_in, k).wait_send()
    for n in range(3):
        tab_copy(n)[0].wait_send()
    for sent, unused in opened:
        sent.wait_send()


def scratch():
    dma = pltpu.SemaphoreType.DMA
    vm = pltpu.VMEM
    first = []
    for lo, width, axis, plane in PARTS_A:
        spots = [1 if a == axis else 2 if a == "h" else 4 for a in "hzx"]
        first.append(vm((1 if axis == "h" else 3, *spots, 16, width), BF16))
    rr = []
    for stage in range(3):
        row = []
        for lo, width, order in PARTS_G:
            spots = [4 if a in order[stage + 1 :] else 1 for a in "yzx"]
            row.append(vm((3, *spots, 16, width), BF16))
        rr.append(tuple(row))
    return {
        "w_t": vm((D_T, VOC), BF16),
        "w_s": vm((D_S, VOC), BF16),
        "pb": vm((2, 4, 4, 16, QT), BF16),
        "first_in": tuple(first),
        "second_in": tuple(vm((n, 16, PARTS_A[0][1]), BF16) for n in (7, 7, 15)),
        "rows_in": vm((4, 16, QT), BF16),
        "tb": vm((2, 4, 4, 4, 16, QT), BF16),
        "sb": vm((2, 4, 4, 4, 16, QS), BF16),
        "res_in": vm((4, 4, D_T), BF16),
        "stu_out": vm((4, 4, QS), BF16),
        "stu_in": vm((4, 4, QS), BF16),
        "asm_t": vm((4, 16, QT), F32),
        "asm_s": vm((16, QS), F32),
        "normed": vm((4, 16, QT), BF16),
        "tab_own": vm((8, LANES), F32),
        "tab": vm((4, 8, LANES), F32),
        "lab_col": vm((ROWS, LANES), F32),
        "wgt_col": vm((ROWS, LANES), F32),
        "t_log": vm((ROWS, VOC), F32),
        "s_log": vm((ROWS, VOC), F32),
        "lg": vm((ROWS, VOC), BF16),
        "stat": vm((5, 8, ROWS), F32),
        "stat_in": vm((4, 3, 8, ROWS), F32),
        "back": vm((ROWS, LANES), F32),
        "loss_blk": vm((2, 4, 4, 16, LANES), F32),
        "g": vm((2, 4, 4, 4, 16, QS), BF16),
        "core_in": vm((4, 4, 4, 16, QS), BF16),
        "rr": tuple(rr),
        "ng_out": vm((4, 4, QS), F32),
        "ng_in": vm((4, 4, QS), F32),
        "sem_w": dma((2,)),
        "a_own": dma((4,)),
        "f_send": dma((3, 3)),
        "f_recv": dma((3, 3)),
        "h_send": dma((3, 15)),
        "h_recv": dma((3, 15)),
        "x_send": dma((5, 3)),
        "x_recv": dma((5, 3)),
        "tab_send": dma((3,)),
        "tab_recv": dma((3,)),
        "ag_send": dma((2, 3, 3, 15)),
        "ag_recv": dma((2, 3, 3, 15)),
        "sib_send": dma((3, 2)),
        "sib_recv": dma((3, 2)),
        "st_send": dma((4, 3)),
        "st_recv": dma((4, 3)),
        "rs_send": dma((3, 3, 3)),
        "rs_recv": dma((3, 3, 3)),
    }


def shards(
    teacher_partial,
    teacher_residual,
    post_gain,
    final_gain,
    teacher_head,
    student_hidden,
    student_gain,
    student_head,
    labels,
    lengths,
):
    whole = pl.BlockSpec(memory_space=pltpu.VMEM)
    place = pl.BlockSpec(memory_space=pl.ANY)
    spaces = scratch()
    names = list(spaces)
    leaves, tree = jax.tree.flatten([spaces[n] for n in names])

    def body(*refs):
        held = jax.tree.unflatten(tree, refs[12:])
        kernel(*refs[:12], **dict(zip(names, held)))

    grad, loss = pl.pallas_call(
        body,
        out_shape=(
            jax.ShapeDtypeStruct((4, D_S), F32),
            jax.ShapeDtypeStruct((1, LANES), F32),
        ),
        in_specs=[
            place,
            whole,
            whole,
            whole,
            place,
            whole,
            whole,
            place,
            whole,
            pl.BlockSpec(memory_space=pltpu.SMEM),
        ],
        out_specs=(whole, whole),
        scratch_shapes=leaves,
        compiler_params=pltpu.CompilerParams(
            collective_id=0, has_side_effects=True, vmem_limit_bytes=60 * 2**20
        ),
        name="distill",
    )(
        teacher_partial.reshape(2, 4, 16, D_T),
        teacher_residual,
        post_gain,
        final_gain,
        teacher_head,
        student_hidden,
        student_gain,
        student_head,
        labels.reshape(1, -1),
        lengths,
    )
    return grad, loss[0, :4]


def solution(mesh):
    torus = Mesh(mesh.devices.reshape(2, 2, 2, 4, 4), ("dp_0", "dp_1", "tp_0", "tp_1", "tp_2"))
    return jax.shard_map(
        shards,
        mesh=torus,
        in_specs=(
            P(TP, DP, None),
            P(DP_TP, None),
            P(),
            P(),
            P(None, DP_TP),
            P(DP_TP, None),
            P(),
            P(None, DP_TP),
            P(DP),
            P(DP, None),
        ),
        out_specs=(P(DP_TP, None), P(DP_TP)),
        check_vma=False,
    )
```

```python
import functools
import itertools

import jax
import jax.numpy as jnp
from jax import lax
from jax.experimental import pallas as pl
from jax.experimental.pallas import tpu as pltpu
from jax.sharding import Mesh
from jax.sharding import PartitionSpec as P

TP = ("tp_0", "tp_1", "tp_2")
DP = ("dp_0", "dp_1")
DP_TP = ("dp_0", "dp_1", "tp_0", "tp_1", "tp_2")
MESH = pl.DeviceIdType.MESH

EPS = 1e-06
BETA = 0.5
LOSS_SCALE = 1024.0

F32 = jnp.float32
BF16 = jnp.bfloat16

D_T = 4608
D_S = 3584
QT = D_T // 4
QS = D_S // 4
VOC = 1024
ROWS = 384
HALF = 192
NSEQ = 8
LANES = 128

PARTS_A = ((0, 384, "x", "hz"), (384, 384, "z", "hx"), (768, 384, "h", "zx"))
PARTS_T = ((0, 384, "x", "y", "z"), (384, 384, "x", "z", "y"), (768, 384, "", "yz", "x"))
PARTS_S = ((0, 256, "xyz"), (256, 384, "yzx"), (640, 256, "zxy"))
PARTS_G = ((0, 256, "z", "y"), (256, 256, "y", "z"))
LO_X, W_X = (512, 384)
W_YZ = 512


def live_pieces():
    held = []
    for c in range(2):
        held += [(c, y, z) for y in range(2) for z in range(4)]
        held += [(c, y, z) for y in range(2, 4) for z in range(2)]
    return held


PIECES = live_pieces()
LIVE = ((pl.ds(0, 2), pl.ds(0, 4)), (pl.ds(2, 2), pl.ds(0, 2)))


class Place:
    def __init__(self):
        self.c = lax.axis_index("dp_1")
        self.z = lax.axis_index("tp_1")
        self.x = lax.axis_index("tp_2")
        self.y_lo = lax.axis_index("dp_0")
        self.y_hi = lax.axis_index("tp_0")
        self.y = self.y_hi * 2 + self.y_lo

    def at(self, axis):
        return {"x": self.x, "y": self.y, "z": self.z, "h": self.y_hi}[axis]

    def shifted(self, axis, k):
        return lax.rem(self.at(axis) + k, 2 if axis == "h" else 4)

    def to(self, **spots):
        y_lo, y_hi = self.y_lo, self.y_hi
        if "y" in spots:
            y_lo, y_hi = lax.rem(spots["y"], 2), lax.div(spots["y"], 2)
        y_hi = spots.get("h", y_hi)
        return (y_lo, self.c, y_hi, spots.get("z", self.z), spots.get("x", self.x))

    def along(self, axis, to):
        return self.to(**{axis: to})

    def offsets(self, axes):
        sizes = [2 if a == "h" else 4 for a in axes]
        for ks in itertools.product(*[range(n) for n in sizes]):
            if any(ks):
                sent = {a: self.shifted(a, k) for a, k in zip(axes, ks)}
                heard = {a: self.shifted(a, n - k) for a, k, n in zip(axes, ks, sizes)}
                yield (sent, heard)

    def sibling(self):
        return (self.y_lo, 1 - self.c, self.y_hi, self.z, self.x)


def remote(src, dst, send, recv, to):
    return pltpu.make_async_remote_copy(
        src_ref=src, dst_ref=dst, send_sem=send, recv_sem=recv, device_id=to, device_id_type=MESH
    )


def kernel(
    partial_ref,
    residual_ref,
    post_ref,
    final_ref,
    t_head_ref,
    hidden_ref,
    s_gain_ref,
    s_head_ref,
    labels_ref,
    lengths_ref,
    grad_ref,
    loss_ref,
    w_t,
    w_s,
    pb,
    first_in,
    second_in,
    rows_in,
    tb,
    sb,
    res_in,
    stu_out,
    stu_in,
    asm_t,
    asm_s,
    normed,
    tab_own,
    tab,
    lab_col,
    wgt_col,
    t_log,
    s_log,
    lg,
    stat,
    stat_in,
    back,
    loss_blk,
    g,
    core_in,
    rr0,
    rr_x,
    rr1,
    rr2,
    ng_out,
    ng_in,
    sem_w,
    a_own,
    f_send,
    f_recv,
    h_send,
    h_recv,
    x_send,
    x_recv,
    tab_send,
    tab_recv,
    ag_send,
    ag_recv,
    sib_send,
    sib_recv,
    st_send,
    st_recv,
    cs_send,
    cs_recv,
    rs_send,
    rs_recv,
    rx_send,
    rx_recv,
    r1_send,
    r1_recv,
    r2_send,
    r2_recv,
):
    me = Place()
    tp = me.y_hi * 16 + me.z * 4 + me.x
    dp = me.y_lo * 2 + me.c
    position = dp * 32 + tp

    load_s = pltpu.make_async_copy(s_head_ref, w_s, sem_w.at[0])
    load_t = pltpu.make_async_copy(t_head_ref, w_t, sem_w.at[1])
    own_copies = []
    for q in range(4):
        copy = pltpu.make_async_copy(
            partial_ref.at[:, :, :, pl.ds(q * QT, QT)], pb.at[:, :, q], a_own.at[q]
        )
        copy.start()
        own_copies.append(copy)

    barrier = pltpu.get_barrier_semaphore()
    near = [me.to(**sent) for sent, heard in me.offsets("yz")]
    near += [me.along("x", me.shifted("x", k)) for k in (1, 2, 3)]
    for k in (1, 2, 3):
        near += [me.to(x=me.shifted("x", k), z=me.shifted("z", n)) for n in (1, 2, 3)]
        near += [me.to(x=me.shifted("x", k), h=1 - me.y_hi)]
    near += [me.sibling(), (1 - me.y_lo, 1 - me.c, me.y_hi, me.z, me.x)]
    for to in near:
        pl.semaphore_signal(barrier, inc=1, device_id=to, device_id_type=MESH)
    pl.semaphore_wait(barrier, len(near))

    opened = []

    def start_all(copies):
        for sent, unused in copies:
            sent.start()
        opened.extend(copies)

    def arrive_all(copies):
        for unused, arrived in copies:
            arrived.wait_recv()

    for copy in own_copies:
        copy.wait()

    def pb_box(spots, lo, width):
        where = [pl.ds(spots[a], 1) if a in spots else slice(None) for a in "hzx"]
        return pb.at[where[0], where[1], where[2], :, pl.ds(lo, width)]

    first_stage, second_stage = [], []
    for p, (lo, width, axis, plane) in enumerate(PARTS_A):
        for n, (sent, heard) in enumerate(me.offsets(axis)):
            copy = remote(
                pb_box(sent, lo, width),
                first_in[p].at[n],
                f_send.at[p, n],
                f_recv.at[p, n],
                me.to(**sent),
            )
            first_stage.append((copy, copy))
        for n, (sent, heard) in enumerate(me.offsets(plane)):
            spots = {axis: me.at(axis), **sent}
            src = pb.at[spots["h"], spots["z"], spots["x"], :, pl.ds(lo, width)]
            copy = remote(
                src, second_in[p].at[n], h_send.at[p, n], h_recv.at[p, n], me.to(**sent)
            )
            second_stage.append((copy, copy))

    start_all(first_stage)
    load_t.start()
    load_s.start()

    hidden = hidden_ref[...].astype(F32)
    s_gain = s_gain_ref[...].reshape(1, D_S)
    inverse = lax.rsqrt(jnp.mean(hidden * hidden, axis=-1, keepdims=True) + EPS)
    student = (hidden * inverse * s_gain).astype(BF16)
    for q in range(4):
        stu_out[q] = student[:, q * QS : (q + 1) * QS]
    stu_in[me.x] = stu_out[me.x]
    res_in[me.x] = residual_ref[...]

    def x_copy(kind, src, dst, k):
        to = me.shifted("x", k)
        return remote(
            src.at[to],
            dst.at[me.x],
            x_send.at[kind, k - 1],
            x_recv.at[kind, k - 1],
            me.along("x", to),
        )

    def x_arrival(kind, src, dst, k):
        frm = me.shifted("x", 4 - k)
        return remote(
            src.at[frm],
            dst.at[frm],
            x_send.at[kind, k - 1],
            x_recv.at[kind, k - 1],
            me.along("x", frm),
        )

    for k in (1, 2, 3):
        x_copy(0, stu_out, stu_in, k).start()
    def spread(kind, own, where):
        copies = []
        for k in (1, 2, 3):
            frm = me.shifted("x", 4 - k)
            sems = (x_send.at[kind, k - 1], x_recv.at[kind, k - 1])
            copies.append(
                (
                    remote(own, where(me.x), *sems, me.along("x", me.shifted("x", k))),
                    remote(own, where(frm), *sems, me.along("x", frm)),
                )
            )
        return copies

    residual_copies = spread(1, residual_ref, lambda i: res_in.at[i])
    start_all(residual_copies)

    lane = lax.broadcasted_iota(jnp.int32, (1, LANES), 1)
    start = jnp.int32(0)
    weight = jnp.zeros((1, LANES), F32)
    for i in range(NSEQ):
        length = lengths_ref[0, i]
        end = start + length
        inside = (lane >= start) & (lane < end)
        share = 1.0 / jnp.full((1, LANES), length, jnp.int32).astype(F32)
        weight = jnp.where(inside, share, weight)
        start = end
    sub = lax.broadcasted_iota(jnp.int32, (8, LANES), 0)
    label_row = labels_ref[...].astype(F32)
    tab_own[...] = jnp.where(
        sub == 0,
        jnp.broadcast_to(label_row, (8, LANES)),
        jnp.where(sub == 1, jnp.broadcast_to(weight, (8, LANES)), 0.0),
    )
    tab[dp] = tab_own[...]
    dp_peers = ((0, 1), (1, 0), (1, 1))

    def tab_copy(n):
        dy, dc = dp_peers[n]
        y_lo = 1 - me.y_lo if dy else me.y_lo
        c = 1 - me.c if dc else me.c
        to = (y_lo, c, me.y_hi, me.z, me.x)
        return (
            remote(tab_own, tab.at[dp], tab_send.at[n], tab_recv.at[n], to),
            remote(tab_own, tab.at[y_lo * 2 + c], tab_send.at[n], tab_recv.at[n], to),
        )

    for n in range(3):
        tab_copy(n)[0].start()

    def box(buf, spots, done, lo, width):
        where = []
        for a in "yzx":
            where.append(pl.ds(0, 4) if a in done else pl.ds(spots.get(a, me.at(a)), 1))
        return buf.at[me.c, where[0], where[1], where[2], :, pl.ds(lo, width)]

    def gather(which, buf, parts, stage):
        out = []
        for p, (lo, width, order) in enumerate(parts):
            axis, done = order[stage], order[:stage]
            out += one_part(which, buf, stage, p, lo, width, axis, done)
        return out

    def one_part(which, buf, stage, p, lo, width, axes, done):
        out = []
        cols = pl.ds(lo, width)
        for n, (sent, heard) in enumerate(me.offsets(axes)):
            if "y" in done and "z" in done:
                boxes = [
                    (buf.at[me.c, y, z, pl.ds(me.x, 1), :, cols], buf.at[me.c, y, z, pl.ds(heard["x"], 1), :, cols])
                    for y, z in LIVE
                ]
            else:
                boxes = [(box(buf, {}, done, lo, width), box(buf, heard, done, lo, width))]
            for i, (own, theirs) in enumerate(boxes):
                at = n * len(boxes) + i
                sems = (ag_send.at[which, stage, p, at], ag_recv.at[which, stage, p, at])
                out.append(
                    (
                        remote(own, own, *sems, me.to(**sent)),
                        remote(theirs, theirs, *sems, me.to(**heard)),
                    )
                )
        return out

    def swap(which, buf):
        out = []
        for n, (y, z) in enumerate(LIVE):
            sems = (sib_send.at[which, n], sib_recv.at[which, n])
            own, theirs = buf.at[me.c, y, z], buf.at[1 - me.c, y, z]
            out.append(
                (remote(own, own, *sems, me.sibling()), remote(theirs, theirs, *sems, me.sibling()))
            )
        return out

    student_stages = [gather(1, sb, PARTS_S, s) for s in range(3)]
    teacher_stages = [[], []]
    for p, (lo, width, done, first, second) in enumerate(PARTS_T):
        teacher_stages[0] += one_part(0, tb, 0, p, lo, width, first, done)
        teacher_stages[1] += one_part(0, tb, 1, p, lo, width, second, done + first)
    student_swap, teacher_swap = swap(1, sb), swap(0, tb)

    for k in (1, 2, 3):
        x_arrival(0, stu_out, stu_in, k).wait_recv()
    for i in range(4):
        asm_s[4 * i : 4 * i + 4, :] = stu_in[i].astype(F32)
    sb[me.c, me.y, me.z, me.x] = asm_s[...].astype(BF16)
    start_all(student_stages[0])

    arrive_all(first_stage)
    for p, (lo, width, axis, plane) in enumerate(PARTS_A):
        came = first_in[p]
        count = came.shape[0]

        @pl.loop(0, came.shape[1] * came.shape[2] * came.shape[3])
        def _(n, lo=lo, width=width, axis=axis, plane=plane, came=came, count=count):
            at, slot = {axis: me.at(axis)}, {axis: 0}
            for a in reversed(plane):
                size = 2 if a == "h" else 4
                at[a] = slot[a] = lax.rem(n, size)
                n = lax.div(n, size)
            cols = slice(lo, lo + width)
            whole = pb[at["h"], at["z"], at["x"], :, cols].astype(F32)
            for i in range(count):
                whole = whole + came[i, slot["h"], slot["z"], slot["x"]].astype(F32)
            pb[at["h"], at["z"], at["x"], :, cols] = whole.astype(BF16)

    start_all(second_stage)
    arrive_all(student_stages[0])
    start_all(student_stages[1])
    arrive_all(residual_copies)
    for q in range(4):
        for i in range(4):
            asm_t[q, 4 * i : 4 * i + 4, :] = res_in[i, :, q * QT : (q + 1) * QT].astype(F32)
    arrive_all(second_stage)
    for p, (lo, width, axis, plane) in enumerate(PARTS_A):
        whole = pb[me.y_hi, me.z, me.x, :, lo : lo + width].astype(F32)
        for n in range(second_in[p].shape[0]):
            whole = whole + second_in[p][n].astype(F32)
        rows_in[me.x, :, lo : lo + width] = whole.astype(BF16)

    row_copies = spread(2, rows_in.at[me.x], lambda i: rows_in.at[i])
    start_all(row_copies)
    arrive_all(row_copies)

    def row_inverse(quarters):
        total = sum(jnp.sum(v * v, axis=1, keepdims=True) for v in quarters)
        return lax.rsqrt(total / D_T + EPS)

    sums = [rows_in[q].astype(F32) for q in range(4)]
    scale = row_inverse(sums)
    for q in range(4):
        cols = slice(q * QT, (q + 1) * QT)
        asm_t[q] = asm_t[q] + sums[q] * scale * post_ref[cols].reshape(1, QT)
    scale = row_inverse([asm_t[q] for q in range(4)])
    for q in range(4):
        cols = slice(q * QT, (q + 1) * QT)
        normed[q] = (asm_t[q] * scale * final_ref[cols].reshape(1, QT)).astype(BF16)
    for lo, width, done, first, second in PARTS_T:
        cols = slice(lo, lo + width)
        if done:
            for q in range(4):
                tb[me.c, me.y, me.z, q, :, cols] = normed[q, :, cols]
        else:
            tb[me.c, me.y, me.z, me.x, :, cols] = normed[me.x, :, cols]
    start_all(teacher_stages[0])

    for n in range(3):
        tab_copy(n)[1].wait_recv()
    for group in range(4):
        table = tab[group]
        for row, col in ((0, lab_col), (1, wgt_col)):
            turned = jnp.broadcast_to(table[row : row + 1, :], (LANES, LANES)).T
            for m, (c, y, z) in enumerate(PIECES):
                if (y % 2) * 2 + c == group:
                    j = (y // 2) * 4 + z
                    col[m * 16 : (m + 1) * 16, :] = turned[j * 16 : (j + 1) * 16, :]
    g[:, 2:4, 2:4] = jnp.zeros((2, 2, 2, 4, 16, QS), BF16)
    loss_blk[:, 2:4, 2:4] = jnp.zeros((2, 2, 2, 16, LANES), F32)

    arrive_all(student_stages[1])
    arrive_all(teacher_stages[0])
    start_all(teacher_stages[1])
    start_all(student_stages[2])

    def logits(buf, head, out, width, core):
        rows = pl.ds(pl.multiple_of(core * HALF, HALF), HALF)

        @pl.loop(0, VOC // 256)
        def _(n):
            cols = pl.ds(pl.multiple_of(n * 256, 256), 256)
            acc = None
            for q in range(4):
                live = jnp.concatenate(
                    [
                        buf[core, 0:2, :, q].reshape(128, width),
                        buf[core, 2:4, 0:2, q].reshape(64, width),
                    ],
                    axis=0,
                )
                head_rows = head[q * width : (q + 1) * width, cols]
                term = jnp.dot(live, head_rows, preferred_element_type=F32)
                acc = term if acc is None else acc + term
            out[rows, cols] = acc

    load_t.wait()
    arrive_all(teacher_stages[1])
    start_all(teacher_swap)
    logits(tb, w_t, t_log, QT, me.c)
    arrive_all(student_stages[2])
    start_all(student_swap)
    arrive_all(teacher_swap)
    logits(tb, w_t, t_log, QT, 1 - me.c)
    load_s.wait()
    logits(sb, w_s, s_log, QS, me.c)
    arrive_all(student_swap)
    logits(sb, w_s, s_log, QS, 1 - me.c)

    first_col = (position * VOC).astype(F32)

    def columns():
        return lax.broadcasted_iota(jnp.int32, (32, VOC), 1).astype(F32) + first_col

    lanes = lax.broadcasted_iota(jnp.int32, (32, LANES), 1)

    @pl.loop(0, ROWS // 32)
    def _(r):
        rows = pl.ds(pl.multiple_of(r * 32, 32), 32)
        t, s = t_log[rows, :], s_log[rows, :]
        t_max = jnp.max(t, axis=1, keepdims=True)
        s_max = jnp.max(s, axis=1, keepdims=True)
        t_exp = jnp.exp(t - t_max)
        t_sum = jnp.sum(t_exp, axis=1, keepdims=True)
        cross = jnp.sum(t_exp * (t - s), axis=1, keepdims=True)
        s_sum = jnp.sum(jnp.exp(s - s_max), axis=1, keepdims=True)
        hit = columns() == lab_col[rows, 0:1]
        value = jnp.sum(jnp.where(hit, s, 0.0), axis=1, keepdims=True)
        held = wgt_col[rows, :]
        for n, one in enumerate((t_max, t_sum, cross, s_max, s_sum, value)):
            held = jnp.where(lanes == n, one, held)
        back[rows, :] = held

    for i in range(3):
        turned = back[i * 128 : (i + 1) * 128, :].T
        stat[0, :, i * 128 : (i + 1) * 128] = turned[0:8, :]

    def merged(values):
        t_max = functools.reduce(jnp.maximum, [v[0:1] for v in values])
        s_max = functools.reduce(jnp.maximum, [v[3:4] for v in values])
        t_sum = cross = s_sum = label = 0.0
        for v in values:
            t_one = jnp.exp(v[0:1] - t_max)
            s_one = jnp.exp(v[3:4] - s_max)
            t_sum += v[1:2] * t_one
            cross += v[2:3] * t_one
            s_sum += v[4:5] * s_one
            label += v[5:6]
        return [t_max, t_sum, cross, s_max, s_sum, label, values[0][6:7]]

    for n, axis in enumerate("cxyz"):
        copies = []
        for k in (1,) if axis == "c" else (1, 2, 3):
            sems = (st_send.at[n, k - 1], st_recv.at[n, k - 1])
            dst = stat_in.at[n, k - 1]
            to = me.sibling() if axis == "c" else me.along(axis, me.shifted(axis, k))
            copy = remote(stat.at[n], dst, *sems, to)
            copies.append((copy, copy))
        start_all(copies)
        arrive_all(copies)
        values = [stat[n]] + [stat_in[n, k] for k in range(len(copies))]
        for i, line in enumerate(merged(values)):
            stat[n + 1, i : i + 1, :] = line

    end = stat[4]
    t_whole = end[0:1] + jnp.log(end[1:2])
    s_whole = end[3:4] + jnp.log(end[4:5])
    divergence = end[2:3] / end[1:2] - t_whole + s_whole
    row_loss = jnp.where(end[6:7] > 0, divergence + BETA * (s_whole - end[5:6]), 0.0)
    sub = lax.broadcasted_iota(jnp.int32, (8, ROWS), 0)
    lines = jnp.zeros((8, ROWS), F32)
    for n, one in enumerate((t_whole, s_whole, row_loss)):
        lines = jnp.where(sub == n, jnp.broadcast_to(one, (8, ROWS)), lines)
    for i in range(3):
        tall = jnp.concatenate(
            [lines[:, i * 128 : (i + 1) * 128], jnp.zeros((120, LANES), F32)], axis=0
        )
        back[i * 128 : (i + 1) * 128, :] = tall.T
    for m, (c, y, z) in enumerate(PIECES):
        loss_blk[c, y, z] = jnp.broadcast_to(back[m * 16 : (m + 1) * 16, 2:3], (16, LANES))

    @pl.loop(0, ROWS // 32)
    def _(r):
        rows = pl.ds(pl.multiple_of(r * 32, 32), 32)
        t_prob = jnp.exp(t_log[rows, :] - back[rows, 0:1])
        s_prob = jnp.exp(s_log[rows, :] - back[rows, 1:2])
        hit = (columns() == lab_col[rows, 0:1]).astype(F32)
        scale = LOSS_SCALE * wgt_col[rows, 0:1]
        lg[rows, :] = (scale * ((1.0 + BETA) * s_prob - t_prob - BETA * hit)).astype(BF16)

    def quarter(k, core):
        q = me.shifted("x", k)
        return lax.dot_general(
            lg[pl.ds(pl.multiple_of(core * HALF, HALF), HALF), :],
            w_s[pl.ds(pl.multiple_of(q * QS, QS), QS), :],
            (((1,), (1,)), ((), ())),
            preferred_element_type=F32,
        )

    def first_reduce(k):
        q = me.shifted("x", k)
        copies = []
        for p, (lo, width, axis, then) in enumerate(PARTS_G):
            for n, (sent, heard) in enumerate(me.offsets(axis)):
                where = {a: pl.ds(sent[a], 1) if a in sent else slice(None) for a in "yz"}
                copy = remote(
                    g.at[me.c, where["y"], where["z"], q, :, pl.ds(lo, width)],
                    rr0[p].at[n, k - 1],
                    rs_send.at[p, n, k - 1],
                    rs_recv.at[p, n, k - 1],
                    me.to(**sent),
                )
                copies.append((copy, copy))
        if k < 4:
            for i, (y, z) in enumerate(LIVE):
                copy = remote(
                    g.at[me.c, y, z, q, :, pl.ds(LO_X, W_X)],
                    rr_x.at[k - 1, y, z],
                    rx_send.at[k - 1, i],
                    rx_recv.at[k - 1, i],
                    me.along("x", q),
                )
                copies.append((copy, copy))
        return copies

    core_copies, reduce_copies = [], []
    for k in range(1, 6):
        if k < 5:
            q = me.shifted("x", k)
            share = quarter(k, 1 - me.c).astype(BF16)
            g[1 - me.c, 0:2, :, q] = share[0:128].reshape(2, 4, 16, QS)
            g[1 - me.c, 2:4, 0:2, q] = share[128:192].reshape(2, 2, 16, QS)
            copies = []
            for i, (y, z) in enumerate(LIVE):
                copy = remote(
                    g.at[1 - me.c, y, z, q],
                    core_in.at[k - 1, y, z],
                    cs_send.at[k - 1, i],
                    cs_recv.at[k - 1, i],
                    me.sibling(),
                )
                copies.append((copy, copy))
            start_all(copies)
            core_copies.append(copies)
        if k > 1:
            q = me.shifted("x", k - 1)
            share = quarter(k - 1, me.c)
            arrive_all(core_copies[k - 2])
            other = core_in[k - 2, 0:2].reshape(128, QS).astype(F32)
            g[me.c, 0:2, :, q] = (share[0:128] + other).astype(BF16).reshape(2, 4, 16, QS)
            other = core_in[k - 2, 2:4, 0:2].reshape(64, QS).astype(F32)
            g[me.c, 2:4, 0:2, q] = (share[128:192] + other).astype(BF16).reshape(2, 2, 16, QS)
            copies = first_reduce(k - 1)
            start_all(copies)
            reduce_copies += copies

    arrive_all(reduce_copies)
    for p, (lo, width, axis, then) in enumerate(PARTS_G):
        cols = slice(lo, lo + width)
        for k in range(1, 5):
            q = me.shifted("x", k)

            @pl.loop(0, 4)
            def _(i, p=p, axis=axis, then=then, cols=cols, k=k, q=q):
                at = {axis: me.at(axis), then: i}
                slot = {axis: 0, then: i}
                whole = g[me.c, at["y"], at["z"], q, :, cols].astype(F32)
                for n in range(3):
                    whole = whole + rr0[p][n, k - 1, slot["y"], slot["z"]].astype(F32)
                g[me.c, at["y"], at["z"], q, :, cols] = whole.astype(BF16)

    cols_x = slice(LO_X, LO_X + W_X)
    for ys, zs in (((0, 1), 4), ((2, 3), 2)):
        for y in ys:

            @pl.loop(0, zs)
            def _(z, y=y):
                whole = g[me.c, y, z, me.x, :, cols_x].astype(F32)
                for n in range(3):
                    whole = whole + rr_x[n, y, z].astype(F32)
                g[me.c, y, z, me.x, :, cols_x] = whole.astype(BF16)

    second = []
    for p, (lo, width, axis, then) in enumerate(PARTS_G):
        for n, (sent, heard) in enumerate(me.offsets(then)):
            at = {axis: me.at(axis), **sent}
            copy = remote(
                g.at[me.c, at["y"], at["z"], :, :, pl.ds(lo, width)],
                rr1.at[p, n],
                r1_send.at[p, n],
                r1_recv.at[p, n],
                me.to(**sent),
            )
            second.append((copy, copy))
    for n, (sent, heard) in enumerate(me.offsets("yz")):
        copy = remote(
            g.at[me.c, sent["y"], sent["z"], me.x, :, pl.ds(LO_X, W_X)],
            rr2.at[n],
            r2_send.at[n],
            r2_recv.at[n],
            me.to(**sent),
        )
        second.append((copy, copy))
    start_all(second)
    arrive_all(second)
    for p, (lo, width, axis, then) in enumerate(PARTS_G):
        for q in range(4):
            whole = g[me.c, me.y, me.z, q, :, lo : lo + width].astype(F32)
            for n in range(3):
                whole = whole + rr1[p, n, q].astype(F32)
            for i in range(4):
                ng_out[i, :, q * W_YZ + lo : q * W_YZ + lo + width] = whole[4 * i : 4 * i + 4]
    whole = g[me.c, me.y, me.z, me.x, :, cols_x].astype(F32)
    for n in range(15):
        whole = whole + rr2[n].astype(F32)
    for i in range(4):
        ng_out[i, :, 4 * W_YZ : 4 * W_YZ + W_X] = whole[4 * i : 4 * i + 4]

    ng_in[me.x] = ng_out[me.x]
    for k in (1, 2, 3):
        x_copy(4, ng_out, ng_in, k).start()

    losses = loss_blk[me.c, me.y, me.z]
    mine = jnp.zeros((4, LANES), F32)
    for i in range(4):
        mine = jnp.where(me.x == i, losses[4 * i : 4 * i + 4], mine)
    diagonal = lax.broadcasted_iota(jnp.int32, (4, LANES), 0) == lax.broadcasted_iota(
        jnp.int32, (4, LANES), 1
    )
    loss_ref[...] = jnp.sum(jnp.where(diagonal, mine, 0.0), axis=0, keepdims=True)

    for k in (1, 2, 3):
        x_arrival(4, ng_out, ng_in, k).wait_recv()
    norm_parts = []
    for q in range(4):
        cols = slice(q * W_YZ, (q + 1) * W_YZ)
        norm_parts.append(ng_in[0, :, cols] + ng_in[1, :, cols] + ng_in[2, :, cols] + ng_in[3, :, cols])
        norm_parts.append(ng_in[q, :, 4 * W_YZ : 4 * W_YZ + W_X])
    norm_grad = jnp.concatenate(norm_parts, axis=1)
    live = me.y_hi * 4 + me.z < 6
    scaled = norm_grad * s_gain
    inner = jnp.mean(scaled * hidden, axis=1, keepdims=True)
    grad = inverse * scaled - hidden * (inverse * inverse * inverse) * inner
    grad_ref[...] = jnp.where(live, grad, 0.0)

    for k in (1, 2, 3):
        x_copy(0, stu_out, stu_in, k).wait_send()
        x_copy(4, ng_out, ng_in, k).wait_send()
    for n in range(3):
        tab_copy(n)[0].wait_send()
    for sent, unused in opened:
        sent.wait_send()


def scratch():
    dma = pltpu.SemaphoreType.DMA
    vm = pltpu.VMEM
    first = []
    for lo, width, axis, plane in PARTS_A:
        spots = [1 if a == axis else 2 if a == "h" else 4 for a in "hzx"]
        first.append(vm((1 if axis == "h" else 3, *spots, 16, width), BF16))
    rr0 = []
    for lo, width, axis, then in PARTS_G:
        spots = [1 if a == axis else 4 for a in "yz"]
        rr0.append(vm((3, 4, *spots, 16, width), BF16))
    return {
        "w_t": vm((D_T, VOC), BF16),
        "w_s": vm((D_S, VOC), BF16),
        "pb": vm((2, 4, 4, 16, QT), BF16),
        "first_in": tuple(first),
        "second_in": tuple(vm((n, 16, PARTS_A[0][1]), BF16) for n in (7, 7, 15)),
        "rows_in": vm((4, 16, QT), BF16),
        "tb": vm((2, 4, 4, 4, 16, QT), BF16),
        "sb": vm((2, 4, 4, 4, 16, QS), BF16),
        "res_in": vm((4, 4, D_T), BF16),
        "stu_out": vm((4, 4, QS), BF16),
        "stu_in": vm((4, 4, QS), BF16),
        "asm_t": vm((4, 16, QT), F32),
        "asm_s": vm((16, QS), F32),
        "normed": vm((4, 16, QT), BF16),
        "tab_own": vm((8, LANES), F32),
        "tab": vm((4, 8, LANES), F32),
        "lab_col": vm((ROWS, LANES), F32),
        "wgt_col": vm((ROWS, LANES), F32),
        "t_log": vm((ROWS, VOC), F32),
        "s_log": vm((ROWS, VOC), F32),
        "lg": vm((ROWS, VOC), BF16),
        "stat": vm((5, 8, ROWS), F32),
        "stat_in": vm((4, 3, 8, ROWS), F32),
        "back": vm((ROWS, LANES), F32),
        "loss_blk": vm((2, 4, 4, 16, LANES), F32),
        "g": vm((2, 4, 4, 4, 16, QS), BF16),
        "core_in": vm((4, 4, 4, 16, QS), BF16),
        "rr0": tuple(rr0),
        "rr_x": vm((3, 4, 4, 16, W_X), BF16),
        "rr1": vm((2, 3, 4, 16, PARTS_G[0][1]), BF16),
        "rr2": vm((15, 16, W_X), BF16),
        "ng_out": vm((4, 4, 4 * W_YZ + W_X), F32),
        "ng_in": vm((4, 4, 4 * W_YZ + W_X), F32),
        "sem_w": dma((2,)),
        "a_own": dma((4,)),
        "f_send": dma((3, 3)),
        "f_recv": dma((3, 3)),
        "h_send": dma((3, 15)),
        "h_recv": dma((3, 15)),
        "x_send": dma((5, 3)),
        "x_recv": dma((5, 3)),
        "tab_send": dma((3,)),
        "tab_recv": dma((3,)),
        "ag_send": dma((2, 3, 3, 15)),
        "ag_recv": dma((2, 3, 3, 15)),
        "sib_send": dma((3, 2)),
        "sib_recv": dma((3, 2)),
        "st_send": dma((4, 3)),
        "st_recv": dma((4, 3)),
        "cs_send": dma((4, 2)),
        "cs_recv": dma((4, 2)),
        "rs_send": dma((2, 3, 4)),
        "rs_recv": dma((2, 3, 4)),
        "rx_send": dma((3, 2)),
        "rx_recv": dma((3, 2)),
        "r1_send": dma((2, 3)),
        "r1_recv": dma((2, 3)),
        "r2_send": dma((15,)),
        "r2_recv": dma((15,)),
    }


def shards(
    teacher_partial,
    teacher_residual,
    post_gain,
    final_gain,
    teacher_head,
    student_hidden,
    student_gain,
    student_head,
    labels,
    lengths,
):
    whole = pl.BlockSpec(memory_space=pltpu.VMEM)
    place = pl.BlockSpec(memory_space=pl.ANY)
    spaces = scratch()
    names = list(spaces)
    leaves, tree = jax.tree.flatten([spaces[n] for n in names])

    def body(*refs):
        held = jax.tree.unflatten(tree, refs[12:])
        kernel(*refs[:12], **dict(zip(names, held)))

    grad, loss = pl.pallas_call(
        body,
        out_shape=(
            jax.ShapeDtypeStruct((4, D_S), F32),
            jax.ShapeDtypeStruct((1, LANES), F32),
        ),
        in_specs=[
            place,
            whole,
            whole,
            whole,
            place,
            whole,
            whole,
            place,
            whole,
            pl.BlockSpec(memory_space=pltpu.SMEM),
        ],
        out_specs=(whole, whole),
        scratch_shapes=leaves,
        compiler_params=pltpu.CompilerParams(
            collective_id=0, has_side_effects=True, vmem_limit_bytes=60 * 2**20
        ),
        name="distill",
    )(
        teacher_partial.reshape(2, 4, 16, D_T),
        teacher_residual,
        post_gain,
        final_gain,
        teacher_head,
        student_hidden,
        student_gain,
        student_head,
        labels.reshape(1, -1),
        lengths,
    )
    return grad, loss[0, :4]


def solution(mesh):
    torus = Mesh(mesh.devices.reshape(2, 2, 2, 4, 4), ("dp_0", "dp_1", "tp_0", "tp_1", "tp_2"))
    return jax.shard_map(
        shards,
        mesh=torus,
        in_specs=(
            P(TP, DP, None),
            P(DP_TP, None),
            P(),
            P(),
            P(None, DP_TP),
            P(DP_TP, None),
            P(),
            P(None, DP_TP),
            P(DP),
            P(DP, None),
        ),
        out_specs=(P(DP_TP, None), P(DP_TP)),
        check_vma=False,
    )
```

```python
import functools
import itertools
import types

import jax
import jax.numpy as jnp
from jax import lax
from jax.experimental import pallas as pl
from jax.experimental.pallas import tpu as pltpu
from jax.sharding import Mesh
from jax.sharding import PartitionSpec as P

TP = ("tp_0", "tp_1", "tp_2")
DP = ("dp_0", "dp_1")
DP_TP = ("dp_0", "dp_1", "tp_0", "tp_1", "tp_2")
MESH = pl.DeviceIdType.MESH

EPS = 1e-06
BETA = 0.5
LOSS_SCALE = 1024.0

F32 = jnp.float32
BF16 = jnp.bfloat16

D_T = 4608
D_S = 3584
QT = D_T // 4
QS = D_S // 4
VOC = 1024
ROWS = 384
HALF = 192
NSEQ = 8
LANES = 128

PARTS_A = ((0, 384, "x", "hz"), (384, 384, "z", "hx"), (768, 384, "h", "zx"))
PARTS_T = ((0, 384, "x", "y", "z"), (384, 384, "x", "z", "y"), (768, 384, "", "yz", "x"))
PARTS_S = ((0, 256, "xyz"), (256, 384, "yzx"), (640, 256, "zxy"))
PARTS_G = ((0, 256, "z", "y"), (256, 256, "y", "z"))
LO_X, W_X = (512, 384)
W_YZ = 512
GROUPS = 40


def live_pieces():
    held = []
    for c in range(2):
        held += [(c, y, z) for y in range(2) for z in range(4)]
        held += [(c, y, z) for y in range(2, 4) for z in range(2)]
    return held


PIECES = live_pieces()
LIVE = ((pl.ds(0, 2), pl.ds(0, 4)), (pl.ds(2, 2), pl.ds(0, 2)))


class Place:
    def __init__(self):
        self.c = lax.axis_index("dp_1")
        self.z = lax.axis_index("tp_1")
        self.x = lax.axis_index("tp_2")
        self.y_lo = lax.axis_index("dp_0")
        self.y_hi = lax.axis_index("tp_0")
        self.y = self.y_hi * 2 + self.y_lo

    def at(self, axis):
        return {"x": self.x, "y": self.y, "z": self.z, "h": self.y_hi}[axis]

    def shifted(self, axis, k):
        return lax.rem(self.at(axis) + k, 2 if axis == "h" else 4)

    def to(self, **spots):
        y_lo, y_hi = self.y_lo, self.y_hi
        if "y" in spots:
            y_lo, y_hi = lax.rem(spots["y"], 2), lax.div(spots["y"], 2)
        y_hi = spots.get("h", y_hi)
        return (y_lo, self.c, y_hi, spots.get("z", self.z), spots.get("x", self.x))

    def along(self, axis, to):
        return self.to(**{axis: to})

    def offsets(self, axes):
        sizes = [2 if a == "h" else 4 for a in axes]
        for ks in itertools.product(*[range(n) for n in sizes]):
            if any(ks):
                sent = {a: self.shifted(a, k) for a, k in zip(axes, ks)}
                heard = {a: self.shifted(a, n - k) for a, k, n in zip(axes, ks, sizes)}
                yield (sent, heard)

    def sibling(self):
        return (self.y_lo, 1 - self.c, self.y_hi, self.z, self.x)


def remote(src, dst, send, recv, to):
    return pltpu.make_async_remote_copy(
        src_ref=src, dst_ref=dst, send_sem=send, recv_sem=recv, device_id=to, device_id_type=MESH
    )


def kernel(
    partial_ref,
    residual_hbm,
    post_hbm,
    final_hbm,
    t_head_ref,
    hidden_hbm,
    s_gain_hbm,
    s_head_ref,
    labels_hbm,
    lengths_hbm,
    grad_hbm,
    loss_hbm,
    residual_ref,
    post_ref,
    final_ref,
    hidden_ref,
    s_gain_ref,
    labels_ref,
    lengths_ref,
    grad_ref,
    loss_ref,
    in_sem,
    out_sem,
    w_t,
    w_s,
    pb,
    first_in,
    second_in,
    rows_in,
    tb,
    sb,
    res_in,
    stu_out,
    stu_in,
    asm_t,
    asm_s,
    normed,
    tab_own,
    tab,
    lab_col,
    wgt_col,
    t_log,
    s_log,
    lg,
    stat,
    stat_in,
    back,
    loss_blk,
    g,
    share,
    core_in,
    rr0,
    rr_x,
    rr1,
    rr2,
    ng_out,
    ng_in,
    sem_w,
    a_own,
    pool,
):
    me = Place()
    tp = me.y_hi * 16 + me.z * 4 + me.x
    dp = me.y_lo * 2 + me.c
    position = dp * 32 + tp

    load_s = pltpu.make_async_copy(s_head_ref, w_s, sem_w.at[0])
    load_t = pltpu.make_async_copy(t_head_ref, w_t, sem_w.at[1])
    small_copies = []
    for n, (src, dst) in enumerate(
        (
            (hidden_hbm, hidden_ref),
            (s_gain_hbm, s_gain_ref),
            (residual_hbm, residual_ref),
            (labels_hbm, labels_ref),
            (lengths_hbm, lengths_ref),
            (post_hbm, post_ref),
            (final_hbm, final_ref),
        )
    ):
        copy = pltpu.make_async_copy(src, dst, in_sem.at[n])
        copy.start()
        small_copies.append(copy)
    own_copies = []
    for q in range(4):
        copy = pltpu.make_async_copy(
            partial_ref.at[:, :, :, pl.ds(q * QT, QT)], pb.at[:, :, q], a_own.at[q]
        )
        copy.start()
        own_copies.append(copy)

    barrier = pltpu.get_barrier_semaphore()
    near = [me.to(**sent) for sent, heard in me.offsets("yz")]
    near += [me.along("x", me.shifted("x", k)) for k in (1, 2, 3)]
    for k in (1, 2, 3):
        near += [me.to(x=me.shifted("x", k), z=me.shifted("z", n)) for n in (1, 2, 3)]
        near += [me.to(x=me.shifted("x", k), h=1 - me.y_hi)]
    near += [me.sibling(), (1 - me.y_lo, 1 - me.c, me.y_hi, me.z, me.x)]
    for to in near:
        pl.semaphore_signal(barrier, inc=1, device_id=to, device_id_type=MESH)
    pl.semaphore_wait(barrier, len(near))

    opened = []

    def group(whole):
        n = len(opened)
        made = types.SimpleNamespace(
            whole=whole, send=pool.at[2 * n], recv=pool.at[2 * n + 1], copies=[], started=0
        )
        opened.append(made)
        return made

    def put(made, src, dst, to):
        made.to = to
        made.copies.append(remote(src, dst, made.send, made.recv, to))

    def start_all(groups):
        for made in groups:
            for copy in made.copies[made.started :]:
                copy.start()
            made.started = len(made.copies)

    def both_ends(made):
        return remote(made.whole, made.whole, made.send, made.recv, made.to)

    def arrive_all(groups):
        for made in groups:
            both_ends(made).wait_recv()

    for copy in own_copies:
        copy.wait()

    def pb_box(spots, lo, width):
        where = [pl.ds(spots[a], 1) if a in spots else slice(None) for a in "hzx"]
        return pb.at[where[0], where[1], where[2], :, pl.ds(lo, width)]

    first_stage, second_stage = [], []
    for p, (lo, width, axis, plane) in enumerate(PARTS_A):
        first = group(first_in[p])
        for n, (sent, heard) in enumerate(me.offsets(axis)):
            put(first, pb_box(sent, lo, width), first_in[p].at[n], me.to(**sent))
        second = group(second_in[p])
        for n, (sent, heard) in enumerate(me.offsets(plane)):
            spots = {axis: me.at(axis), **sent}
            src = pb.at[spots["h"], spots["z"], spots["x"], :, pl.ds(lo, width)]
            put(second, src, second_in[p].at[n], me.to(**sent))
        first_stage.append(first)
        second_stage.append(second)

    start_all(first_stage)
    load_t.start()
    load_s.start()

    for copy in small_copies:
        copy.wait()

    hidden = hidden_ref[...].astype(F32)
    s_gain = s_gain_ref[...].reshape(1, D_S)
    inverse = lax.rsqrt(jnp.mean(hidden * hidden, axis=-1, keepdims=True) + EPS)
    student = (hidden * inverse * s_gain).astype(BF16)
    for q in range(4):
        stu_out[q] = student[:, q * QS : (q + 1) * QS]
    stu_in[me.x] = stu_out[me.x]
    res_in[me.x] = residual_ref[...]

    def along_x(whole, src, dst):
        made = group(whole)
        for sent, heard in me.offsets("x"):
            put(made, src(sent["x"]), dst, me.to(**sent))
        return [made]

    student_copies = along_x(stu_in.at[pl.ds(0, 3)], lambda to: stu_out.at[to], stu_in.at[me.x])
    start_all(student_copies)
    residual_copies = along_x(res_in.at[pl.ds(0, 3)], lambda to: residual_ref, res_in.at[me.x])
    start_all(residual_copies)

    lane = lax.broadcasted_iota(jnp.int32, (1, LANES), 1)
    start = jnp.int32(0)
    weight = jnp.zeros((1, LANES), F32)
    for i in range(NSEQ):
        length = lengths_ref[0, i]
        end = start + length
        inside = (lane >= start) & (lane < end)
        one_over = 1.0 / jnp.full((1, LANES), length, jnp.int32).astype(F32)
        weight = jnp.where(inside, one_over, weight)
        start = end
    sub = lax.broadcasted_iota(jnp.int32, (8, LANES), 0)
    label_row = labels_ref[...].astype(F32)
    tab_own[...] = jnp.where(
        sub == 0,
        jnp.broadcast_to(label_row, (8, LANES)),
        jnp.where(sub == 1, jnp.broadcast_to(weight, (8, LANES)), 0.0),
    )
    tab[dp] = tab_own[...]
    tables = group(tab.at[pl.ds(0, 3)])
    for y_lo, c in ((me.y_lo, 1 - me.c), (1 - me.y_lo, me.c), (1 - me.y_lo, 1 - me.c)):
        put(tables, tab_own, tab.at[dp], (y_lo, c, me.y_hi, me.z, me.x))
    start_all([tables])

    def box(buf, spots, done, lo, width):
        where = []
        for a in "yzx":
            where.append(pl.ds(0, 4) if a in done else pl.ds(spots.get(a, me.at(a)), 1))
        return buf.at[me.c, where[0], where[1], where[2], :, pl.ds(lo, width)]

    def one_part(buf, lo, width, axes, done, whole=None):
        cols = pl.ds(lo, width)
        three = [pl.ds(0, 4) if a in done else pl.ds(me.at(a), 1) for a in "yzx"]
        three["yzx".index(axes[0])] = pl.ds(0, 3)
        live = LIVE if "y" in done and "z" in done else ()
        if live:
            three = [pl.ds(0, 4), pl.ds(0, 3), pl.ds(0, 3)]
        made = group(buf.at[me.c, three[0], three[1], three[2], :, cols] if whole is None else whole)
        own = [buf.at[me.c, y, z, pl.ds(me.x, 1), :, cols] for y, z in live]
        for sent, heard in me.offsets(axes):
            for src in own or [box(buf, {}, done, lo, width)]:
                put(made, src, src, me.to(**sent))
        return made

    def swap(buf):
        made = group(buf.at[0, pl.ds(0, 3)])
        for y, z in LIVE:
            own = buf.at[me.c, y, z]
            put(made, own, own, me.sibling())
        return [made]

    student_stages, teacher_stages = [[], [], []], [[], []]
    for stage in range(3):
        for lo, width, order in PARTS_S:
            made = one_part(sb, lo, width, order[stage], order[:stage])
            student_stages[stage].append(made)
    for lo, width, done, first, second in PARTS_T:
        whole = second_in[2] if len(first) == 2 else None
        teacher_stages[0].append(one_part(tb, lo, width, first, done, whole))
        teacher_stages[1].append(one_part(tb, lo, width, second, done + first))
    student_swap, teacher_swap = swap(sb), swap(tb)

    arrive_all(first_stage)
    for p, (lo, width, axis, plane) in enumerate(PARTS_A):
        came = first_in[p]
        count = came.shape[0]

        @pl.loop(0, came.shape[1] * came.shape[2] * came.shape[3])
        def _(n, lo=lo, width=width, axis=axis, plane=plane, came=came, count=count):
            at, slot = {axis: me.at(axis)}, {axis: 0}
            for a in reversed(plane):
                size = 2 if a == "h" else 4
                at[a] = slot[a] = lax.rem(n, size)
                n = lax.div(n, size)
            cols = slice(lo, lo + width)
            whole = pb[at["h"], at["z"], at["x"], :, cols].astype(F32)
            for i in range(count):
                whole = whole + came[i, slot["h"], slot["z"], slot["x"]].astype(F32)
            pb[at["h"], at["z"], at["x"], :, cols] = whole.astype(BF16)

    start_all(second_stage)
    arrive_all(student_copies)
    for i in range(4):
        asm_s[4 * i : 4 * i + 4, :] = stu_in[i].astype(F32)
    sb[me.c, me.y, me.z, me.x] = asm_s[...].astype(BF16)
    start_all(student_stages[0])

    arrive_all(residual_copies)
    for q in range(4):
        for i in range(4):
            asm_t[q, 4 * i : 4 * i + 4, :] = res_in[i, :, q * QT : (q + 1) * QT].astype(F32)
    arrive_all(second_stage)
    for p, (lo, width, axis, plane) in enumerate(PARTS_A):
        whole = pb[me.y_hi, me.z, me.x, :, lo : lo + width].astype(F32)
        for n in range(second_in[p].shape[0]):
            whole = whole + second_in[p][n].astype(F32)
        rows_in[me.x, :, lo : lo + width] = whole.astype(BF16)

    row_copies = along_x(rows_in.at[pl.ds(0, 3)], lambda to: rows_in.at[me.x], rows_in.at[me.x])
    start_all(row_copies)
    arrive_all(student_stages[0])
    start_all(student_stages[1])
    arrive_all(row_copies)

    def row_inverse(quarters):
        total = sum(jnp.sum(v * v, axis=1, keepdims=True) for v in quarters)
        return lax.rsqrt(total / D_T + EPS)

    sums = [rows_in[q].astype(F32) for q in range(4)]
    scale = row_inverse(sums)
    for q in range(4):
        cols = slice(q * QT, (q + 1) * QT)
        asm_t[q] = asm_t[q] + sums[q] * scale * post_ref[cols].reshape(1, QT)
    scale = row_inverse([asm_t[q] for q in range(4)])
    for q in range(4):
        cols = slice(q * QT, (q + 1) * QT)
        normed[q] = (asm_t[q] * scale * final_ref[cols].reshape(1, QT)).astype(BF16)
    for lo, width, done, first, second in PARTS_T:
        cols = slice(lo, lo + width)
        if done:
            for q in range(4):
                tb[me.c, me.y, me.z, q, :, cols] = normed[q, :, cols]
        else:
            tb[me.c, me.y, me.z, me.x, :, cols] = normed[me.x, :, cols]
    start_all(teacher_stages[0])

    arrive_all([tables])
    for part in range(4):
        table = tab[part]
        for row, col in ((0, lab_col), (1, wgt_col)):
            turned = jnp.broadcast_to(table[row : row + 1, :], (LANES, LANES)).T
            for m, (c, y, z) in enumerate(PIECES):
                if (y % 2) * 2 + c == part:
                    j = (y // 2) * 4 + z
                    col[m * 16 : (m + 1) * 16, :] = turned[j * 16 : (j + 1) * 16, :]
    g[:, 2:4, 2:4] = jnp.zeros((2, 2, 2, 4, 16, QS), BF16)
    loss_blk[:, 2:4, 2:4] = jnp.zeros((2, 2, 2, 16, LANES), F32)

    arrive_all(student_stages[1])
    arrive_all(teacher_stages[0])
    start_all(teacher_stages[1])
    start_all(student_stages[2])

    def logits(buf, head, out, width, core):
        rows = pl.ds(pl.multiple_of(core * HALF, HALF), HALF)

        @pl.loop(0, VOC // 256)
        def _(n):
            cols = pl.ds(pl.multiple_of(n * 256, 256), 256)
            acc = None
            for q in range(4):
                live = jnp.concatenate(
                    [
                        buf[core, 0:2, :, q].reshape(128, width),
                        buf[core, 2:4, 0:2, q].reshape(64, width),
                    ],
                    axis=0,
                )
                head_rows = head[q * width : (q + 1) * width, cols]
                term = jnp.dot(live, head_rows, preferred_element_type=F32)
                acc = term if acc is None else acc + term
            out[rows, cols] = acc

    load_t.wait()
    arrive_all(teacher_stages[1])
    start_all(teacher_swap)
    logits(tb, w_t, t_log, QT, me.c)
    arrive_all(student_stages[2])
    start_all(student_swap)
    arrive_all(teacher_swap)
    logits(tb, w_t, t_log, QT, 1 - me.c)
    load_s.wait()
    logits(sb, w_s, s_log, QS, me.c)
    arrive_all(student_swap)
    logits(sb, w_s, s_log, QS, 1 - me.c)

    first_col = (position * VOC).astype(F32)

    def columns():
        return lax.broadcasted_iota(jnp.int32, (32, VOC), 1).astype(F32) + first_col

    lanes = lax.broadcasted_iota(jnp.int32, (32, LANES), 1)

    @pl.loop(0, ROWS // 32)
    def _(r):
        rows = pl.ds(pl.multiple_of(r * 32, 32), 32)
        t, s = t_log[rows, :], s_log[rows, :]
        t_max = jnp.max(t, axis=1, keepdims=True)
        s_max = jnp.max(s, axis=1, keepdims=True)
        t_exp = jnp.exp(t - t_max)
        t_sum = jnp.sum(t_exp, axis=1, keepdims=True)
        cross = jnp.sum(t_exp * (t - s), axis=1, keepdims=True)
        s_sum = jnp.sum(jnp.exp(s - s_max), axis=1, keepdims=True)
        hit = columns() == lab_col[rows, 0:1]
        value = jnp.sum(jnp.where(hit, s, 0.0), axis=1, keepdims=True)
        held = wgt_col[rows, :]
        for n, one in enumerate((t_max, t_sum, cross, s_max, s_sum, value)):
            held = jnp.where(lanes == n, one, held)
        back[rows, :] = held

    for i in range(3):
        turned = back[i * 128 : (i + 1) * 128, :].T
        stat[0, :, i * 128 : (i + 1) * 128] = turned[0:8, :]

    def merged(values):
        t_max = functools.reduce(jnp.maximum, [v[0:1] for v in values])
        s_max = functools.reduce(jnp.maximum, [v[3:4] for v in values])
        t_sum = cross = s_sum = label = 0.0
        for v in values:
            t_one = jnp.exp(v[0:1] - t_max)
            s_one = jnp.exp(v[3:4] - s_max)
            t_sum += v[1:2] * t_one
            cross += v[2:3] * t_one
            s_sum += v[4:5] * s_one
            label += v[5:6]
        return [t_max, t_sum, cross, s_max, s_sum, label, values[0][6:7]]

    for n, axes in enumerate(("c", "xz", "y")):
        if axes == "c":
            peers = [me.sibling()]
        else:
            peers = [me.to(**sent) for sent, heard in me.offsets(axes)]
        made = group(stat_in.at[n, pl.ds(0, len(peers))])
        for k, to in enumerate(peers):
            put(made, stat.at[n], stat_in.at[n, k], to)
        start_all([made])
        arrive_all([made])
        values = [stat[n]] + [stat_in[n, k] for k in range(len(peers))]
        for i, line in enumerate(merged(values)):
            stat[n + 1, i : i + 1, :] = line

    end = stat[3]
    t_whole = end[0:1] + jnp.log(end[1:2])
    s_whole = end[3:4] + jnp.log(end[4:5])
    divergence = end[2:3] / end[1:2] - t_whole + s_whole
    row_loss = jnp.where(end[6:7] > 0, divergence + BETA * (s_whole - end[5:6]), 0.0)
    sub = lax.broadcasted_iota(jnp.int32, (8, ROWS), 0)
    lines = jnp.zeros((8, ROWS), F32)
    for n, one in enumerate((t_whole, s_whole, row_loss)):
        lines = jnp.where(sub == n, jnp.broadcast_to(one, (8, ROWS)), lines)
    for i in range(3):
        tall = jnp.concatenate(
            [lines[:, i * 128 : (i + 1) * 128], jnp.zeros((120, LANES), F32)], axis=0
        )
        back[i * 128 : (i + 1) * 128, :] = tall.T
    for m, (c, y, z) in enumerate(PIECES):
        loss_blk[c, y, z] = jnp.broadcast_to(back[m * 16 : (m + 1) * 16, 2:3], (16, LANES))

    @pl.loop(0, ROWS // 32)
    def _(r):
        rows = pl.ds(pl.multiple_of(r * 32, 32), 32)
        t_prob = jnp.exp(t_log[rows, :] - back[rows, 0:1])
        s_prob = jnp.exp(s_log[rows, :] - back[rows, 1:2])
        hit = (columns() == lab_col[rows, 0:1]).astype(F32)
        scale = LOSS_SCALE * wgt_col[rows, 0:1]
        lg[rows, :] = (scale * ((1.0 + BETA) * s_prob - t_prob - BETA * hit)).astype(BF16)

    def quarter(k):
        q = me.shifted("x", k)
        share[k % 2] = lax.dot_general(
            lg[...],
            w_s[pl.ds(pl.multiple_of(q * QS, QS), QS), :],
            (((1,), (1,)), ((), ())),
            preferred_element_type=F32,
        )

    def core_rows(k, core, at, count):
        return share[k % 2, pl.ds(pl.multiple_of(core * HALF + at, 64), count), :]

    reduce_copies = [group(rr0[0]), group(rr0[1]), group(rr_x.at[:, pl.ds(0, 3)])]

    def first_reduce(k):
        q = me.shifted("x", k)
        for p, (lo, width, axis, then) in enumerate(PARTS_G):
            for n, (sent, heard) in enumerate(me.offsets(axis)):
                where = {a: pl.ds(sent[a], 1) if a in sent else slice(None) for a in "yz"}
                src = g.at[me.c, where["y"], where["z"], q, :, pl.ds(lo, width)]
                put(reduce_copies[p], src, rr0[p].at[n, k - 1], me.to(**sent))
        if k < 4:
            for y, z in LIVE:
                src = g.at[me.c, y, z, q, :, pl.ds(LO_X, W_X)]
                put(reduce_copies[2], src, rr_x.at[k - 1, y, z], me.along("x", q))

    core_copies = []
    for k in range(1, 6):
        if k < 5:
            q = me.shifted("x", k)
            quarter(k)
            theirs = 1 - me.c
            g[theirs, 0:2, :, q] = core_rows(k, theirs, 0, 128).astype(BF16).reshape(2, 4, 16, QS)
            g[theirs, 2:4, 0:2, q] = core_rows(k, theirs, 128, 64).astype(BF16).reshape(2, 2, 16, QS)
            made = group(core_in.at[k - 1, pl.ds(0, 3)])
            for y, z in LIVE:
                put(made, g.at[theirs, y, z, q], core_in.at[k - 1, y, z], me.sibling())
            start_all([made])
            core_copies.append(made)
        if k > 1:
            q = me.shifted("x", k - 1)
            arrive_all([core_copies[k - 2]])
            other = core_in[k - 2, 0:2].reshape(128, QS).astype(F32)
            g[me.c, 0:2, :, q] = (core_rows(k - 1, me.c, 0, 128) + other).astype(BF16).reshape(2, 4, 16, QS)
            other = core_in[k - 2, 2:4, 0:2].reshape(64, QS).astype(F32)
            g[me.c, 2:4, 0:2, q] = (core_rows(k - 1, me.c, 128, 64) + other).astype(BF16).reshape(2, 2, 16, QS)
            first_reduce(k - 1)
            start_all(reduce_copies)

    arrive_all(reduce_copies)
    for p, (lo, width, axis, then) in enumerate(PARTS_G):
        cols = slice(lo, lo + width)
        for k in range(1, 5):
            q = me.shifted("x", k)

            @pl.loop(0, 4)
            def _(i, p=p, axis=axis, then=then, cols=cols, k=k, q=q):
                at = {axis: me.at(axis), then: i}
                slot = {axis: 0, then: i}
                whole = g[me.c, at["y"], at["z"], q, :, cols].astype(F32)
                for n in range(3):
                    whole = whole + rr0[p][n, k - 1, slot["y"], slot["z"]].astype(F32)
                g[me.c, at["y"], at["z"], q, :, cols] = whole.astype(BF16)

    cols_x = slice(LO_X, LO_X + W_X)
    for ys, zs in (((0, 1), 4), ((2, 3), 2)):
        for y in ys:

            @pl.loop(0, zs)
            def _(z, y=y):
                whole = g[me.c, y, z, me.x, :, cols_x].astype(F32)
                for n in range(3):
                    whole = whole + rr_x[n, y, z].astype(F32)
                g[me.c, y, z, me.x, :, cols_x] = whole.astype(BF16)

    second = [group(rr1), group(rr2)]
    for p, (lo, width, axis, then) in enumerate(PARTS_G):
        for n, (sent, heard) in enumerate(me.offsets(then)):
            at = {axis: me.at(axis), **sent}
            src = g.at[me.c, at["y"], at["z"], :, :, pl.ds(lo, width)]
            put(second[0], src, rr1.at[p, n], me.to(**sent))
    for n, (sent, heard) in enumerate(me.offsets("yz")):
        src = g.at[me.c, sent["y"], sent["z"], me.x, :, pl.ds(LO_X, W_X)]
        put(second[1], src, rr2.at[n], me.to(**sent))
    start_all(second)
    arrive_all(second)
    for p, (lo, width, axis, then) in enumerate(PARTS_G):
        for q in range(4):
            whole = g[me.c, me.y, me.z, q, :, lo : lo + width].astype(F32)
            for n in range(3):
                whole = whole + rr1[p, n, q].astype(F32)
            for i in range(4):
                ng_out[i, :, q * W_YZ + lo : q * W_YZ + lo + width] = whole[4 * i : 4 * i + 4]
    whole = g[me.c, me.y, me.z, me.x, :, cols_x].astype(F32)
    for n in range(15):
        whole = whole + rr2[n].astype(F32)
    for i in range(4):
        ng_out[i, :, 4 * W_YZ : 4 * W_YZ + W_X] = whole[4 * i : 4 * i + 4]

    ng_in[me.x] = ng_out[me.x]
    last = along_x(ng_in.at[pl.ds(0, 3)], lambda to: ng_out.at[to], ng_in.at[me.x])
    start_all(last)

    losses = loss_blk[me.c, me.y, me.z]
    mine = jnp.zeros((4, LANES), F32)
    for i in range(4):
        mine = jnp.where(me.x == i, losses[4 * i : 4 * i + 4], mine)
    diagonal = lax.broadcasted_iota(jnp.int32, (4, LANES), 0) == lax.broadcasted_iota(
        jnp.int32, (4, LANES), 1
    )
    loss_ref[...] = jnp.sum(jnp.where(diagonal, mine, 0.0), axis=0, keepdims=True)

    arrive_all(last)
    norm_parts = []
    for q in range(4):
        cols = slice(q * W_YZ, (q + 1) * W_YZ)
        norm_parts.append(ng_in[0, :, cols] + ng_in[1, :, cols] + ng_in[2, :, cols] + ng_in[3, :, cols])
        norm_parts.append(ng_in[q, :, 4 * W_YZ : 4 * W_YZ + W_X])
    norm_grad = jnp.concatenate(norm_parts, axis=1)
    live = me.y_hi * 4 + me.z < 6
    scaled = norm_grad * s_gain
    inner = jnp.mean(scaled * hidden, axis=1, keepdims=True)
    grad = inverse * scaled - hidden * (inverse * inverse * inverse) * inner
    grad_ref[...] = jnp.where(live, grad, 0.0)

    out_copies = (
        pltpu.make_async_copy(grad_ref, grad_hbm, out_sem.at[0]),
        pltpu.make_async_copy(loss_ref, loss_hbm, out_sem.at[1]),
    )
    for copy in out_copies:
        copy.start()

    for made in opened:
        both_ends(made).wait_send()
    assert len(opened) == GROUPS
    for copy in out_copies:
        copy.wait()


def scratch():
    dma = pltpu.SemaphoreType.DMA
    vm = pltpu.VMEM
    first = []
    for lo, width, axis, plane in PARTS_A:
        spots = [1 if a == axis else 2 if a == "h" else 4 for a in "hzx"]
        first.append(vm((1 if axis == "h" else 3, *spots, 16, width), BF16))
    rr0 = []
    for lo, width, axis, then in PARTS_G:
        spots = [1 if a == axis else 4 for a in "yz"]
        rr0.append(vm((3, 4, *spots, 16, width), BF16))
    return {
        "residual_ref": vm((4, D_T), BF16),
        "post_ref": vm((D_T,), F32),
        "final_ref": vm((D_T,), F32),
        "hidden_ref": vm((4, D_S), BF16),
        "s_gain_ref": vm((D_S,), F32),
        "labels_ref": vm((1, LANES), jnp.int32),
        "lengths_ref": pltpu.SMEM((1, NSEQ), jnp.int32),
        "grad_ref": vm((4, D_S), F32),
        "loss_ref": vm((1, LANES), F32),
        "in_sem": dma((7,)),
        "out_sem": dma((2,)),
        "w_t": vm((D_T, VOC), BF16),
        "w_s": vm((D_S, VOC), BF16),
        "pb": vm((2, 4, 4, 16, QT), BF16),
        "first_in": tuple(first),
        "second_in": tuple(vm((n, 16, PARTS_A[0][1]), BF16) for n in (7, 7, 15)),
        "rows_in": vm((4, 16, QT), BF16),
        "tb": vm((2, 4, 4, 4, 16, QT), BF16),
        "sb": vm((2, 4, 4, 4, 16, QS), BF16),
        "res_in": vm((4, 4, D_T), BF16),
        "stu_out": vm((4, 4, QS), BF16),
        "stu_in": vm((4, 4, QS), BF16),
        "asm_t": vm((4, 16, QT), F32),
        "asm_s": vm((16, QS), F32),
        "normed": vm((4, 16, QT), BF16),
        "tab_own": vm((8, LANES), F32),
        "tab": vm((4, 8, LANES), F32),
        "lab_col": vm((ROWS, LANES), F32),
        "wgt_col": vm((ROWS, LANES), F32),
        "t_log": vm((ROWS, VOC), F32),
        "s_log": vm((ROWS, VOC), F32),
        "lg": vm((ROWS, VOC), BF16),
        "stat": vm((4, 8, ROWS), F32),
        "stat_in": vm((3, 15, 8, ROWS), F32),
        "back": vm((ROWS, LANES), F32),
        "loss_blk": vm((2, 4, 4, 16, LANES), F32),
        "g": vm((2, 4, 4, 4, 16, QS), BF16),
        "share": vm((2, ROWS, QS), F32),
        "core_in": vm((4, 4, 4, 16, QS), BF16),
        "rr0": tuple(rr0),
        "rr_x": vm((3, 4, 4, 16, W_X), BF16),
        "rr1": vm((2, 3, 4, 16, PARTS_G[0][1]), BF16),
        "rr2": vm((15, 16, W_X), BF16),
        "ng_out": vm((4, 4, 4 * W_YZ + W_X), F32),
        "ng_in": vm((4, 4, 4 * W_YZ + W_X), F32),
        "sem_w": dma((2,)),
        "a_own": dma((4,)),
        "pool": dma((2 * GROUPS,)),
    }


def shards(
    teacher_partial,
    teacher_residual,
    post_gain,
    final_gain,
    teacher_head,
    student_hidden,
    student_gain,
    student_head,
    labels,
    lengths,
):
    place = pl.BlockSpec(memory_space=pl.ANY)
    spaces = scratch()
    names = list(spaces)
    leaves, tree = jax.tree.flatten([spaces[n] for n in names])

    def body(*refs):
        held = jax.tree.unflatten(tree, refs[12:])
        kernel(*refs[:12], **dict(zip(names, held)))

    grad, loss = pl.pallas_call(
        body,
        out_shape=(
            jax.ShapeDtypeStruct((4, D_S), F32),
            jax.ShapeDtypeStruct((1, LANES), F32),
        ),
        in_specs=[place] * 10,
        out_specs=(place, place),
        scratch_shapes=leaves,
        compiler_params=pltpu.CompilerParams(
            collective_id=0, has_side_effects=True, vmem_limit_bytes=60 * 2**20
        ),
        name="distill",
    )(
        teacher_partial.reshape(2, 4, 16, D_T),
        teacher_residual,
        post_gain,
        final_gain,
        teacher_head,
        student_hidden,
        student_gain,
        student_head,
        labels.reshape(1, -1),
        lengths,
    )
    return grad, loss[0, :4]


def solution(mesh):
    torus = Mesh(mesh.devices.reshape(2, 2, 2, 4, 4), ("dp_0", "dp_1", "tp_0", "tp_1", "tp_2"))
    return jax.shard_map(
        shards,
        mesh=torus,
        in_specs=(
            P(TP, DP, None),
            P(DP_TP, None),
            P(),
            P(),
            P(None, DP_TP),
            P(DP_TP, None),
            P(),
            P(None, DP_TP),
            P(DP),
            P(DP, None),
        ),
        out_specs=(P(DP_TP, None), P(DP_TP)),
        check_vma=False,
    )
```

```python
import functools
import itertools
import types

import jax
import jax.numpy as jnp
from jax import lax
from jax.experimental import pallas as pl
from jax.experimental.pallas import tpu as pltpu
from jax.sharding import Mesh
from jax.sharding import PartitionSpec as P

TP = ("tp_0", "tp_1", "tp_2")
DP = ("dp_0", "dp_1")
DP_TP = ("dp_0", "dp_1", "tp_0", "tp_1", "tp_2")
MESH = pl.DeviceIdType.MESH

EPS = 1e-06
BETA = 0.5
LOSS_SCALE = 1024.0

F32 = jnp.float32
BF16 = jnp.bfloat16

D_T = 4608
D_S = 3584
QT = D_T // 4
QS = D_S // 4
VOC = 1024
ROWS = 384
HALF = 192
NSEQ = 8
LANES = 128

PARTS_A = ((0, 384, "x", "hz"), (384, 384, "z", "hx"), (768, 384, "h", "zx"))
PARTS_T = ((0, 384, "x", "y", "z"), (384, 384, "x", "z", "y"), (768, 384, "", "yz", "x"))
PARTS_S = ((0, 256, "xyz"), (256, 384, "yzx"), (640, 256, "zxy"))
PARTS_G = ((0, 256, "z", "y"), (256, 256, "y", "z"))
LO_X, W_X = (512, 384)
W_YZ = 512
GROUPS = 42


def live_pieces():
    held = []
    for c in range(2):
        held += [(c, y, z) for y in range(2) for z in range(4)]
        held += [(c, y, z) for y in range(2, 4) for z in range(2)]
    return held


PIECES = live_pieces()
LIVE = ((pl.ds(0, 2), pl.ds(0, 4)), (pl.ds(2, 2), pl.ds(0, 2)))


class Place:
    def __init__(self):
        self.c = lax.axis_index("dp_1")
        self.z = lax.axis_index("tp_1")
        self.x = lax.axis_index("tp_2")
        self.y_lo = lax.axis_index("dp_0")
        self.y_hi = lax.axis_index("tp_0")
        self.y = self.y_hi * 2 + self.y_lo

    def at(self, axis):
        return {"x": self.x, "y": self.y, "z": self.z, "h": self.y_hi}[axis]

    def shifted(self, axis, k):
        return lax.rem(self.at(axis) + k, 2 if axis == "h" else 4)

    def to(self, **spots):
        y_lo, y_hi = self.y_lo, self.y_hi
        if "y" in spots:
            y_lo, y_hi = lax.rem(spots["y"], 2), lax.div(spots["y"], 2)
        y_hi = spots.get("h", y_hi)
        return (y_lo, self.c, y_hi, spots.get("z", self.z), spots.get("x", self.x))

    def along(self, axis, to):
        return self.to(**{axis: to})

    def offsets(self, axes):
        sizes = [2 if a == "h" else 4 for a in axes]
        for ks in itertools.product(*[range(n) for n in sizes]):
            if any(ks):
                sent = {a: self.shifted(a, k) for a, k in zip(axes, ks)}
                heard = {a: self.shifted(a, n - k) for a, k, n in zip(axes, ks, sizes)}
                yield (sent, heard)

    def sibling(self):
        return (self.y_lo, 1 - self.c, self.y_hi, self.z, self.x)


def remote(src, dst, send, recv, to):
    return pltpu.make_async_remote_copy(
        src_ref=src, dst_ref=dst, send_sem=send, recv_sem=recv, device_id=to, device_id_type=MESH
    )


def kernel(
    partial_ref,
    residual_hbm,
    post_hbm,
    final_hbm,
    t_head_ref,
    hidden_hbm,
    s_gain_hbm,
    s_head_ref,
    labels_hbm,
    lengths_hbm,
    grad_hbm,
    loss_hbm,
    residual_ref,
    post_ref,
    final_ref,
    hidden_ref,
    s_gain_ref,
    labels_ref,
    lengths_ref,
    grad_ref,
    loss_ref,
    in_sem,
    out_sem,
    w_t,
    w_s,
    pb,
    first_in,
    second_in,
    rows_in,
    tb,
    sb,
    res_in,
    stu_out,
    stu_in,
    asm_t,
    asm_s,
    normed,
    tab_own,
    tab,
    lab_col,
    wgt_col,
    t_log,
    s_log,
    lg,
    stat,
    stat_in,
    back,
    loss_blk,
    g,
    share,
    core_in,
    rr0,
    rr_x,
    rr1,
    rr2,
    ng_out,
    ng_in,
    sem_w,
    a_own,
    pool,
):
    me = Place()
    tp = me.y_hi * 16 + me.z * 4 + me.x
    dp = me.y_lo * 2 + me.c
    position = dp * 32 + tp

    load_s = pltpu.make_async_copy(s_head_ref, w_s, sem_w.at[0])
    load_t = pltpu.make_async_copy(t_head_ref, w_t, sem_w.at[1])
    small_copies = []
    for n, (src, dst) in enumerate(
        (
            (hidden_hbm, hidden_ref),
            (s_gain_hbm, s_gain_ref),
            (residual_hbm, residual_ref),
            (labels_hbm, labels_ref),
            (lengths_hbm, lengths_ref),
            (post_hbm, post_ref),
            (final_hbm, final_ref),
        )
    ):
        copy = pltpu.make_async_copy(src, dst, in_sem.at[n])
        copy.start()
        small_copies.append(copy)
    own_copies = []
    for q in range(4):
        copy = pltpu.make_async_copy(
            partial_ref.at[:, :, :, pl.ds(q * QT, QT)], pb.at[:, :, q], a_own.at[q]
        )
        copy.start()
        own_copies.append(copy)

    barrier = pltpu.get_barrier_semaphore()
    near = [me.to(**sent) for sent, heard in me.offsets("yz")]
    near += [me.along("x", me.shifted("x", k)) for k in (1, 2, 3)]
    for k in (1, 2, 3):
        near += [me.to(x=me.shifted("x", k), z=me.shifted("z", n)) for n in (1, 2, 3)]
        near += [me.to(x=me.shifted("x", k), h=1 - me.y_hi)]
    near += [me.sibling(), (1 - me.y_lo, 1 - me.c, me.y_hi, me.z, me.x)]
    for to in near:
        pl.semaphore_signal(barrier, inc=1, device_id=to, device_id_type=MESH)
    pl.semaphore_wait(barrier, len(near))

    opened = []

    def group(whole):
        n = len(opened)
        made = types.SimpleNamespace(
            whole=whole, send=pool.at[2 * n], recv=pool.at[2 * n + 1], copies=[], started=0
        )
        opened.append(made)
        return made

    def put(made, src, dst, to):
        made.to = to
        made.copies.append(remote(src, dst, made.send, made.recv, to))

    def start_all(groups):
        for made in groups:
            for copy in made.copies[made.started :]:
                copy.start()
            made.started = len(made.copies)

    def both_ends(made):
        return remote(made.whole, made.whole, made.send, made.recv, made.to)

    def arrive_all(groups):
        for made in groups:
            both_ends(made).wait_recv()

    for copy in own_copies:
        copy.wait()

    def pb_box(spots, lo, width):
        where = [pl.ds(spots[a], 1) if a in spots else slice(None) for a in "hzx"]
        return pb.at[where[0], where[1], where[2], :, pl.ds(lo, width)]

    first_stage, second_stage = [], []
    for p, (lo, width, axis, plane) in enumerate(PARTS_A):
        first = group(first_in[p])
        for n, (sent, heard) in enumerate(me.offsets(axis)):
            put(first, pb_box(sent, lo, width), first_in[p].at[n], me.to(**sent))
        second = group(second_in[p])
        for n, (sent, heard) in enumerate(me.offsets(plane)):
            spots = {axis: me.at(axis), **sent}
            src = pb.at[spots["h"], spots["z"], spots["x"], :, pl.ds(lo, width)]
            put(second, src, second_in[p].at[n], me.to(**sent))
        first_stage.append(first)
        second_stage.append(second)

    start_all(first_stage)
    load_t.start()
    load_s.start()

    for copy in small_copies:
        copy.wait()

    hidden = hidden_ref[...].astype(F32)
    s_gain = s_gain_ref[...].reshape(1, D_S)
    inverse = lax.rsqrt(jnp.mean(hidden * hidden, axis=-1, keepdims=True) + EPS)
    student = (hidden * inverse * s_gain).astype(BF16)
    for q in range(4):
        stu_out[q] = student[:, q * QS : (q + 1) * QS]
    stu_in[me.x] = stu_out[me.x]
    res_in[me.x] = residual_ref[...]

    def along_x(whole, src, dst):
        made = group(whole)
        for sent, heard in me.offsets("x"):
            put(made, src(sent["x"]), dst, me.to(**sent))
        return [made]

    student_copies = along_x(stu_in.at[pl.ds(0, 3)], lambda to: stu_out.at[to], stu_in.at[me.x])
    start_all(student_copies)
    residual_copies = along_x(res_in.at[pl.ds(0, 3)], lambda to: residual_ref, res_in.at[me.x])
    start_all(residual_copies)

    lane = lax.broadcasted_iota(jnp.int32, (1, LANES), 1)
    start = jnp.int32(0)
    weight = jnp.zeros((1, LANES), F32)
    for i in range(NSEQ):
        length = lengths_ref[0, i]
        end = start + length
        inside = (lane >= start) & (lane < end)
        one_over = 1.0 / jnp.full((1, LANES), length, jnp.int32).astype(F32)
        weight = jnp.where(inside, one_over, weight)
        start = end
    sub = lax.broadcasted_iota(jnp.int32, (8, LANES), 0)
    label_row = labels_ref[...].astype(F32)
    tab_own[...] = jnp.where(
        sub == 0,
        jnp.broadcast_to(label_row, (8, LANES)),
        jnp.where(sub == 1, jnp.broadcast_to(weight, (8, LANES)), 0.0),
    )
    tab[dp] = tab_own[...]
    tables = group(tab.at[pl.ds(0, 3)])
    for y_lo, c in ((me.y_lo, 1 - me.c), (1 - me.y_lo, me.c), (1 - me.y_lo, 1 - me.c)):
        put(tables, tab_own, tab.at[dp], (y_lo, c, me.y_hi, me.z, me.x))
    start_all([tables])

    def box(buf, spots, done, lo, width):
        where = []
        for a in "yzx":
            where.append(pl.ds(0, 4) if a in done else pl.ds(spots.get(a, me.at(a)), 1))
        return buf.at[me.c, where[0], where[1], where[2], :, pl.ds(lo, width)]

    def one_part(buf, lo, width, axes, done, whole=None):
        cols = pl.ds(lo, width)
        three = [pl.ds(0, 4) if a in done else pl.ds(me.at(a), 1) for a in "yzx"]
        three["yzx".index(axes[0])] = pl.ds(0, 3)
        live = LIVE if "y" in done and "z" in done else ()
        if live:
            three = [pl.ds(0, 4), pl.ds(0, 3), pl.ds(0, 3)]
        made = group(buf.at[me.c, three[0], three[1], three[2], :, cols] if whole is None else whole)
        own = [buf.at[me.c, y, z, pl.ds(me.x, 1), :, cols] for y, z in live]
        for sent, heard in me.offsets(axes):
            for src in own or [box(buf, {}, done, lo, width)]:
                put(made, src, src, me.to(**sent))
        return made

    def swap(buf, cols):
        made = group(buf.at[0, pl.ds(0, 3), :, :, :, cols])
        for y, z in LIVE:
            own = buf.at[me.c, y, z, :, :, cols]
            put(made, own, own, me.sibling())
        return made

    student_stages, teacher_stages = [[], [], []], [[], []]
    for stage in range(3):
        for lo, width, order in PARTS_S:
            made = one_part(sb, lo, width, order[stage], order[:stage])
            student_stages[stage].append(made)
    for lo, width, done, first, second in PARTS_T:
        whole = second_in[2] if len(first) == 2 else None
        teacher_stages[0].append(one_part(tb, lo, width, first, done, whole))
        teacher_stages[1].append(one_part(tb, lo, width, second, done + first))
    student_swap = [swap(sb, pl.ds(0, QS))]
    teacher_swap = [swap(tb, pl.ds(part[0], part[1])) for part in PARTS_T]

    arrive_all(student_copies)
    for i in range(4):
        asm_s[4 * i : 4 * i + 4, :] = stu_in[i].astype(F32)
    sb[me.c, me.y, me.z, me.x] = asm_s[...].astype(BF16)
    start_all(student_stages[0])


    arrive_all(first_stage)
    for p, (lo, width, axis, plane) in enumerate(PARTS_A):
        came = first_in[p]
        count = came.shape[0]

        @pl.loop(0, came.shape[1] * came.shape[2] * came.shape[3])
        def _(n, lo=lo, width=width, axis=axis, plane=plane, came=came, count=count):
            at, slot = {axis: me.at(axis)}, {axis: 0}
            for a in reversed(plane):
                size = 2 if a == "h" else 4
                at[a] = slot[a] = lax.rem(n, size)
                n = lax.div(n, size)
            cols = slice(lo, lo + width)
            whole = pb[at["h"], at["z"], at["x"], :, cols].astype(F32)
            for i in range(count):
                whole = whole + came[i, slot["h"], slot["z"], slot["x"]].astype(F32)
            pb[at["h"], at["z"], at["x"], :, cols] = whole.astype(BF16)

    start_all(second_stage)
    arrive_all(student_stages[0])
    start_all(student_stages[1])
    arrive_all(residual_copies)
    for q in range(4):
        for i in range(4):
            asm_t[q, 4 * i : 4 * i + 4, :] = res_in[i, :, q * QT : (q + 1) * QT].astype(F32)
    arrive_all(second_stage)
    for p, (lo, width, axis, plane) in enumerate(PARTS_A):
        whole = pb[me.y_hi, me.z, me.x, :, lo : lo + width].astype(F32)
        for n in range(second_in[p].shape[0]):
            whole = whole + second_in[p][n].astype(F32)
        rows_in[me.x, :, lo : lo + width] = whole.astype(BF16)

    row_copies = along_x(rows_in.at[pl.ds(0, 3)], lambda to: rows_in.at[me.x], rows_in.at[me.x])
    start_all(row_copies)
    arrive_all(student_stages[1])
    start_all(student_stages[2])
    arrive_all(row_copies)

    def row_inverse(quarters):
        total = sum(jnp.sum(v * v, axis=1, keepdims=True) for v in quarters)
        return lax.rsqrt(total / D_T + EPS)

    sums = [rows_in[q].astype(F32) for q in range(4)]
    scale = row_inverse(sums)
    for q in range(4):
        cols = slice(q * QT, (q + 1) * QT)
        asm_t[q] = asm_t[q] + sums[q] * scale * post_ref[cols].reshape(1, QT)
    scale = row_inverse([asm_t[q] for q in range(4)])
    for q in range(4):
        cols = slice(q * QT, (q + 1) * QT)
        normed[q] = (asm_t[q] * scale * final_ref[cols].reshape(1, QT)).astype(BF16)
    for lo, width, done, first, second in PARTS_T:
        cols = slice(lo, lo + width)
        if done:
            for q in range(4):
                tb[me.c, me.y, me.z, q, :, cols] = normed[q, :, cols]
        else:
            tb[me.c, me.y, me.z, me.x, :, cols] = normed[me.x, :, cols]
    start_all(teacher_stages[0])

    arrive_all([tables])
    for part in range(4):
        table = tab[part]
        for row, col in ((0, lab_col), (1, wgt_col)):
            turned = jnp.broadcast_to(table[row : row + 1, :], (LANES, LANES)).T
            for m, (c, y, z) in enumerate(PIECES):
                if (y % 2) * 2 + c == part:
                    j = (y // 2) * 4 + z
                    col[m * 16 : (m + 1) * 16, :] = turned[j * 16 : (j + 1) * 16, :]
    g[:, 2:4, 2:4] = jnp.zeros((2, 2, 2, 4, 16, QS), BF16)
    loss_blk[:, 2:4, 2:4] = jnp.zeros((2, 2, 2, 16, LANES), F32)

    arrive_all(teacher_stages[0])
    start_all(teacher_stages[1])

    def logits(buf, head, out, width, core):
        rows = pl.ds(pl.multiple_of(core * HALF, HALF), HALF)

        @pl.loop(0, VOC // 256)
        def _(n):
            cols = pl.ds(pl.multiple_of(n * 256, 256), 256)
            acc = None
            for q in range(4):
                live = jnp.concatenate(
                    [
                        buf[core, 0:2, :, q].reshape(128, width),
                        buf[core, 2:4, 0:2, q].reshape(64, width),
                    ],
                    axis=0,
                )
                head_rows = head[q * width : (q + 1) * width, cols]
                term = jnp.dot(live, head_rows, preferred_element_type=F32)
                acc = term if acc is None else acc + term
            out[rows, cols] = acc

    first_col = (position * VOC).astype(F32)

    def columns():
        return lax.broadcasted_iota(jnp.int32, (32, VOC), 1).astype(F32) + first_col

    lanes = lax.broadcasted_iota(jnp.int32, (32, LANES), 1)

    def student_stats():
        @pl.loop(0, ROWS // 32)
        def _(r):
            rows = pl.ds(pl.multiple_of(r * 32, 32), 32)
            s = s_log[rows, :]
            s_max = jnp.max(s, axis=1, keepdims=True)
            s_sum = jnp.sum(jnp.exp(s - s_max), axis=1, keepdims=True)
            hit = columns() == lab_col[rows, 0:1]
            value = jnp.sum(jnp.where(hit, s, 0.0), axis=1, keepdims=True)
            held = wgt_col[rows, :]
            for n, one in ((3, s_max), (4, s_sum), (5, value)):
                held = jnp.where(lanes == n, one, held)
            back[rows, :] = held

    def teacher_stats():
        @pl.loop(0, ROWS // 32)
        def _(r):
            rows = pl.ds(pl.multiple_of(r * 32, 32), 32)
            t = t_log[rows, :]
            t_max = jnp.max(t, axis=1, keepdims=True)
            t_exp = jnp.exp(t - t_max)
            t_sum = jnp.sum(t_exp, axis=1, keepdims=True)
            cross = jnp.sum(t_exp * (t - s_log[rows, :]), axis=1, keepdims=True)
            held = back[rows, :]
            for n, one in ((0, t_max), (1, t_sum), (2, cross)):
                held = jnp.where(lanes == n, one, held)
            back[rows, :] = held

    load_s.wait()
    arrive_all(student_stages[2])
    start_all(student_swap)
    logits(sb, w_s, s_log, QS, me.c)
    arrive_all(student_swap)
    logits(sb, w_s, s_log, QS, 1 - me.c)
    student_stats()
    load_t.wait()
    for p in (2, 0, 1):
        arrive_all([teacher_stages[1][p]])
        start_all([teacher_swap[p]])
    logits(tb, w_t, t_log, QT, me.c)
    arrive_all(teacher_swap)
    logits(tb, w_t, t_log, QT, 1 - me.c)
    teacher_stats()

    for i in range(3):
        turned = back[i * 128 : (i + 1) * 128, :].T
        stat[0, :, i * 128 : (i + 1) * 128] = turned[0:8, :]

    def merged(values):
        t_max = functools.reduce(jnp.maximum, [v[0:1] for v in values])
        s_max = functools.reduce(jnp.maximum, [v[3:4] for v in values])
        t_sum = cross = s_sum = label = 0.0
        for v in values:
            t_one = jnp.exp(v[0:1] - t_max)
            s_one = jnp.exp(v[3:4] - s_max)
            t_sum += v[1:2] * t_one
            cross += v[2:3] * t_one
            s_sum += v[4:5] * s_one
            label += v[5:6]
        return [t_max, t_sum, cross, s_max, s_sum, label, values[0][6:7]]

    for n, axes in enumerate(("c", "xz", "y")):
        if axes == "c":
            peers = [me.sibling()]
        else:
            peers = [me.to(**sent) for sent, heard in me.offsets(axes)]
        made = group(stat_in.at[n, pl.ds(0, len(peers))])
        for k, to in enumerate(peers):
            put(made, stat.at[n], stat_in.at[n, k], to)
        start_all([made])
        arrive_all([made])
        values = [stat[n]] + [stat_in[n, k] for k in range(len(peers))]
        for i, line in enumerate(merged(values)):
            stat[n + 1, i : i + 1, :] = line

    end = stat[3]
    t_whole = end[0:1] + jnp.log(end[1:2])
    s_whole = end[3:4] + jnp.log(end[4:5])
    divergence = end[2:3] / end[1:2] - t_whole + s_whole
    row_loss = jnp.where(end[6:7] > 0, divergence + BETA * (s_whole - end[5:6]), 0.0)
    sub = lax.broadcasted_iota(jnp.int32, (8, ROWS), 0)
    lines = jnp.zeros((8, ROWS), F32)
    for n, one in enumerate((t_whole, s_whole, row_loss)):
        lines = jnp.where(sub == n, jnp.broadcast_to(one, (8, ROWS)), lines)
    for i in range(3):
        tall = jnp.concatenate(
            [lines[:, i * 128 : (i + 1) * 128], jnp.zeros((120, LANES), F32)], axis=0
        )
        back[i * 128 : (i + 1) * 128, :] = tall.T
    for m, (c, y, z) in enumerate(PIECES):
        loss_blk[c, y, z] = jnp.broadcast_to(back[m * 16 : (m + 1) * 16, 2:3], (16, LANES))

    @pl.loop(0, ROWS // 32)
    def _(r):
        rows = pl.ds(pl.multiple_of(r * 32, 32), 32)
        t_prob = jnp.exp(t_log[rows, :] - back[rows, 0:1])
        s_prob = jnp.exp(s_log[rows, :] - back[rows, 1:2])
        hit = (columns() == lab_col[rows, 0:1]).astype(F32)
        scale = LOSS_SCALE * wgt_col[rows, 0:1]
        lg[rows, :] = (scale * ((1.0 + BETA) * s_prob - t_prob - BETA * hit)).astype(BF16)

    def quarter(k):
        q = me.shifted("x", k)
        share[k % 2] = lax.dot_general(
            lg[...],
            w_s[pl.ds(pl.multiple_of(q * QS, QS), QS), :],
            (((1,), (1,)), ((), ())),
            preferred_element_type=F32,
        )

    def core_rows(k, core, at, count):
        return share[k % 2, pl.ds(pl.multiple_of(core * HALF + at, 64), count), :]

    reduce_copies = [group(rr0[0]), group(rr0[1]), group(rr_x.at[:, pl.ds(0, 3)])]

    def first_reduce(k):
        q = me.shifted("x", k)
        for p, (lo, width, axis, then) in enumerate(PARTS_G):
            for n, (sent, heard) in enumerate(me.offsets(axis)):
                where = {a: pl.ds(sent[a], 1) if a in sent else slice(None) for a in "yz"}
                src = g.at[me.c, where["y"], where["z"], q, :, pl.ds(lo, width)]
                put(reduce_copies[p], src, rr0[p].at[n, k - 1], me.to(**sent))
        if k < 4:
            for y, z in LIVE:
                src = g.at[me.c, y, z, q, :, pl.ds(LO_X, W_X)]
                put(reduce_copies[2], src, rr_x.at[k - 1, y, z], me.along("x", q))

    core_copies = []
    for k in range(1, 6):
        if k < 5:
            q = me.shifted("x", k)
            quarter(k)
            theirs = 1 - me.c
            g[theirs, 0:2, :, q] = core_rows(k, theirs, 0, 128).astype(BF16).reshape(2, 4, 16, QS)
            g[theirs, 2:4, 0:2, q] = core_rows(k, theirs, 128, 64).astype(BF16).reshape(2, 2, 16, QS)
            made = group(core_in.at[k - 1, pl.ds(0, 3)])
            for y, z in LIVE:
                put(made, g.at[theirs, y, z, q], core_in.at[k - 1, y, z], me.sibling())
            start_all([made])
            core_copies.append(made)
        if k > 1:
            q = me.shifted("x", k - 1)
            arrive_all([core_copies[k - 2]])
            other = core_in[k - 2, 0:2].reshape(128, QS).astype(F32)
            g[me.c, 0:2, :, q] = (core_rows(k - 1, me.c, 0, 128) + other).astype(BF16).reshape(2, 4, 16, QS)
            other = core_in[k - 2, 2:4, 0:2].reshape(64, QS).astype(F32)
            g[me.c, 2:4, 0:2, q] = (core_rows(k - 1, me.c, 128, 64) + other).astype(BF16).reshape(2, 2, 16, QS)
            first_reduce(k - 1)
            start_all(reduce_copies)

    arrive_all(reduce_copies)
    for p, (lo, width, axis, then) in enumerate(PARTS_G):
        cols = slice(lo, lo + width)
        for k in range(1, 5):
            q = me.shifted("x", k)

            @pl.loop(0, 4)
            def _(i, p=p, axis=axis, then=then, cols=cols, k=k, q=q):
                at = {axis: me.at(axis), then: i}
                slot = {axis: 0, then: i}
                whole = g[me.c, at["y"], at["z"], q, :, cols].astype(F32)
                for n in range(3):
                    whole = whole + rr0[p][n, k - 1, slot["y"], slot["z"]].astype(F32)
                g[me.c, at["y"], at["z"], q, :, cols] = whole.astype(BF16)

    cols_x = slice(LO_X, LO_X + W_X)
    for ys, zs in (((0, 1), 4), ((2, 3), 2)):
        for y in ys:

            @pl.loop(0, zs)
            def _(z, y=y):
                whole = g[me.c, y, z, me.x, :, cols_x].astype(F32)
                for n in range(3):
                    whole = whole + rr_x[n, y, z].astype(F32)
                g[me.c, y, z, me.x, :, cols_x] = whole.astype(BF16)

    second = [group(rr1), group(rr2)]
    for p, (lo, width, axis, then) in enumerate(PARTS_G):
        for n, (sent, heard) in enumerate(me.offsets(then)):
            at = {axis: me.at(axis), **sent}
            src = g.at[me.c, at["y"], at["z"], :, :, pl.ds(lo, width)]
            put(second[0], src, rr1.at[p, n], me.to(**sent))
    for n, (sent, heard) in enumerate(me.offsets("yz")):
        src = g.at[me.c, sent["y"], sent["z"], me.x, :, pl.ds(LO_X, W_X)]
        put(second[1], src, rr2.at[n], me.to(**sent))
    start_all(second)
    arrive_all(second)
    for p, (lo, width, axis, then) in enumerate(PARTS_G):
        for q in range(4):
            whole = g[me.c, me.y, me.z, q, :, lo : lo + width].astype(F32)
            for n in range(3):
                whole = whole + rr1[p, n, q].astype(F32)
            for i in range(4):
                ng_out[i, :, q * W_YZ + lo : q * W_YZ + lo + width] = whole[4 * i : 4 * i + 4]
    whole = g[me.c, me.y, me.z, me.x, :, cols_x].astype(F32)
    for n in range(15):
        whole = whole + rr2[n].astype(F32)
    for i in range(4):
        ng_out[i, :, 4 * W_YZ : 4 * W_YZ + W_X] = whole[4 * i : 4 * i + 4]

    ng_in[me.x] = ng_out[me.x]
    last = along_x(ng_in.at[pl.ds(0, 3)], lambda to: ng_out.at[to], ng_in.at[me.x])
    start_all(last)

    losses = loss_blk[me.c, me.y, me.z]
    mine = jnp.zeros((4, LANES), F32)
    for i in range(4):
        mine = jnp.where(me.x == i, losses[4 * i : 4 * i + 4], mine)
    diagonal = lax.broadcasted_iota(jnp.int32, (4, LANES), 0) == lax.broadcasted_iota(
        jnp.int32, (4, LANES), 1
    )
    loss_ref[...] = jnp.sum(jnp.where(diagonal, mine, 0.0), axis=0, keepdims=True)

    arrive_all(last)
    norm_parts = []
    for q in range(4):
        cols = slice(q * W_YZ, (q + 1) * W_YZ)
        norm_parts.append(ng_in[0, :, cols] + ng_in[1, :, cols] + ng_in[2, :, cols] + ng_in[3, :, cols])
        norm_parts.append(ng_in[q, :, 4 * W_YZ : 4 * W_YZ + W_X])
    norm_grad = jnp.concatenate(norm_parts, axis=1)
    live = me.y_hi * 4 + me.z < 6
    scaled = norm_grad * s_gain
    inner = jnp.mean(scaled * hidden, axis=1, keepdims=True)
    grad = inverse * scaled - hidden * (inverse * inverse * inverse) * inner
    grad_ref[...] = jnp.where(live, grad, 0.0)

    out_copies = (
        pltpu.make_async_copy(grad_ref, grad_hbm, out_sem.at[0]),
        pltpu.make_async_copy(loss_ref, loss_hbm, out_sem.at[1]),
    )
    for copy in out_copies:
        copy.start()

    for made in opened:
        both_ends(made).wait_send()
    assert len(opened) == GROUPS
    for copy in out_copies:
        copy.wait()


def scratch():
    dma = pltpu.SemaphoreType.DMA
    vm = pltpu.VMEM
    first = []
    for lo, width, axis, plane in PARTS_A:
        spots = [1 if a == axis else 2 if a == "h" else 4 for a in "hzx"]
        first.append(vm((1 if axis == "h" else 3, *spots, 16, width), BF16))
    rr0 = []
    for lo, width, axis, then in PARTS_G:
        spots = [1 if a == axis else 4 for a in "yz"]
        rr0.append(vm((3, 4, *spots, 16, width), BF16))
    return {
        "residual_ref": vm((4, D_T), BF16),
        "post_ref": vm((D_T,), F32),
        "final_ref": vm((D_T,), F32),
        "hidden_ref": vm((4, D_S), BF16),
        "s_gain_ref": vm((D_S,), F32),
        "labels_ref": vm((1, LANES), jnp.int32),
        "lengths_ref": pltpu.SMEM((1, NSEQ), jnp.int32),
        "grad_ref": vm((4, D_S), F32),
        "loss_ref": vm((1, LANES), F32),
        "in_sem": dma((7,)),
        "out_sem": dma((2,)),
        "w_t": vm((D_T, VOC), BF16),
        "w_s": vm((D_S, VOC), BF16),
        "pb": vm((2, 4, 4, 16, QT), BF16),
        "first_in": tuple(first),
        "second_in": tuple(vm((n, 16, PARTS_A[0][1]), BF16) for n in (7, 7, 15)),
        "rows_in": vm((4, 16, QT), BF16),
        "tb": vm((2, 4, 4, 4, 16, QT), BF16),
        "sb": vm((2, 4, 4, 4, 16, QS), BF16),
        "res_in": vm((4, 4, D_T), BF16),
        "stu_out": vm((4, 4, QS), BF16),
        "stu_in": vm((4, 4, QS), BF16),
        "asm_t": vm((4, 16, QT), F32),
        "asm_s": vm((16, QS), F32),
        "normed": vm((4, 16, QT), BF16),
        "tab_own": vm((8, LANES), F32),
        "tab": vm((4, 8, LANES), F32),
        "lab_col": vm((ROWS, LANES), F32),
        "wgt_col": vm((ROWS, LANES), F32),
        "t_log": vm((ROWS, VOC), F32),
        "s_log": vm((ROWS, VOC), F32),
        "lg": vm((ROWS, VOC), BF16),
        "stat": vm((4, 8, ROWS), F32),
        "stat_in": vm((3, 15, 8, ROWS), F32),
        "back": vm((ROWS, LANES), F32),
        "loss_blk": vm((2, 4, 4, 16, LANES), F32),
        "g": vm((2, 4, 4, 4, 16, QS), BF16),
        "share": vm((2, ROWS, QS), F32),
        "core_in": vm((4, 4, 4, 16, QS), BF16),
        "rr0": tuple(rr0),
        "rr_x": vm((3, 4, 4, 16, W_X), BF16),
        "rr1": vm((2, 3, 4, 16, PARTS_G[0][1]), BF16),
        "rr2": vm((15, 16, W_X), BF16),
        "ng_out": vm((4, 4, 4 * W_YZ + W_X), F32),
        "ng_in": vm((4, 4, 4 * W_YZ + W_X), F32),
        "sem_w": dma((2,)),
        "a_own": dma((4,)),
        "pool": dma((2 * GROUPS,)),
    }


def shards(
    teacher_partial,
    teacher_residual,
    post_gain,
    final_gain,
    teacher_head,
    student_hidden,
    student_gain,
    student_head,
    labels,
    lengths,
):
    place = pl.BlockSpec(memory_space=pl.ANY)
    spaces = scratch()
    names = list(spaces)
    leaves, tree = jax.tree.flatten([spaces[n] for n in names])

    def body(*refs):
        held = jax.tree.unflatten(tree, refs[12:])
        kernel(*refs[:12], **dict(zip(names, held)))

    grad, loss = pl.pallas_call(
        body,
        out_shape=(
            jax.ShapeDtypeStruct((4, D_S), F32),
            jax.ShapeDtypeStruct((1, LANES), F32),
        ),
        in_specs=[place] * 10,
        out_specs=(place, place),
        scratch_shapes=leaves,
        compiler_params=pltpu.CompilerParams(
            collective_id=0, has_side_effects=True, vmem_limit_bytes=60 * 2**20
        ),
        name="distill",
    )(
        teacher_partial.reshape(2, 4, 16, D_T),
        teacher_residual,
        post_gain,
        final_gain,
        teacher_head,
        student_hidden,
        student_gain,
        student_head,
        labels.reshape(1, -1),
        lengths,
    )
    return grad, loss[0, :4]


def solution(mesh):
    torus = Mesh(mesh.devices.reshape(2, 2, 2, 4, 4), ("dp_0", "dp_1", "tp_0", "tp_1", "tp_2"))
    return jax.shard_map(
        shards,
        mesh=torus,
        in_specs=(
            P(TP, DP, None),
            P(DP_TP, None),
            P(),
            P(),
            P(None, DP_TP),
            P(DP_TP, None),
            P(),
            P(None, DP_TP),
            P(DP),
            P(DP, None),
        ),
        out_specs=(P(DP_TP, None), P(DP_TP)),
        check_vma=False,
    )
```

```python
import functools
import itertools
import types

import jax
import jax.numpy as jnp
from jax import lax
from jax.experimental import pallas as pl
from jax.experimental.pallas import tpu as pltpu
from jax.sharding import Mesh
from jax.sharding import PartitionSpec as P

TP = ("tp_0", "tp_1", "tp_2")
DP = ("dp_0", "dp_1")
DP_TP = ("dp_0", "dp_1", "tp_0", "tp_1", "tp_2")
MESH = pl.DeviceIdType.MESH

EPS = 1e-06
BETA = 0.5
LOSS_SCALE = 1024.0

F32 = jnp.float32
BF16 = jnp.bfloat16

D_T = 4608
D_S = 3584
QT = D_T // 4
QS = D_S // 4
VOC = 1024
ROWS = 384
HALF = 192
NSEQ = 8
LANES = 128

PARTS_A = ((0, 384, "x", "hz"), (384, 384, "z", "hx"), (768, 384, "h", "zx"))
PARTS_T = ((0, 384, "x", "y", "z"), (384, 384, "x", "z", "y"), (768, 384, "", "yz", "x"))
PARTS_S = ((0, 256, "xyz"), (256, 384, "yzx"), (640, 256, "zxy"))
PARTS_G = ((0, 256, "z", "y"), (256, 256, "y", "z"))
LO_X, W_X = (512, 384)
W_YZ = 512
GROUPS = 42


def live_pieces():
    held = []
    for c in range(2):
        held += [(c, y, z) for y in range(2) for z in range(4)]
        held += [(c, y, z) for y in range(2, 4) for z in range(2)]
    return held


PIECES = live_pieces()
LIVE = ((pl.ds(0, 2), pl.ds(0, 4)), (pl.ds(2, 2), pl.ds(0, 2)))


class Place:
    def __init__(self):
        self.c = lax.axis_index("dp_1")
        self.z = lax.axis_index("tp_1")
        self.x = lax.axis_index("tp_2")
        self.y_lo = lax.axis_index("dp_0")
        self.y_hi = lax.axis_index("tp_0")
        self.y = self.y_hi * 2 + self.y_lo

    def at(self, axis):
        return {"x": self.x, "y": self.y, "z": self.z, "h": self.y_hi}[axis]

    def shifted(self, axis, k):
        return lax.rem(self.at(axis) + k, 2 if axis == "h" else 4)

    def to(self, **spots):
        y_lo, y_hi = self.y_lo, self.y_hi
        if "y" in spots:
            y_lo, y_hi = lax.rem(spots["y"], 2), lax.div(spots["y"], 2)
        y_hi = spots.get("h", y_hi)
        return (y_lo, self.c, y_hi, spots.get("z", self.z), spots.get("x", self.x))

    def along(self, axis, to):
        return self.to(**{axis: to})

    def offsets(self, axes):
        sizes = [2 if a == "h" else 4 for a in axes]
        for ks in itertools.product(*[range(n) for n in sizes]):
            if any(ks):
                sent = {a: self.shifted(a, k) for a, k in zip(axes, ks)}
                heard = {a: self.shifted(a, n - k) for a, k, n in zip(axes, ks, sizes)}
                yield (sent, heard)

    def across(self, k):
        to = self.shifted("y", k)
        return (lax.rem(to, 2), 1 - self.c, lax.div(to, 2), self.z, self.x)

    def sibling(self):
        return (self.y_lo, 1 - self.c, self.y_hi, self.z, self.x)


def remote(src, dst, send, recv, to):
    return pltpu.make_async_remote_copy(
        src_ref=src, dst_ref=dst, send_sem=send, recv_sem=recv, device_id=to, device_id_type=MESH
    )


def kernel(
    partial_ref,
    residual_hbm,
    post_hbm,
    final_hbm,
    t_head_ref,
    hidden_hbm,
    s_gain_hbm,
    s_head_ref,
    labels_hbm,
    lengths_hbm,
    grad_hbm,
    loss_hbm,
    residual_ref,
    post_ref,
    final_ref,
    hidden_ref,
    s_gain_ref,
    labels_ref,
    lengths_ref,
    grad_ref,
    loss_ref,
    in_sem,
    out_sem,
    w_t,
    w_s,
    pb,
    first_in,
    second_in,
    rows_in,
    tb,
    sb,
    res_in,
    stu_out,
    stu_in,
    asm_t,
    asm_s,
    normed,
    tab_own,
    tab,
    lab_col,
    wgt_col,
    t_log,
    s_log,
    lg,
    stat,
    stat_in,
    back,
    loss_blk,
    g,
    share,
    core_in,
    rr0,
    rr_x,
    rr1,
    rr2,
    ng_out,
    ng_in,
    sem_w,
    a_own,
    pool,
):
    me = Place()
    tp = me.y_hi * 16 + me.z * 4 + me.x
    dp = me.y_lo * 2 + me.c
    position = dp * 32 + tp

    load_s = pltpu.make_async_copy(s_head_ref, w_s, sem_w.at[0])
    load_t = pltpu.make_async_copy(t_head_ref, w_t, sem_w.at[1])
    small_copies = []
    for n, (src, dst) in enumerate(
        (
            (hidden_hbm, hidden_ref),
            (s_gain_hbm, s_gain_ref),
            (residual_hbm, residual_ref),
            (labels_hbm, labels_ref),
            (lengths_hbm, lengths_ref),
            (post_hbm, post_ref),
            (final_hbm, final_ref),
        )
    ):
        copy = pltpu.make_async_copy(src, dst, in_sem.at[n])
        copy.start()
        small_copies.append(copy)
    own_copies = []
    for q in range(4):
        copy = pltpu.make_async_copy(
            partial_ref.at[:, :, :, pl.ds(q * QT, QT)], pb.at[:, :, q], a_own.at[q]
        )
        copy.start()
        own_copies.append(copy)

    barrier = pltpu.get_barrier_semaphore()
    near = [me.to(**sent) for sent, heard in me.offsets("yz")]
    near += [me.along("x", me.shifted("x", k)) for k in (1, 2, 3)]
    for k in (1, 2, 3):
        near += [me.to(x=me.shifted("x", k), z=me.shifted("z", n)) for n in (1, 2, 3)]
        near += [me.to(x=me.shifted("x", k), h=1 - me.y_hi)]
    near += [me.sibling()] + [me.across(k) for k in (1, 2, 3)]
    for to in near:
        pl.semaphore_signal(barrier, inc=1, device_id=to, device_id_type=MESH)
    pl.semaphore_wait(barrier, len(near))

    opened = []

    def group(whole):
        n = len(opened)
        made = types.SimpleNamespace(
            whole=whole, send=pool.at[2 * n], recv=pool.at[2 * n + 1], copies=[], started=0
        )
        opened.append(made)
        return made

    def put(made, src, dst, to):
        made.to = to
        made.copies.append(remote(src, dst, made.send, made.recv, to))

    def start_all(groups):
        for made in groups:
            for copy in made.copies[made.started :]:
                copy.start()
            made.started = len(made.copies)

    def both_ends(made):
        return remote(made.whole, made.whole, made.send, made.recv, made.to)

    def arrive_all(groups):
        for made in groups:
            both_ends(made).wait_recv()

    for copy in own_copies:
        copy.wait()

    def pb_box(spots, lo, width):
        where = [pl.ds(spots[a], 1) if a in spots else slice(None) for a in "hzx"]
        return pb.at[where[0], where[1], where[2], :, pl.ds(lo, width)]

    first_stage, second_stage = [], []
    for p, (lo, width, axis, plane) in enumerate(PARTS_A):
        first = group(first_in[p])
        for n, (sent, heard) in enumerate(me.offsets(axis)):
            put(first, pb_box(sent, lo, width), first_in[p].at[n], me.to(**sent))
        second = group(second_in[p])
        for n, (sent, heard) in enumerate(me.offsets(plane)):
            spots = {axis: me.at(axis), **sent}
            src = pb.at[spots["h"], spots["z"], spots["x"], :, pl.ds(lo, width)]
            put(second, src, second_in[p].at[n], me.to(**sent))
        first_stage.append(first)
        second_stage.append(second)

    start_all(first_stage)
    load_t.start()
    load_s.start()

    for copy in small_copies:
        copy.wait()

    hidden = hidden_ref[...].astype(F32)
    s_gain = s_gain_ref[...].reshape(1, D_S)
    inverse = lax.rsqrt(jnp.mean(hidden * hidden, axis=-1, keepdims=True) + EPS)
    student = (hidden * inverse * s_gain).astype(BF16)
    for q in range(4):
        stu_out[q] = student[:, q * QS : (q + 1) * QS]
    stu_in[me.x] = stu_out[me.x]
    res_in[me.x] = residual_ref[...]

    def along_x(whole, src, dst):
        made = group(whole)
        for sent, heard in me.offsets("x"):
            put(made, src(sent["x"]), dst, me.to(**sent))
        return [made]

    student_copies = along_x(stu_in.at[pl.ds(0, 3)], lambda to: stu_out.at[to], stu_in.at[me.x])
    start_all(student_copies)
    residual_copies = along_x(res_in.at[pl.ds(0, 3)], lambda to: residual_ref, res_in.at[me.x])
    start_all(residual_copies)

    lane = lax.broadcasted_iota(jnp.int32, (1, LANES), 1)
    start = jnp.int32(0)
    weight = jnp.zeros((1, LANES), F32)
    for i in range(NSEQ):
        length = lengths_ref[0, i]
        end = start + length
        inside = (lane >= start) & (lane < end)
        one_over = 1.0 / jnp.full((1, LANES), length, jnp.int32).astype(F32)
        weight = jnp.where(inside, one_over, weight)
        start = end
    sub = lax.broadcasted_iota(jnp.int32, (8, LANES), 0)
    label_row = labels_ref[...].astype(F32)
    tab_own[...] = jnp.where(
        sub == 0,
        jnp.broadcast_to(label_row, (8, LANES)),
        jnp.where(sub == 1, jnp.broadcast_to(weight, (8, LANES)), 0.0),
    )
    tab[dp] = tab_own[...]
    tables = group(tab.at[pl.ds(0, 3)])
    for y_lo, c in ((me.y_lo, 1 - me.c), (1 - me.y_lo, me.c), (1 - me.y_lo, 1 - me.c)):
        put(tables, tab_own, tab.at[dp], (y_lo, c, me.y_hi, me.z, me.x))
    start_all([tables])

    def box(buf, spots, done, lo, width):
        where = []
        for a in "yzx":
            where.append(pl.ds(0, 4) if a in done else pl.ds(spots.get(a, me.at(a)), 1))
        return buf.at[me.c, where[0], where[1], where[2], :, pl.ds(lo, width)]

    def one_part(buf, lo, width, axes, done, whole=None):
        cols = pl.ds(lo, width)
        three = [pl.ds(0, 4) if a in done else pl.ds(me.at(a), 1) for a in "yzx"]
        three["yzx".index(axes[0])] = pl.ds(0, 3)
        live = LIVE if "y" in done and "z" in done else ()
        if live:
            three = [pl.ds(0, 4), pl.ds(0, 3), pl.ds(0, 3)]
        made = group(buf.at[me.c, three[0], three[1], three[2], :, cols] if whole is None else whole)
        own = [buf.at[me.c, y, z, pl.ds(me.x, 1), :, cols] for y, z in live]
        for sent, heard in me.offsets(axes):
            for src in own or [box(buf, {}, done, lo, width)]:
                put(made, src, src, me.to(**sent))
        return made

    def swap(buf, cols):
        made = group(buf.at[0, pl.ds(0, 3), :, :, :, cols])
        for y, z in LIVE:
            own = buf.at[me.c, y, z, :, :, cols]
            put(made, own, own, me.sibling())
        return made

    student_stages, teacher_stages = [[], [], []], [[], []]
    for stage in range(3):
        for lo, width, order in PARTS_S:
            made = one_part(sb, lo, width, order[stage], order[:stage])
            student_stages[stage].append(made)
    for lo, width, done, first, second in PARTS_T:
        whole = second_in[2] if len(first) == 2 else None
        teacher_stages[0].append(one_part(tb, lo, width, first, done, whole))
        teacher_stages[1].append(one_part(tb, lo, width, second, done + first))
    student_swap = [swap(sb, pl.ds(0, QS))]
    teacher_swap = [swap(tb, pl.ds(part[0], part[1])) for part in PARTS_T]

    arrive_all(student_copies)
    for i in range(4):
        asm_s[4 * i : 4 * i + 4, :] = stu_in[i].astype(F32)
    sb[me.c, me.y, me.z, me.x] = asm_s[...].astype(BF16)
    start_all(student_stages[0])


    for p, (lo, width, axis, plane) in enumerate(PARTS_A):
        arrive_all([first_stage[p]])
        came = first_in[p]
        count = came.shape[0]

        @pl.loop(0, came.shape[1] * came.shape[2] * came.shape[3])
        def _(n, lo=lo, width=width, axis=axis, plane=plane, came=came, count=count):
            at, slot = {axis: me.at(axis)}, {axis: 0}
            for a in reversed(plane):
                size = 2 if a == "h" else 4
                at[a] = slot[a] = lax.rem(n, size)
                n = lax.div(n, size)
            cols = slice(lo, lo + width)
            whole = pb[at["h"], at["z"], at["x"], :, cols].astype(F32)
            for i in range(count):
                whole = whole + came[i, slot["h"], slot["z"], slot["x"]].astype(F32)
            pb[at["h"], at["z"], at["x"], :, cols] = whole.astype(BF16)

        start_all([second_stage[p]])

    arrive_all(student_stages[0])
    start_all(student_stages[1])
    arrive_all(residual_copies)
    for q in range(4):
        for i in range(4):
            asm_t[q, 4 * i : 4 * i + 4, :] = res_in[i, :, q * QT : (q + 1) * QT].astype(F32)
    for p, (lo, width, axis, plane) in enumerate(PARTS_A):
        arrive_all([second_stage[p]])
        whole = pb[me.y_hi, me.z, me.x, :, lo : lo + width].astype(F32)
        for n in range(second_in[p].shape[0]):
            whole = whole + second_in[p][n].astype(F32)
        rows_in[me.x, :, lo : lo + width] = whole.astype(BF16)

    row_copies = along_x(rows_in.at[pl.ds(0, 3)], lambda to: rows_in.at[me.x], rows_in.at[me.x])
    start_all(row_copies)
    arrive_all(student_stages[1])
    start_all(student_stages[2])
    arrive_all(row_copies)

    def row_inverse(quarters):
        total = sum(jnp.sum(v * v, axis=1, keepdims=True) for v in quarters)
        return lax.rsqrt(total / D_T + EPS)

    sums = [rows_in[q].astype(F32) for q in range(4)]
    scale = row_inverse(sums)
    for q in range(4):
        cols = slice(q * QT, (q + 1) * QT)
        asm_t[q] = asm_t[q] + sums[q] * scale * post_ref[cols].reshape(1, QT)
    scale = row_inverse([asm_t[q] for q in range(4)])
    for q in range(4):
        cols = slice(q * QT, (q + 1) * QT)
        normed[q] = (asm_t[q] * scale * final_ref[cols].reshape(1, QT)).astype(BF16)
    for lo, width, done, first, second in PARTS_T:
        cols = slice(lo, lo + width)
        if done:
            for q in range(4):
                tb[me.c, me.y, me.z, q, :, cols] = normed[q, :, cols]
        else:
            tb[me.c, me.y, me.z, me.x, :, cols] = normed[me.x, :, cols]
    start_all(teacher_stages[0])

    arrive_all([tables])
    for part in range(4):
        table = tab[part]
        for row, col in ((0, lab_col), (1, wgt_col)):
            turned = jnp.broadcast_to(table[row : row + 1, :], (LANES, LANES)).T
            for m, (c, y, z) in enumerate(PIECES):
                if (y % 2) * 2 + c == part:
                    j = (y // 2) * 4 + z
                    col[m * 16 : (m + 1) * 16, :] = turned[j * 16 : (j + 1) * 16, :]
    g[:, 2:4, 2:4] = jnp.zeros((2, 2, 2, 4, 16, QS), BF16)
    loss_blk[:, 2:4, 2:4] = jnp.zeros((2, 2, 2, 16, LANES), F32)

    for p in range(3):
        arrive_all([teacher_stages[0][p]])
        start_all([teacher_stages[1][p]])

    def logits(buf, head, out, width, core):
        rows = pl.ds(pl.multiple_of(core * HALF, HALF), HALF)

        @pl.loop(0, VOC // 256)
        def _(n):
            cols = pl.ds(pl.multiple_of(n * 256, 256), 256)
            acc = None
            for q in range(4):
                live = jnp.concatenate(
                    [
                        buf[core, 0:2, :, q].reshape(128, width),
                        buf[core, 2:4, 0:2, q].reshape(64, width),
                    ],
                    axis=0,
                )
                head_rows = head[q * width : (q + 1) * width, cols]
                term = jnp.dot(live, head_rows, preferred_element_type=F32)
                acc = term if acc is None else acc + term
            out[rows, cols] = acc

    first_col = (position * VOC).astype(F32)

    def columns():
        return lax.broadcasted_iota(jnp.int32, (32, VOC), 1).astype(F32) + first_col

    lanes = lax.broadcasted_iota(jnp.int32, (32, LANES), 1)

    def student_stats():
        @pl.loop(0, ROWS // 32)
        def _(r):
            rows = pl.ds(pl.multiple_of(r * 32, 32), 32)
            s = s_log[rows, :]
            s_max = jnp.max(s, axis=1, keepdims=True)
            s_sum = jnp.sum(jnp.exp(s - s_max), axis=1, keepdims=True)
            hit = columns() == lab_col[rows, 0:1]
            value = jnp.sum(jnp.where(hit, s, 0.0), axis=1, keepdims=True)
            held = wgt_col[rows, :]
            for n, one in ((3, s_max), (4, s_sum), (5, value)):
                held = jnp.where(lanes == n, one, held)
            back[rows, :] = held

    def teacher_stats():
        @pl.loop(0, ROWS // 32)
        def _(r):
            rows = pl.ds(pl.multiple_of(r * 32, 32), 32)
            t = t_log[rows, :]
            t_max = jnp.max(t, axis=1, keepdims=True)
            t_exp = jnp.exp(t - t_max)
            t_sum = jnp.sum(t_exp, axis=1, keepdims=True)
            cross = jnp.sum(t_exp * (t - s_log[rows, :]), axis=1, keepdims=True)
            held = back[rows, :]
            for n, one in ((0, t_max), (1, t_sum), (2, cross)):
                held = jnp.where(lanes == n, one, held)
            back[rows, :] = held

    load_s.wait()
    arrive_all(student_stages[2])
    start_all(student_swap)
    logits(sb, w_s, s_log, QS, me.c)
    arrive_all(student_swap)
    logits(sb, w_s, s_log, QS, 1 - me.c)
    student_stats()
    load_t.wait()
    for p in (2, 0, 1):
        arrive_all([teacher_stages[1][p]])
        start_all([teacher_swap[p]])
    logits(tb, w_t, t_log, QT, me.c)
    arrive_all(teacher_swap)
    logits(tb, w_t, t_log, QT, 1 - me.c)
    teacher_stats()

    for i in range(3):
        turned = back[i * 128 : (i + 1) * 128, :].T
        stat[0, :, i * 128 : (i + 1) * 128] = turned[0:8, :]

    def merged(values):
        t_max = functools.reduce(jnp.maximum, [v[0:1] for v in values])
        s_max = functools.reduce(jnp.maximum, [v[3:4] for v in values])
        t_sum = cross = s_sum = label = 0.0
        for v in values:
            t_one = jnp.exp(v[0:1] - t_max)
            s_one = jnp.exp(v[3:4] - s_max)
            t_sum += v[1:2] * t_one
            cross += v[2:3] * t_one
            s_sum += v[4:5] * s_one
            label += v[5:6]
        return [t_max, t_sum, cross, s_max, s_sum, label, values[0][6:7]]

    for n, axes in enumerate(("xz", "yc")):
        if axes == "xz":
            peers = [me.to(**sent) for sent, heard in me.offsets(axes)]
        else:
            peers = [me.along("y", me.shifted("y", k)) for k in (1, 2, 3)]
            peers += [me.sibling()] + [me.across(k) for k in (1, 2, 3)]
        made = group(stat_in.at[n, pl.ds(0, len(peers))])
        for k, to in enumerate(peers):
            put(made, stat.at[n], stat_in.at[n, k], to)
        start_all([made])
        arrive_all([made])
        values = [stat[n]] + [stat_in[n, k] for k in range(len(peers))]
        for i, line in enumerate(merged(values)):
            stat[n + 1, i : i + 1, :] = line

    end = stat[2]
    t_whole = end[0:1] + jnp.log(end[1:2])
    s_whole = end[3:4] + jnp.log(end[4:5])
    divergence = end[2:3] / end[1:2] - t_whole + s_whole
    row_loss = jnp.where(end[6:7] > 0, divergence + BETA * (s_whole - end[5:6]), 0.0)
    sub = lax.broadcasted_iota(jnp.int32, (8, ROWS), 0)
    lines = jnp.zeros((8, ROWS), F32)
    for n, one in enumerate((t_whole, s_whole, row_loss)):
        lines = jnp.where(sub == n, jnp.broadcast_to(one, (8, ROWS)), lines)
    for i in range(3):
        tall = jnp.concatenate(
            [lines[:, i * 128 : (i + 1) * 128], jnp.zeros((120, LANES), F32)], axis=0
        )
        back[i * 128 : (i + 1) * 128, :] = tall.T
    for m, (c, y, z) in enumerate(PIECES):
        loss_blk[c, y, z] = jnp.broadcast_to(back[m * 16 : (m + 1) * 16, 2:3], (16, LANES))

    @pl.loop(0, ROWS // 32)
    def _(r):
        rows = pl.ds(pl.multiple_of(r * 32, 32), 32)
        t_prob = jnp.exp(t_log[rows, :] - back[rows, 0:1])
        s_prob = jnp.exp(s_log[rows, :] - back[rows, 1:2])
        hit = (columns() == lab_col[rows, 0:1]).astype(F32)
        scale = LOSS_SCALE * wgt_col[rows, 0:1]
        lg[rows, :] = (scale * ((1.0 + BETA) * s_prob - t_prob - BETA * hit)).astype(BF16)

    def quarter(k):
        q = me.shifted("x", k)
        share[k % 2] = lax.dot_general(
            lg[...],
            w_s[pl.ds(pl.multiple_of(q * QS, QS), QS), :],
            (((1,), (1,)), ((), ())),
            preferred_element_type=F32,
        )

    def core_rows(k, core, at, count):
        return share[k % 2, pl.ds(pl.multiple_of(core * HALF + at, 64), count), :]

    reduce_copies = [group(rr0[0]), group(rr0[1]), group(rr_x.at[:, pl.ds(0, 3)])]

    def first_reduce(k):
        q = me.shifted("x", k)
        for p, (lo, width, axis, then) in enumerate(PARTS_G):
            for n, (sent, heard) in enumerate(me.offsets(axis)):
                where = {a: pl.ds(sent[a], 1) if a in sent else slice(None) for a in "yz"}
                src = g.at[me.c, where["y"], where["z"], q, :, pl.ds(lo, width)]
                put(reduce_copies[p], src, rr0[p].at[n, k - 1], me.to(**sent))
        if k < 4:
            for y, z in LIVE:
                src = g.at[me.c, y, z, q, :, pl.ds(LO_X, W_X)]
                put(reduce_copies[2], src, rr_x.at[k - 1, y, z], me.along("x", q))

    core_copies = []
    for k in range(1, 6):
        if k < 5:
            q = me.shifted("x", k)
            quarter(k)
            theirs = 1 - me.c
            g[theirs, 0:2, :, q] = core_rows(k, theirs, 0, 128).astype(BF16).reshape(2, 4, 16, QS)
            g[theirs, 2:4, 0:2, q] = core_rows(k, theirs, 128, 64).astype(BF16).reshape(2, 2, 16, QS)
            made = group(core_in.at[k - 1, pl.ds(0, 3)])
            for y, z in LIVE:
                put(made, g.at[theirs, y, z, q], core_in.at[k - 1, y, z], me.sibling())
            start_all([made])
            core_copies.append(made)
        if k > 1:
            q = me.shifted("x", k - 1)
            arrive_all([core_copies[k - 2]])
            other = core_in[k - 2, 0:2].reshape(128, QS).astype(F32)
            g[me.c, 0:2, :, q] = (core_rows(k - 1, me.c, 0, 128) + other).astype(BF16).reshape(2, 4, 16, QS)
            other = core_in[k - 2, 2:4, 0:2].reshape(64, QS).astype(F32)
            g[me.c, 2:4, 0:2, q] = (core_rows(k - 1, me.c, 128, 64) + other).astype(BF16).reshape(2, 2, 16, QS)
            first_reduce(k - 1)
            start_all(reduce_copies)

    second = [group(rr1.at[0]), group(rr1.at[1]), group(rr2)]
    for p, (lo, width, axis, then) in enumerate(PARTS_G):
        cols = slice(lo, lo + width)
        arrive_all([reduce_copies[p]])
        for k in range(1, 5):
            q = me.shifted("x", k)

            @pl.loop(0, 4)
            def _(i, p=p, axis=axis, then=then, cols=cols, k=k, q=q):
                at = {axis: me.at(axis), then: i}
                slot = {axis: 0, then: i}
                whole = g[me.c, at["y"], at["z"], q, :, cols].astype(F32)
                for n in range(3):
                    whole = whole + rr0[p][n, k - 1, slot["y"], slot["z"]].astype(F32)
                g[me.c, at["y"], at["z"], q, :, cols] = whole.astype(BF16)

        for n, (sent, heard) in enumerate(me.offsets(then)):
            at = {axis: me.at(axis), **sent}
            src = g.at[me.c, at["y"], at["z"], :, :, pl.ds(lo, width)]
            put(second[p], src, rr1.at[p, n], me.to(**sent))
        start_all([second[p]])

    cols_x = slice(LO_X, LO_X + W_X)
    arrive_all([reduce_copies[2]])
    for ys, zs in (((0, 1), 4), ((2, 3), 2)):
        for y in ys:

            @pl.loop(0, zs)
            def _(z, y=y):
                whole = g[me.c, y, z, me.x, :, cols_x].astype(F32)
                for n in range(3):
                    whole = whole + rr_x[n, y, z].astype(F32)
                g[me.c, y, z, me.x, :, cols_x] = whole.astype(BF16)

    for n, (sent, heard) in enumerate(me.offsets("yz")):
        src = g.at[me.c, sent["y"], sent["z"], me.x, :, pl.ds(LO_X, W_X)]
        put(second[2], src, rr2.at[n], me.to(**sent))
    start_all([second[2]])
    for p, (lo, width, axis, then) in enumerate(PARTS_G):
        arrive_all([second[p]])
        for q in range(4):
            whole = g[me.c, me.y, me.z, q, :, lo : lo + width].astype(F32)
            for n in range(3):
                whole = whole + rr1[p, n, q].astype(F32)
            for i in range(4):
                ng_out[i, :, q * W_YZ + lo : q * W_YZ + lo + width] = whole[4 * i : 4 * i + 4]
    arrive_all([second[2]])
    whole = g[me.c, me.y, me.z, me.x, :, cols_x].astype(F32)
    for n in range(15):
        whole = whole + rr2[n].astype(F32)
    for i in range(4):
        ng_out[i, :, 4 * W_YZ : 4 * W_YZ + W_X] = whole[4 * i : 4 * i + 4]

    ng_in[me.x] = ng_out[me.x]
    last = along_x(ng_in.at[pl.ds(0, 3)], lambda to: ng_out.at[to], ng_in.at[me.x])
    start_all(last)

    losses = loss_blk[me.c, me.y, me.z]
    mine = jnp.zeros((4, LANES), F32)
    for i in range(4):
        mine = jnp.where(me.x == i, losses[4 * i : 4 * i + 4], mine)
    diagonal = lax.broadcasted_iota(jnp.int32, (4, LANES), 0) == lax.broadcasted_iota(
        jnp.int32, (4, LANES), 1
    )
    loss_ref[...] = jnp.sum(jnp.where(diagonal, mine, 0.0), axis=0, keepdims=True)

    arrive_all(last)
    norm_parts = []
    for q in range(4):
        cols = slice(q * W_YZ, (q + 1) * W_YZ)
        norm_parts.append(ng_in[0, :, cols] + ng_in[1, :, cols] + ng_in[2, :, cols] + ng_in[3, :, cols])
        norm_parts.append(ng_in[q, :, 4 * W_YZ : 4 * W_YZ + W_X])
    norm_grad = jnp.concatenate(norm_parts, axis=1)
    live = me.y_hi * 4 + me.z < 6
    scaled = norm_grad * s_gain
    inner = jnp.mean(scaled * hidden, axis=1, keepdims=True)
    grad = inverse * scaled - hidden * (inverse * inverse * inverse) * inner
    grad_ref[...] = jnp.where(live, grad, 0.0)

    out_copies = (
        pltpu.make_async_copy(grad_ref, grad_hbm, out_sem.at[0]),
        pltpu.make_async_copy(loss_ref, loss_hbm, out_sem.at[1]),
    )
    for copy in out_copies:
        copy.start()

    for made in opened:
        both_ends(made).wait_send()
    assert len(opened) == GROUPS
    for copy in out_copies:
        copy.wait()


def scratch():
    dma = pltpu.SemaphoreType.DMA
    vm = pltpu.VMEM
    first = []
    for lo, width, axis, plane in PARTS_A:
        spots = [1 if a == axis else 2 if a == "h" else 4 for a in "hzx"]
        first.append(vm((1 if axis == "h" else 3, *spots, 16, width), BF16))
    rr0 = []
    for lo, width, axis, then in PARTS_G:
        spots = [1 if a == axis else 4 for a in "yz"]
        rr0.append(vm((3, 4, *spots, 16, width), BF16))
    return {
        "residual_ref": vm((4, D_T), BF16),
        "post_ref": vm((D_T,), F32),
        "final_ref": vm((D_T,), F32),
        "hidden_ref": vm((4, D_S), BF16),
        "s_gain_ref": vm((D_S,), F32),
        "labels_ref": vm((1, LANES), jnp.int32),
        "lengths_ref": pltpu.SMEM((1, NSEQ), jnp.int32),
        "grad_ref": vm((4, D_S), F32),
        "loss_ref": vm((1, LANES), F32),
        "in_sem": dma((7,)),
        "out_sem": dma((2,)),
        "w_t": vm((D_T, VOC), BF16),
        "w_s": vm((D_S, VOC), BF16),
        "pb": vm((2, 4, 4, 16, QT), BF16),
        "first_in": tuple(first),
        "second_in": tuple(vm((n, 16, PARTS_A[0][1]), BF16) for n in (7, 7, 15)),
        "rows_in": vm((4, 16, QT), BF16),
        "tb": vm((2, 4, 4, 4, 16, QT), BF16),
        "sb": vm((2, 4, 4, 4, 16, QS), BF16),
        "res_in": vm((4, 4, D_T), BF16),
        "stu_out": vm((4, 4, QS), BF16),
        "stu_in": vm((4, 4, QS), BF16),
        "asm_t": vm((4, 16, QT), F32),
        "asm_s": vm((16, QS), F32),
        "normed": vm((4, 16, QT), BF16),
        "tab_own": vm((8, LANES), F32),
        "tab": vm((4, 8, LANES), F32),
        "lab_col": vm((ROWS, LANES), F32),
        "wgt_col": vm((ROWS, LANES), F32),
        "t_log": vm((ROWS, VOC), F32),
        "s_log": vm((ROWS, VOC), F32),
        "lg": vm((ROWS, VOC), BF16),
        "stat": vm((3, 8, ROWS), F32),
        "stat_in": vm((2, 15, 8, ROWS), F32),
        "back": vm((ROWS, LANES), F32),
        "loss_blk": vm((2, 4, 4, 16, LANES), F32),
        "g": vm((2, 4, 4, 4, 16, QS), BF16),
        "share": vm((2, ROWS, QS), F32),
        "core_in": vm((4, 4, 4, 16, QS), BF16),
        "rr0": tuple(rr0),
        "rr_x": vm((3, 4, 4, 16, W_X), BF16),
        "rr1": vm((2, 3, 4, 16, PARTS_G[0][1]), BF16),
        "rr2": vm((15, 16, W_X), BF16),
        "ng_out": vm((4, 4, 4 * W_YZ + W_X), F32),
        "ng_in": vm((4, 4, 4 * W_YZ + W_X), F32),
        "sem_w": dma((2,)),
        "a_own": dma((4,)),
        "pool": dma((2 * GROUPS,)),
    }


def shards(
    teacher_partial,
    teacher_residual,
    post_gain,
    final_gain,
    teacher_head,
    student_hidden,
    student_gain,
    student_head,
    labels,
    lengths,
):
    place = pl.BlockSpec(memory_space=pl.ANY)
    spaces = scratch()
    names = list(spaces)
    leaves, tree = jax.tree.flatten([spaces[n] for n in names])

    def body(*refs):
        held = jax.tree.unflatten(tree, refs[12:])
        kernel(*refs[:12], **dict(zip(names, held)))

    grad, loss = pl.pallas_call(
        body,
        out_shape=(
            jax.ShapeDtypeStruct((4, D_S), F32),
            jax.ShapeDtypeStruct((1, LANES), F32),
        ),
        in_specs=[place] * 10,
        out_specs=(place, place),
        scratch_shapes=leaves,
        compiler_params=pltpu.CompilerParams(
            collective_id=0, has_side_effects=True, vmem_limit_bytes=60 * 2**20
        ),
        name="distill",
    )(
        teacher_partial.reshape(2, 4, 16, D_T),
        teacher_residual,
        post_gain,
        final_gain,
        teacher_head,
        student_hidden,
        student_gain,
        student_head,
        labels.reshape(1, -1),
        lengths,
    )
    return grad, loss[0, :4]


def solution(mesh):
    torus = Mesh(mesh.devices.reshape(2, 2, 2, 4, 4), ("dp_0", "dp_1", "tp_0", "tp_1", "tp_2"))
    return jax.shard_map(
        shards,
        mesh=torus,
        in_specs=(
            P(TP, DP, None),
            P(DP_TP, None),
            P(),
            P(),
            P(None, DP_TP),
            P(DP_TP, None),
            P(),
            P(None, DP_TP),
            P(DP),
            P(DP, None),
        ),
        out_specs=(P(DP_TP, None), P(DP_TP)),
        check_vma=False,
    )
```

```python
import functools
import itertools
import types

import jax
import jax.numpy as jnp
from jax import lax
from jax.experimental import pallas as pl
from jax.experimental.pallas import tpu as pltpu
from jax.sharding import Mesh
from jax.sharding import PartitionSpec as P

TP = ("tp_0", "tp_1", "tp_2")
DP = ("dp_0", "dp_1")
DP_TP = ("dp_0", "dp_1", "tp_0", "tp_1", "tp_2")
MESH = pl.DeviceIdType.MESH

EPS = 1e-06
BETA = 0.5
LOSS_SCALE = 1024.0

F32 = jnp.float32
BF16 = jnp.bfloat16

D_T = 4608
D_S = 3584
QT = D_T // 4
QS = D_S // 4
VOC = 1024
ROWS = 384
HALF = 192
NSEQ = 8
LANES = 128

PARTS_A = ((0, 384, "x", "hz"), (384, 384, "z", "hx"), (768, 384, "h", "zx"))
PARTS_T = ((0, 384, "x", "y", "z"), (384, 384, "x", "z", "y"), (768, 384, "", "yz", "x"))
PARTS_S = ((0, 256, "xyz"), (256, 384, "yzx"), (640, 256, "zxy"))
PARTS_G = ((0, 256, "z", "y"), (256, 256, "y", "z"))
LO_X, W_X = (512, 384)
W_YZ = 512
GROUPS = 42


def live_pieces():
    held = []
    for c in range(2):
        held += [(c, y, z) for y in range(2) for z in range(4)]
        held += [(c, y, z) for y in range(2, 4) for z in range(2)]
    return held


PIECES = live_pieces()
LIVE = ((pl.ds(0, 2), pl.ds(0, 4)), (pl.ds(2, 2), pl.ds(0, 2)))


class Place:
    def __init__(self):
        self.c = lax.axis_index("dp_1")
        self.z = lax.axis_index("tp_1")
        self.x = lax.axis_index("tp_2")
        self.y_lo = lax.axis_index("dp_0")
        self.y_hi = lax.axis_index("tp_0")
        self.y = self.y_hi * 2 + self.y_lo

    def at(self, axis):
        return {"x": self.x, "y": self.y, "z": self.z, "h": self.y_hi}[axis]

    def shifted(self, axis, k):
        return lax.rem(self.at(axis) + k, 2 if axis == "h" else 4)

    def to(self, **spots):
        y_lo, y_hi = self.y_lo, self.y_hi
        if "y" in spots:
            y_lo, y_hi = lax.rem(spots["y"], 2), lax.div(spots["y"], 2)
        y_hi = spots.get("h", y_hi)
        return (y_lo, self.c, y_hi, spots.get("z", self.z), spots.get("x", self.x))

    def along(self, axis, to):
        return self.to(**{axis: to})

    def offsets(self, axes):
        sizes = [2 if a == "h" else 4 for a in axes]
        for ks in itertools.product(*[range(n) for n in sizes]):
            if any(ks):
                sent = {a: self.shifted(a, k) for a, k in zip(axes, ks)}
                heard = {a: self.shifted(a, n - k) for a, k, n in zip(axes, ks, sizes)}
                yield (sent, heard)

    def across(self, k):
        to = self.shifted("y", k)
        return (lax.rem(to, 2), 1 - self.c, lax.div(to, 2), self.z, self.x)

    def sibling(self):
        return (self.y_lo, 1 - self.c, self.y_hi, self.z, self.x)


def remote(src, dst, send, recv, to):
    return pltpu.make_async_remote_copy(
        src_ref=src, dst_ref=dst, send_sem=send, recv_sem=recv, device_id=to, device_id_type=MESH
    )


def kernel(
    partial_ref,
    residual_hbm,
    post_hbm,
    final_hbm,
    t_head_ref,
    hidden_hbm,
    s_gain_hbm,
    s_head_ref,
    labels_hbm,
    lengths_hbm,
    grad_hbm,
    loss_hbm,
    residual_ref,
    post_ref,
    final_ref,
    hidden_ref,
    s_gain_ref,
    labels_ref,
    lengths_ref,
    grad_ref,
    loss_ref,
    in_sem,
    out_sem,
    w_t,
    w_s,
    pb,
    first_in,
    second_in,
    rows_in,
    tb,
    sb,
    res_in,
    stu_out,
    stu_in,
    asm_t,
    asm_s,
    normed,
    tab_own,
    tab,
    lab_col,
    wgt_col,
    t_log,
    s_log,
    lg,
    stat,
    stat_in,
    back,
    loss_blk,
    g,
    share,
    core_in,
    rr0,
    rr_x,
    rr1,
    rr2,
    ng_out,
    ng_in,
    sem_w,
    a_own,
    pool,
):
    me = Place()
    tp = me.y_hi * 16 + me.z * 4 + me.x
    dp = me.y_lo * 2 + me.c
    position = dp * 32 + tp

    load_s = pltpu.make_async_copy(s_head_ref, w_s, sem_w.at[0])
    load_t = pltpu.make_async_copy(t_head_ref, w_t, sem_w.at[1])
    barrier = pltpu.get_barrier_semaphore()
    near = [me.to(**sent) for sent, heard in me.offsets("yz")]
    near += [me.along("x", me.shifted("x", k)) for k in (1, 2, 3)]
    for k in (1, 2, 3):
        near += [me.to(x=me.shifted("x", k), z=me.shifted("z", n)) for n in (1, 2, 3)]
        near += [me.to(x=me.shifted("x", k), h=1 - me.y_hi)]
    near += [me.sibling()] + [me.across(k) for k in (1, 2, 3)]
    for to in near:
        pl.semaphore_signal(barrier, inc=1, device_id=to, device_id_type=MESH)

    small_copies = []
    for n, (src, dst) in enumerate(
        (
            (hidden_hbm, hidden_ref),
            (s_gain_hbm, s_gain_ref),
            (residual_hbm, residual_ref),
            (labels_hbm, labels_ref),
            (lengths_hbm, lengths_ref),
            (post_hbm, post_ref),
            (final_hbm, final_ref),
        )
    ):
        copy = pltpu.make_async_copy(src, dst, in_sem.at[n])
        copy.start()
        small_copies.append(copy)
    own_copies = []
    for q in range(4):
        copy = pltpu.make_async_copy(
            partial_ref.at[:, :, :, pl.ds(q * QT, QT)], pb.at[:, :, q], a_own.at[q]
        )
        copy.start()
        own_copies.append(copy)

    pl.semaphore_wait(barrier, len(near))

    opened = []

    def group(whole):
        n = len(opened)
        made = types.SimpleNamespace(
            whole=whole, send=pool.at[2 * n], recv=pool.at[2 * n + 1], copies=[], started=0
        )
        opened.append(made)
        return made

    def put(made, src, dst, to):
        made.to = to
        made.copies.append(remote(src, dst, made.send, made.recv, to))

    def start_all(groups):
        for made in groups:
            for copy in made.copies[made.started :]:
                copy.start()
            made.started = len(made.copies)

    def both_ends(made):
        return remote(made.whole, made.whole, made.send, made.recv, made.to)

    def arrive_all(groups):
        for made in groups:
            both_ends(made).wait_recv()

    for copy in own_copies:
        copy.wait()

    def pb_box(spots, lo, width):
        where = [pl.ds(spots[a], 1) if a in spots else slice(None) for a in "hzx"]
        return pb.at[where[0], where[1], where[2], :, pl.ds(lo, width)]

    first_stage, second_stage = [], []
    for p, (lo, width, axis, plane) in enumerate(PARTS_A):
        first = group(first_in[p])
        for n, (sent, heard) in enumerate(me.offsets(axis)):
            put(first, pb_box(sent, lo, width), first_in[p].at[n], me.to(**sent))
        second = group(second_in[p])
        for n, (sent, heard) in enumerate(me.offsets(plane)):
            spots = {axis: me.at(axis), **sent}
            src = pb.at[spots["h"], spots["z"], spots["x"], :, pl.ds(lo, width)]
            put(second, src, second_in[p].at[n], me.to(**sent))
        first_stage.append(first)
        second_stage.append(second)

    start_all(first_stage)
    load_t.start()
    load_s.start()

    for copy in small_copies:
        copy.wait()

    hidden = hidden_ref[...].astype(F32)
    s_gain = s_gain_ref[...].reshape(1, D_S)
    inverse = lax.rsqrt(jnp.mean(hidden * hidden, axis=-1, keepdims=True) + EPS)
    student = (hidden * inverse * s_gain).astype(BF16)
    for q in range(4):
        stu_out[q] = student[:, q * QS : (q + 1) * QS]
    stu_in[me.x] = stu_out[me.x]
    res_in[me.x] = residual_ref[...]

    def along_x(whole, src, dst):
        made = group(whole)
        for sent, heard in me.offsets("x"):
            put(made, src(sent["x"]), dst, me.to(**sent))
        return [made]

    student_copies = along_x(stu_in.at[pl.ds(0, 3)], lambda to: stu_out.at[to], stu_in.at[me.x])
    start_all(student_copies)
    residual_copies = along_x(res_in.at[pl.ds(0, 3)], lambda to: residual_ref, res_in.at[me.x])
    start_all(residual_copies)

    lane = lax.broadcasted_iota(jnp.int32, (1, LANES), 1)
    start = jnp.int32(0)
    weight = jnp.zeros((1, LANES), F32)
    for i in range(NSEQ):
        length = lengths_ref[0, i]
        end = start + length
        inside = (lane >= start) & (lane < end)
        one_over = 1.0 / jnp.full((1, LANES), length, jnp.int32).astype(F32)
        weight = jnp.where(inside, one_over, weight)
        start = end
    sub = lax.broadcasted_iota(jnp.int32, (8, LANES), 0)
    label_row = labels_ref[...].astype(F32)
    tab_own[...] = jnp.where(
        sub == 0,
        jnp.broadcast_to(label_row, (8, LANES)),
        jnp.where(sub == 1, jnp.broadcast_to(weight, (8, LANES)), 0.0),
    )
    tab[dp] = tab_own[...]
    tables = group(tab.at[pl.ds(0, 3)])
    for y_lo, c in ((me.y_lo, 1 - me.c), (1 - me.y_lo, me.c), (1 - me.y_lo, 1 - me.c)):
        put(tables, tab_own, tab.at[dp], (y_lo, c, me.y_hi, me.z, me.x))
    start_all([tables])

    def box(buf, spots, done, lo, width):
        where = []
        for a in "yzx":
            where.append(pl.ds(0, 4) if a in done else pl.ds(spots.get(a, me.at(a)), 1))
        return buf.at[me.c, where[0], where[1], where[2], :, pl.ds(lo, width)]

    def one_part(buf, lo, width, axes, done, whole=None):
        cols = pl.ds(lo, width)
        three = [pl.ds(0, 4) if a in done else pl.ds(me.at(a), 1) for a in "yzx"]
        three["yzx".index(axes[0])] = pl.ds(0, 3)
        live = LIVE if "y" in done and "z" in done else ()
        if live:
            three = [pl.ds(0, 4), pl.ds(0, 3), pl.ds(0, 3)]
        made = group(buf.at[me.c, three[0], three[1], three[2], :, cols] if whole is None else whole)
        own = [buf.at[me.c, y, z, pl.ds(me.x, 1), :, cols] for y, z in live]
        for sent, heard in me.offsets(axes):
            for src in own or [box(buf, {}, done, lo, width)]:
                put(made, src, src, me.to(**sent))
        return made

    def swap(buf, cols):
        made = group(buf.at[0, pl.ds(0, 3), :, :, :, cols])
        for y, z in LIVE:
            own = buf.at[me.c, y, z, :, :, cols]
            put(made, own, own, me.sibling())
        return made

    student_stages, teacher_stages = [[], [], []], [[], []]
    for stage in range(3):
        for lo, width, order in PARTS_S:
            made = one_part(sb, lo, width, order[stage], order[:stage])
            student_stages[stage].append(made)
    for lo, width, done, first, second in PARTS_T:
        whole = second_in[2] if len(first) == 2 else None
        teacher_stages[0].append(one_part(tb, lo, width, first, done, whole))
        teacher_stages[1].append(one_part(tb, lo, width, second, done + first))
    student_swap = [swap(sb, pl.ds(0, QS))]
    teacher_swap = [swap(tb, pl.ds(part[0], part[1])) for part in PARTS_T]

    arrive_all(student_copies)
    for i in range(4):
        asm_s[4 * i : 4 * i + 4, :] = stu_in[i].astype(F32)
    sb[me.c, me.y, me.z, me.x] = asm_s[...].astype(BF16)
    start_all(student_stages[0])


    for p, (lo, width, axis, plane) in enumerate(PARTS_A):
        arrive_all([first_stage[p]])
        came = first_in[p]
        count = came.shape[0]

        @pl.loop(0, came.shape[1] * came.shape[2] * came.shape[3])
        def _(n, lo=lo, width=width, axis=axis, plane=plane, came=came, count=count):
            at, slot = {axis: me.at(axis)}, {axis: 0}
            for a in reversed(plane):
                size = 2 if a == "h" else 4
                at[a] = slot[a] = lax.rem(n, size)
                n = lax.div(n, size)
            cols = slice(lo, lo + width)
            whole = pb[at["h"], at["z"], at["x"], :, cols].astype(F32)
            for i in range(count):
                whole = whole + came[i, slot["h"], slot["z"], slot["x"]].astype(F32)
            pb[at["h"], at["z"], at["x"], :, cols] = whole.astype(BF16)

        start_all([second_stage[p]])

    arrive_all(student_stages[0])
    start_all(student_stages[1])
    arrive_all(residual_copies)
    for q in range(4):
        for i in range(4):
            asm_t[q, 4 * i : 4 * i + 4, :] = res_in[i, :, q * QT : (q + 1) * QT].astype(F32)
    for p, (lo, width, axis, plane) in enumerate(PARTS_A):
        arrive_all([second_stage[p]])
        whole = pb[me.y_hi, me.z, me.x, :, lo : lo + width].astype(F32)
        for n in range(second_in[p].shape[0]):
            whole = whole + second_in[p][n].astype(F32)
        rows_in[me.x, :, lo : lo + width] = whole.astype(BF16)

    row_copies = along_x(rows_in.at[pl.ds(0, 3)], lambda to: rows_in.at[me.x], rows_in.at[me.x])
    start_all(row_copies)
    arrive_all(student_stages[1])
    start_all(student_stages[2])
    arrive_all(row_copies)

    def row_inverse(quarters):
        total = sum(jnp.sum(v * v, axis=1, keepdims=True) for v in quarters)
        return lax.rsqrt(total / D_T + EPS)

    sums = [rows_in[q].astype(F32) for q in range(4)]
    scale = row_inverse(sums)
    for q in range(4):
        cols = slice(q * QT, (q + 1) * QT)
        asm_t[q] = asm_t[q] + sums[q] * scale * post_ref[cols].reshape(1, QT)
    scale = row_inverse([asm_t[q] for q in range(4)])
    for q in range(4):
        cols = slice(q * QT, (q + 1) * QT)
        normed[q] = (asm_t[q] * scale * final_ref[cols].reshape(1, QT)).astype(BF16)
    for lo, width, done, first, second in PARTS_T:
        cols = slice(lo, lo + width)
        if done:
            for q in range(4):
                tb[me.c, me.y, me.z, q, :, cols] = normed[q, :, cols]
        else:
            tb[me.c, me.y, me.z, me.x, :, cols] = normed[me.x, :, cols]
    start_all(teacher_stages[0])

    arrive_all([tables])
    for part in range(4):
        table = tab[part]
        for row, col in ((0, lab_col), (1, wgt_col)):
            turned = jnp.broadcast_to(table[row : row + 1, :], (LANES, LANES)).T
            for m, (c, y, z) in enumerate(PIECES):
                if (y % 2) * 2 + c == part:
                    j = (y // 2) * 4 + z
                    col[m * 16 : (m + 1) * 16, :] = turned[j * 16 : (j + 1) * 16, :]
    g[:, 2:4, 2:4] = jnp.zeros((2, 2, 2, 4, 16, QS), BF16)
    loss_blk[:, 2:4, 2:4] = jnp.zeros((2, 2, 2, 16, LANES), F32)

    for p in range(3):
        arrive_all([teacher_stages[0][p]])
        start_all([teacher_stages[1][p]])

    def logits(buf, head, out, width, core):
        rows = pl.ds(pl.multiple_of(core * HALF, HALF), HALF)

        @pl.loop(0, VOC // 256)
        def _(n):
            cols = pl.ds(pl.multiple_of(n * 256, 256), 256)
            acc = None
            for q in range(4):
                live = jnp.concatenate(
                    [
                        buf[core, 0:2, :, q].reshape(128, width),
                        buf[core, 2:4, 0:2, q].reshape(64, width),
                    ],
                    axis=0,
                )
                head_rows = head[q * width : (q + 1) * width, cols]
                term = jnp.dot(live, head_rows, preferred_element_type=F32)
                acc = term if acc is None else acc + term
            out[rows, cols] = acc

    first_col = (position * VOC).astype(F32)

    def columns():
        return lax.broadcasted_iota(jnp.int32, (32, VOC), 1).astype(F32) + first_col

    lanes = lax.broadcasted_iota(jnp.int32, (32, LANES), 1)

    def student_stats():
        @pl.loop(0, ROWS // 32)
        def _(r):
            rows = pl.ds(pl.multiple_of(r * 32, 32), 32)
            s = s_log[rows, :]
            s_max = jnp.max(s, axis=1, keepdims=True)
            s_sum = jnp.sum(jnp.exp(s - s_max), axis=1, keepdims=True)
            hit = columns() == lab_col[rows, 0:1]
            value = jnp.sum(jnp.where(hit, s, 0.0), axis=1, keepdims=True)
            held = wgt_col[rows, :]
            for n, one in ((3, s_max), (4, s_sum), (5, value)):
                held = jnp.where(lanes == n, one, held)
            back[rows, :] = held

    def teacher_stats():
        @pl.loop(0, ROWS // 32)
        def _(r):
            rows = pl.ds(pl.multiple_of(r * 32, 32), 32)
            t = t_log[rows, :]
            t_max = jnp.max(t, axis=1, keepdims=True)
            t_exp = jnp.exp(t - t_max)
            t_sum = jnp.sum(t_exp, axis=1, keepdims=True)
            cross = jnp.sum(t_exp * (t - s_log[rows, :]), axis=1, keepdims=True)
            held = back[rows, :]
            for n, one in ((0, t_max), (1, t_sum), (2, cross)):
                held = jnp.where(lanes == n, one, held)
            back[rows, :] = held

    load_s.wait()
    arrive_all(student_stages[2])
    start_all(student_swap)
    logits(sb, w_s, s_log, QS, me.c)
    arrive_all(student_swap)
    logits(sb, w_s, s_log, QS, 1 - me.c)
    student_stats()
    load_t.wait()
    for p in (2, 0, 1):
        arrive_all([teacher_stages[1][p]])
        start_all([teacher_swap[p]])
    logits(tb, w_t, t_log, QT, me.c)
    arrive_all(teacher_swap)
    logits(tb, w_t, t_log, QT, 1 - me.c)
    teacher_stats()

    for i in range(3):
        turned = back[i * 128 : (i + 1) * 128, :].T
        stat[0, :, i * 128 : (i + 1) * 128] = turned[0:8, :]

    def merged(values):
        t_max = functools.reduce(jnp.maximum, [v[0:1] for v in values])
        s_max = functools.reduce(jnp.maximum, [v[3:4] for v in values])
        t_sum = cross = s_sum = label = 0.0
        for v in values:
            t_one = jnp.exp(v[0:1] - t_max)
            s_one = jnp.exp(v[3:4] - s_max)
            t_sum += v[1:2] * t_one
            cross += v[2:3] * t_one
            s_sum += v[4:5] * s_one
            label += v[5:6]
        return [t_max, t_sum, cross, s_max, s_sum, label, values[0][6:7]]

    for n, axes in enumerate(("xz", "yc")):
        if axes == "xz":
            peers = [me.to(**sent) for sent, heard in me.offsets(axes)]
        else:
            peers = [me.along("y", me.shifted("y", k)) for k in (1, 2, 3)]
            peers += [me.sibling()] + [me.across(k) for k in (1, 2, 3)]
        made = group(stat_in.at[n, pl.ds(0, len(peers))])
        for k, to in enumerate(peers):
            put(made, stat.at[n], stat_in.at[n, k], to)
        start_all([made])
        arrive_all([made])
        values = [stat[n]] + [stat_in[n, k] for k in range(len(peers))]
        for i, line in enumerate(merged(values)):
            stat[n + 1, i : i + 1, :] = line

    end = stat[2]
    t_whole = end[0:1] + jnp.log(end[1:2])
    s_whole = end[3:4] + jnp.log(end[4:5])
    divergence = end[2:3] / end[1:2] - t_whole + s_whole
    row_loss = jnp.where(end[6:7] > 0, divergence + BETA * (s_whole - end[5:6]), 0.0)
    sub = lax.broadcasted_iota(jnp.int32, (8, ROWS), 0)
    lines = jnp.zeros((8, ROWS), F32)
    for n, one in enumerate((t_whole, s_whole, row_loss)):
        lines = jnp.where(sub == n, jnp.broadcast_to(one, (8, ROWS)), lines)
    for i in range(3):
        tall = jnp.concatenate(
            [lines[:, i * 128 : (i + 1) * 128], jnp.zeros((120, LANES), F32)], axis=0
        )
        back[i * 128 : (i + 1) * 128, :] = tall.T
    for m, (c, y, z) in enumerate(PIECES):
        loss_blk[c, y, z] = jnp.broadcast_to(back[m * 16 : (m + 1) * 16, 2:3], (16, LANES))

    @pl.loop(0, ROWS // 32)
    def _(r):
        rows = pl.ds(pl.multiple_of(r * 32, 32), 32)
        t_prob = jnp.exp(t_log[rows, :] - back[rows, 0:1])
        s_prob = jnp.exp(s_log[rows, :] - back[rows, 1:2])
        hit = (columns() == lab_col[rows, 0:1]).astype(F32)
        scale = LOSS_SCALE * wgt_col[rows, 0:1]
        lg[rows, :] = (scale * ((1.0 + BETA) * s_prob - t_prob - BETA * hit)).astype(BF16)

    def quarter(k):
        q = me.shifted("x", k)
        share[k % 3] = lax.dot_general(
            lg[...],
            w_s[pl.ds(pl.multiple_of(q * QS, QS), QS), :],
            (((1,), (1,)), ((), ())),
            preferred_element_type=F32,
        )

    def core_rows(k, core, at, count):
        return share[k % 3, pl.ds(pl.multiple_of(core * HALF + at, 64), count), :]

    reduce_copies = [group(rr0[0]), group(rr0[1]), group(rr_x.at[:, pl.ds(0, 3)])]

    def first_reduce(k):
        q = me.shifted("x", k)
        for p, (lo, width, axis, then) in enumerate(PARTS_G):
            for n, (sent, heard) in enumerate(me.offsets(axis)):
                where = {a: pl.ds(sent[a], 1) if a in sent else slice(None) for a in "yz"}
                src = g.at[me.c, where["y"], where["z"], q, :, pl.ds(lo, width)]
                put(reduce_copies[p], src, rr0[p].at[n, k - 1], me.to(**sent))
        if k < 4:
            for y, z in LIVE:
                src = g.at[me.c, y, z, q, :, pl.ds(LO_X, W_X)]
                put(reduce_copies[2], src, rr_x.at[k - 1, y, z], me.along("x", q))

    core_copies = []
    for k in range(1, 7):
        if k < 5:
            q = me.shifted("x", k)
            quarter(k)
            theirs = 1 - me.c
            g[theirs, 0:2, :, q] = core_rows(k, theirs, 0, 128).astype(BF16).reshape(2, 4, 16, QS)
            g[theirs, 2:4, 0:2, q] = core_rows(k, theirs, 128, 64).astype(BF16).reshape(2, 2, 16, QS)
            made = group(core_in.at[k - 1, pl.ds(0, 3)])
            for y, z in LIVE:
                put(made, g.at[theirs, y, z, q], core_in.at[k - 1, y, z], me.sibling())
            start_all([made])
            core_copies.append(made)
        if k > 2:
            q = me.shifted("x", k - 2)
            arrive_all([core_copies[k - 3]])
            other = core_in[k - 3, 0:2].reshape(128, QS).astype(F32)
            g[me.c, 0:2, :, q] = (core_rows(k - 2, me.c, 0, 128) + other).astype(BF16).reshape(2, 4, 16, QS)
            other = core_in[k - 3, 2:4, 0:2].reshape(64, QS).astype(F32)
            g[me.c, 2:4, 0:2, q] = (core_rows(k - 2, me.c, 128, 64) + other).astype(BF16).reshape(2, 2, 16, QS)
            first_reduce(k - 2)
            start_all(reduce_copies)

    second = [group(rr1.at[0]), group(rr1.at[1]), group(rr2)]
    for p, (lo, width, axis, then) in enumerate(PARTS_G):
        cols = slice(lo, lo + width)
        arrive_all([reduce_copies[p]])
        for k in range(1, 5):
            q = me.shifted("x", k)

            @pl.loop(0, 4)
            def _(i, p=p, axis=axis, then=then, cols=cols, k=k, q=q):
                at = {axis: me.at(axis), then: i}
                slot = {axis: 0, then: i}
                whole = g[me.c, at["y"], at["z"], q, :, cols].astype(F32)
                for n in range(3):
                    whole = whole + rr0[p][n, k - 1, slot["y"], slot["z"]].astype(F32)
                g[me.c, at["y"], at["z"], q, :, cols] = whole.astype(BF16)

        for n, (sent, heard) in enumerate(me.offsets(then)):
            at = {axis: me.at(axis), **sent}
            src = g.at[me.c, at["y"], at["z"], :, :, pl.ds(lo, width)]
            put(second[p], src, rr1.at[p, n], me.to(**sent))
        start_all([second[p]])

    cols_x = slice(LO_X, LO_X + W_X)
    arrive_all([reduce_copies[2]])
    for ys, zs in (((0, 1), 4), ((2, 3), 2)):
        for y in ys:

            @pl.loop(0, zs)
            def _(z, y=y):
                whole = g[me.c, y, z, me.x, :, cols_x].astype(F32)
                for n in range(3):
                    whole = whole + rr_x[n, y, z].astype(F32)
                g[me.c, y, z, me.x, :, cols_x] = whole.astype(BF16)

    for n, (sent, heard) in enumerate(me.offsets("yz")):
        src = g.at[me.c, sent["y"], sent["z"], me.x, :, pl.ds(LO_X, W_X)]
        put(second[2], src, rr2.at[n], me.to(**sent))
    start_all([second[2]])
    for p, (lo, width, axis, then) in enumerate(PARTS_G):
        arrive_all([second[p]])
        for q in range(4):
            whole = g[me.c, me.y, me.z, q, :, lo : lo + width].astype(F32)
            for n in range(3):
                whole = whole + rr1[p, n, q].astype(F32)
            for i in range(4):
                ng_out[i, :, q * W_YZ + lo : q * W_YZ + lo + width] = whole[4 * i : 4 * i + 4]
    arrive_all([second[2]])
    whole = g[me.c, me.y, me.z, me.x, :, cols_x].astype(F32)
    for n in range(15):
        whole = whole + rr2[n].astype(F32)
    for i in range(4):
        ng_out[i, :, 4 * W_YZ : 4 * W_YZ + W_X] = whole[4 * i : 4 * i + 4]

    ng_in[me.x] = ng_out[me.x]
    last = along_x(ng_in.at[pl.ds(0, 3)], lambda to: ng_out.at[to], ng_in.at[me.x])
    start_all(last)

    losses = loss_blk[me.c, me.y, me.z]
    mine = jnp.zeros((4, LANES), F32)
    for i in range(4):
        mine = jnp.where(me.x == i, losses[4 * i : 4 * i + 4], mine)
    diagonal = lax.broadcasted_iota(jnp.int32, (4, LANES), 0) == lax.broadcasted_iota(
        jnp.int32, (4, LANES), 1
    )
    loss_ref[...] = jnp.sum(jnp.where(diagonal, mine, 0.0), axis=0, keepdims=True)

    arrive_all(last)
    norm_parts = []
    for q in range(4):
        cols = slice(q * W_YZ, (q + 1) * W_YZ)
        norm_parts.append(ng_in[0, :, cols] + ng_in[1, :, cols] + ng_in[2, :, cols] + ng_in[3, :, cols])
        norm_parts.append(ng_in[q, :, 4 * W_YZ : 4 * W_YZ + W_X])
    norm_grad = jnp.concatenate(norm_parts, axis=1)
    live = me.y_hi * 4 + me.z < 6
    scaled = norm_grad * s_gain
    inner = jnp.mean(scaled * hidden, axis=1, keepdims=True)
    grad = inverse * scaled - hidden * (inverse * inverse * inverse) * inner
    grad_ref[...] = jnp.where(live, grad, 0.0)

    out_copies = (
        pltpu.make_async_copy(grad_ref, grad_hbm, out_sem.at[0]),
        pltpu.make_async_copy(loss_ref, loss_hbm, out_sem.at[1]),
    )
    for copy in out_copies:
        copy.start()

    for made in opened:
        both_ends(made).wait_send()
    assert len(opened) == GROUPS
    for copy in out_copies:
        copy.wait()


def scratch():
    dma = pltpu.SemaphoreType.DMA
    vm = pltpu.VMEM
    first = []
    for lo, width, axis, plane in PARTS_A:
        spots = [1 if a == axis else 2 if a == "h" else 4 for a in "hzx"]
        first.append(vm((1 if axis == "h" else 3, *spots, 16, width), BF16))
    rr0 = []
    for lo, width, axis, then in PARTS_G:
        spots = [1 if a == axis else 4 for a in "yz"]
        rr0.append(vm((3, 4, *spots, 16, width), BF16))
    return {
        "residual_ref": vm((4, D_T), BF16),
        "post_ref": vm((D_T,), F32),
        "final_ref": vm((D_T,), F32),
        "hidden_ref": vm((4, D_S), BF16),
        "s_gain_ref": vm((D_S,), F32),
        "labels_ref": vm((1, LANES), jnp.int32),
        "lengths_ref": pltpu.SMEM((1, NSEQ), jnp.int32),
        "grad_ref": vm((4, D_S), F32),
        "loss_ref": vm((1, LANES), F32),
        "in_sem": dma((7,)),
        "out_sem": dma((2,)),
        "w_t": vm((D_T, VOC), BF16),
        "w_s": vm((D_S, VOC), BF16),
        "pb": vm((2, 4, 4, 16, QT), BF16),
        "first_in": tuple(first),
        "second_in": tuple(vm((n, 16, PARTS_A[0][1]), BF16) for n in (7, 7, 15)),
        "rows_in": vm((4, 16, QT), BF16),
        "tb": vm((2, 4, 4, 4, 16, QT), BF16),
        "sb": vm((2, 4, 4, 4, 16, QS), BF16),
        "res_in": vm((4, 4, D_T), BF16),
        "stu_out": vm((4, 4, QS), BF16),
        "stu_in": vm((4, 4, QS), BF16),
        "asm_t": vm((4, 16, QT), F32),
        "asm_s": vm((16, QS), F32),
        "normed": vm((4, 16, QT), BF16),
        "tab_own": vm((8, LANES), F32),
        "tab": vm((4, 8, LANES), F32),
        "lab_col": vm((ROWS, LANES), F32),
        "wgt_col": vm((ROWS, LANES), F32),
        "t_log": vm((ROWS, VOC), F32),
        "s_log": vm((ROWS, VOC), F32),
        "lg": vm((ROWS, VOC), BF16),
        "stat": vm((3, 8, ROWS), F32),
        "stat_in": vm((2, 15, 8, ROWS), F32),
        "back": vm((ROWS, LANES), F32),
        "loss_blk": vm((2, 4, 4, 16, LANES), F32),
        "g": vm((2, 4, 4, 4, 16, QS), BF16),
        "share": vm((3, ROWS, QS), F32),
        "core_in": vm((4, 4, 4, 16, QS), BF16),
        "rr0": tuple(rr0),
        "rr_x": vm((3, 4, 4, 16, W_X), BF16),
        "rr1": vm((2, 3, 4, 16, PARTS_G[0][1]), BF16),
        "rr2": vm((15, 16, W_X), BF16),
        "ng_out": vm((4, 4, 4 * W_YZ + W_X), F32),
        "ng_in": vm((4, 4, 4 * W_YZ + W_X), F32),
        "sem_w": dma((2,)),
        "a_own": dma((4,)),
        "pool": dma((2 * GROUPS,)),
    }


def shards(
    teacher_partial,
    teacher_residual,
    post_gain,
    final_gain,
    teacher_head,
    student_hidden,
    student_gain,
    student_head,
    labels,
    lengths,
):
    place = pl.BlockSpec(memory_space=pl.ANY)
    spaces = scratch()
    names = list(spaces)
    leaves, tree = jax.tree.flatten([spaces[n] for n in names])

    def body(*refs):
        held = jax.tree.unflatten(tree, refs[12:])
        kernel(*refs[:12], **dict(zip(names, held)))

    grad, loss = pl.pallas_call(
        body,
        out_shape=(
            jax.ShapeDtypeStruct((4, D_S), F32),
            jax.ShapeDtypeStruct((1, LANES), F32),
        ),
        in_specs=[place] * 10,
        out_specs=(place, place),
        scratch_shapes=leaves,
        compiler_params=pltpu.CompilerParams(
            collective_id=0, has_side_effects=True, vmem_limit_bytes=60 * 2**20
        ),
        name="distill",
    )(
        teacher_partial.reshape(2, 4, 16, D_T),
        teacher_residual,
        post_gain,
        final_gain,
        teacher_head,
        student_hidden,
        student_gain,
        student_head,
        labels.reshape(1, -1),
        lengths,
    )
    return grad, loss[0, :4]


def solution(mesh):
    torus = Mesh(mesh.devices.reshape(2, 2, 2, 4, 4), ("dp_0", "dp_1", "tp_0", "tp_1", "tp_2"))
    return jax.shard_map(
        shards,
        mesh=torus,
        in_specs=(
            P(TP, DP, None),
            P(DP_TP, None),
            P(),
            P(),
            P(None, DP_TP),
            P(DP_TP, None),
            P(),
            P(None, DP_TP),
            P(DP),
            P(DP, None),
        ),
        out_specs=(P(DP_TP, None), P(DP_TP)),
        check_vma=False,
    )
```
